32 devices in a mesh: ctx: 4 (over y, x), tp: 4 (over z), dp: 2 (over core).
Axes of the slice: x: 2, y: 2, z: 4, core: 2. Of those that a mesh axis runs over, the one named last changes fastest.
Arguments:
- k_short: bfloat16 [1024, 8192], P(('dp', 'ctx'), 'tp'), parts along dimension 0, may hold values from -6 to 6
- v_short: bfloat16 [1024, 8192], P(('dp', 'ctx'), 'tp'), parts along dimension 0, may hold values from -6 to 6
- mr_filter: bfloat16 [128, 512], P(None, 'tp'), may hold values from -0.5 to 0.5
- li_rate: float32 [8192], P('tp'), may hold values from 0 to 1, as said below
- li_residue: float32 [8192], P('tp'), may hold values from 0.5 to 2
- gate_out: bfloat16 [1024, 8192], P(('dp', 'ctx'), 'tp'), parts along dimension 0, may hold values from -6 to 6
- contig_lengths: int32 [32], P('dp'), parts along dimension 0, may hold values from 1 to 128, 512 in all
- grad_out: bfloat16 [1024, 8192], P(('dp', 'ctx'), 'tp'), parts along dimension 0, may hold values from -6 to 6
Outputs:
- mixed_out: bfloat16 [1024, 8192], P(('dp', 'ctx'), 'tp'), parts along dimension 0
- grad_values: bfloat16 [1024, 8192], P(('dp', 'ctx'), 'tp'), parts along dimension 0
- grad_filter: float32 [256, 512], P(('dp', 'ctx'), 'tp'), parts along dimension 0
The draws below stay inside these ranges and needn't reach their ends.
There are 2 independent parts, one for each index of `dp`. The reference program is written for one: setup_inputs(seed, part) draws one part's arguments, and reference() takes and returns one part's arrays. A program takes and returns all parts, laid end to end along the dimension named above; an argument that names none is the same for every part. Nothing has to cross between parts.
Inputs may be any that keep to these rules, and one draw needn't show every extreme that they name: `li_rate`: rates are positive. `contig_lengths`: they sum to 512.
All inputs are finite; a program needn't handle non-finite values.
Results may differ from the reference program's by a relative error of at most 0.0065.
Values may be sent and summed in bfloat16 or wider, within the bound.
A program may use at most 128 MiB of HBM per device.

```python
import math
import jax
import jax.numpy as jnp
import numpy as np
from jax import lax

D = 8192
MRK = 128
NCONTIG = 16
TOKENS = 512
G = 512


def draw_li_rate(key, part):
    pick_key, fast_key, slow_key = jax.random.split(key, 3)
    share = 0.5
    slow_mask = jax.random.bernoulli(pick_key, share, (D,))
    fast_rate = jnp.exp(jax.random.uniform(fast_key, (D,), jnp.float32, math.log(1.0 / 50.0), math.log(1.0 / 30.0)))
    slow_rate = jnp.exp(jax.random.uniform(slow_key, (D,), jnp.float32, math.log(0.05 / TOKENS), math.log(2.0 / TOKENS)))
    return jnp.where(slow_mask, slow_rate, fast_rate).astype(jnp.float32)


def levels(stream_key, shape, cuts, low, high):
    def one(axis_at, shards_of):
        heights = jax.random.uniform(jax.random.fold_in(jax.random.fold_in(stream_key, 6), axis_at), (shards_of,), jnp.float32, low / len(cuts), high / len(cuts))
        return jnp.repeat(jnp.exp(heights), shape[axis_at] // shards_of).reshape((-1,) + (1,) * (len(shape) - axis_at - 1))

    loudness = one(*cuts[0])
    for cut in cuts[1:]:
        loudness = loudness * one(*cut)
    return loudness


def profile(number_of, total, limit, lean):
    weights = [(1 << 20) // math.isqrt(grade ** lean) + 1 for grade in range(2, number_of + 1)]
    spare, counts = total - limit - (number_of - 1), [1] * (number_of - 1)
    while spare > 0:
        movable = [i for i in range(number_of - 1) if counts[i] < limit]
        whole, budget = sum([weights[i] for i in movable]), spare
        for i in movable:
            more = min(limit - counts[i], max(1, budget * weights[i] // whole), spare)
            counts[i] = counts[i] + more
            spare = spare - more
    return np.array([limit] + counts)


def ragged_sizes(key, number_of, total, bound, lean):
    if number_of == 2:
        one = jax.random.randint(key, (), max(1, total - bound), min(bound, total - 1) + 1)
        return jnp.stack([one, total - one])
    lengths = jnp.asarray(profile(number_of, total, bound, lean), jnp.int32)
    twos = (number_of - 1) // 2
    giver, receiver = lengths[1:1 + 2 * twos:2], lengths[2:2 + 2 * twos:2]
    room = jnp.minimum(giver - 1, bound - receiver)
    shifted = jax.random.randint(jax.random.fold_in(key, 1), (twos,), 0, 1 << 20) % (room + 1)
    lengths = lengths.at[1:1 + 2 * twos:2].set(giver - shifted).at[2:2 + 2 * twos:2].set(receiver + shifted)
    return lengths[jax.random.permutation(jax.random.fold_in(key, 2), number_of)]


def noise(stream_key, dims, spread, reach, pieces=(), kind=jnp.bfloat16):
    array = spread * jax.random.normal(stream_key, dims, jnp.float32)
    if pieces:
        array = array * levels(stream_key, dims, pieces, -0.22, 0.18)
    return jnp.clip(array, -reach, reach).astype(kind)


def setup_inputs(seed: int = 0, part: int = 0) -> dict:
    splits = jax.random.split(jax.random.key(seed), 9)
    part_splits = jax.random.split(jax.random.fold_in(splits[8], part), 9)
    return {
        "k_short": noise(part_splits[0], (TOKENS, D), 1.0, 6.0, ((0, 4), (1, 4))),
        "v_short": noise(part_splits[1], (TOKENS, D), 1.0, 6.0, ((0, 4), (1, 4))),
        "mr_filter": noise(splits[2], (MRK, G), MRK ** -0.5, 0.5, ((1, 4),)),
        "li_rate": draw_li_rate(jax.random.fold_in(splits[8], 71), part),
        "li_residue": jnp.clip(0.5 + 1.5 * jax.random.uniform(splits[4], (D,), jnp.float32) ** levels(splits[4], (D,), ((0, 4),), -0.2, 0.2), 0.5, 2.0),
        "gate_out": noise(part_splits[5], (TOKENS, D), 1.0, 6.0, ((0, 4), (1, 4))),
        "contig_lengths": ragged_sizes(part_splits[6], NCONTIG, TOKENS, TOKENS // 4, 2).astype(jnp.int32),
        "grad_out": noise(part_splits[7], (TOKENS, D), 1.0, 6.0, ((0, 4), (1, 4))),
    }


def contig_tables(contig_lengths, first_row, row_count):
    offsets = (jnp.cumsum(contig_lengths) - contig_lengths).astype(jnp.int32)
    places = first_row + jnp.arange(row_count, dtype=jnp.int32)
    before = offsets[None, :] <= places[:, None]
    begins = lax.optimization_barrier(jnp.max(jnp.where(before, offsets[None, :], 0), axis=1)).astype(jnp.int32)
    fresh_start = jnp.any(offsets[None, :] == places[:, None], axis=1)
    return (begins, fresh_start)

def banded(filter_rows):
    groups, tap_count = filter_rows.shape
    padded = jnp.concatenate([filter_rows, jnp.zeros_like(filter_rows)], axis=1)
    tiled_rows = jnp.tile(padded, (1, tap_count))
    return tiled_rows[:, :tap_count * (2 * tap_count - 1)].reshape(groups, tap_count, 2 * tap_count - 1)

def apply_band(band_rows, keep_mask, window, groups):
    weights = jnp.where(keep_mask[None], band_rows, 0).astype(jnp.float32)
    shaped = window.astype(jnp.float32).reshape(window.shape[0], groups, -1)
    result = jnp.einsum('gts,sgi->tgi', weights, shaped, precision=lax.Precision.HIGHEST)
    return result.reshape(result.shape[0], -1)

def diagonal_sums(products):
    groups, tap_count, window_rows = products.shape
    padded = jnp.pad(products, ((0, 0), (0, 0), (0, 1))).reshape(groups, tap_count * (window_rows + 1))
    padded = jnp.pad(padded, ((0, 0), (0, tap_count)))
    folded = padded.reshape(groups, tap_count, window_rows + 2).sum(axis=1)
    return folded[:, :tap_count][:, ::-1].T

def reference(k_short, v_short, mr_filter, li_rate, li_residue, gate_out, contig_lengths, grad_out):
    window_rows = 2 * MRK - 1
    groups = mr_filter.shape[1]
    block_count = TOKENS // MRK
    u_short = (k_short.astype(jnp.float32) * v_short.astype(jnp.float32)).astype(jnp.bfloat16)
    filter_cols = mr_filter.T
    band_fwd = banded(filter_cols[:, ::-1])
    band_bwd = banded(filter_cols)
    u_ext = jnp.concatenate([jnp.zeros((MRK - 1, D), jnp.bfloat16), u_short], axis=0)

    def forward_mask(block_start):
        begins, _ = contig_tables(contig_lengths, block_start, MRK)
        places = block_start - (MRK - 1) + jnp.arange(window_rows, dtype=jnp.int32)
        return places[None, :] >= begins[:, None]

    def fwd_block(block_id):
        block_start = (block_id * MRK).astype(jnp.int32)
        window = lax.dynamic_slice_in_dim(u_ext, block_start, window_rows, 0)
        return apply_band(band_fwd, forward_mask(block_start), window, groups)
    block_ids = jnp.arange(block_count, dtype=jnp.int32)
    z_short = lax.map(fwd_block, block_ids).reshape(TOKENS, D)
    y_short = z_short.astype(jnp.bfloat16)
    decays = jnp.exp(-li_rate)
    scales = li_residue * jnp.sqrt(-jnp.expm1(-2.0 * li_rate))
    _, fresh_start = contig_tables(contig_lengths, 0, TOKENS + 1)
    keep_all = jnp.where(fresh_start, 0.0, 1.0).astype(jnp.float32)
    keep_rows = keep_all[:TOKENS]
    keep_next = keep_all[1:]

    def advance(carried, element):
        kept_row, value_row = element
        carried = decays * kept_row * carried + value_row.astype(jnp.float32)
        return (carried, carried)
    _, states = lax.scan(advance, jnp.zeros((D,), jnp.float32), (keep_rows, y_short))
    z_long = (scales * states).astype(jnp.bfloat16)
    mixed_out = (gate_out.astype(jnp.float32) * z_long.astype(jnp.float32)).astype(jnp.bfloat16)
    grad_long = (scales * gate_out.astype(jnp.float32) * grad_out.astype(jnp.float32)).astype(jnp.bfloat16)
    _, adjoint = lax.scan(advance, jnp.zeros((D,), jnp.float32), (keep_next, grad_long), reverse=True)
    grad_short = adjoint.astype(jnp.bfloat16)
    g_ext = jnp.concatenate([grad_short, jnp.zeros((MRK - 1, D), jnp.bfloat16)], axis=0)

    def bwd_block(block_id):
        block_start = (block_id * MRK).astype(jnp.int32)
        window = lax.dynamic_slice_in_dim(g_ext, block_start, window_rows, 0)
        begins, _ = contig_tables(contig_lengths, block_start, window_rows)
        out_rows = block_start + jnp.arange(MRK, dtype=jnp.int32)
        keep_mask = begins[None, :] <= out_rows[:, None]
        return apply_band(band_bwd, keep_mask, window, groups)
    grad_u = lax.map(bwd_block, block_ids).reshape(TOKENS, D)
    grad_values = (k_short.astype(jnp.float32) * grad_u).astype(jnp.bfloat16)

    def filt_block(running, block_id):
        block_start = (block_id * MRK).astype(jnp.int32)
        window = lax.dynamic_slice_in_dim(u_ext, block_start, window_rows, 0).astype(jnp.float32)
        grad_block = lax.dynamic_slice_in_dim(grad_short, block_start, MRK, 0).astype(jnp.float32)
        products = jnp.einsum('tgi,sgi->gts', grad_block.reshape(MRK, groups, -1), window.reshape(window_rows, groups, -1), precision=lax.Precision.HIGHEST)
        products = jnp.where(forward_mask(block_start)[None], products, 0.0)
        return (running + diagonal_sums(products), None)
    grad_filter, _ = lax.scan(filt_block, jnp.zeros((MRK, groups), jnp.float32), block_ids)
    return (mixed_out, grad_values, grad_filter)
```

```python
import functools

import jax
import jax.numpy as jnp
from jax import lax
from jax.experimental import pallas as pl
from jax.experimental.pallas import tpu as pltpu
from jax.sharding import PartitionSpec as P

MESH = pl.DeviceIdType.MESH
LANES = 128
SUB = 8
F32 = jnp.float32
BF16 = jnp.bfloat16


def seg_of(lengths_ref, places, total):
    offset = jnp.int32(0)
    seg = jnp.zeros(places.shape, jnp.int32)
    for i in range(lengths_ref.shape[0]):
        seg = seg + (places >= offset).astype(jnp.int32)
        offset = offset + lengths_ref[i]
    return seg + (places >= total).astype(jnp.int32)


def one_minus_exp(x):
    series = jnp.ones_like(x)
    for n in range(9, 1, -1):
        series = 1.0 - x / n * series
    return jnp.where(x < 0.5, x * series, 1.0 - jnp.exp(-x))


def kernel(
    ctx_count, reach, halo_parts,
    lengths, k_ref, v_ref, filt_ref, rate_ref, residue_ref, gate_ref, gout_ref,
    mixed_ref, gv_ref, gf_ref,
    u_ext, g_ext, adj, state, scale, taps, taps_rev, mask_f, mask_b, diag_seg,
    scan_masks, acc, partial, gf_slots, carry_f, carry_b, carry_f_in, carry_b_in,
    u_send, u_recv, g_send, g_recv, cf_send, cf_recv, cb_send, cb_recv, gf_send, gf_recv,
):
    rows, width = k_ref.shape
    groups = filt_ref.shape[1]
    per_group = width // groups
    per_chunk = LANES // per_group
    chunks = width // LANES
    part_width = width // halo_parts
    total = rows * ctx_count
    me = lax.axis_index("ctx")
    first = me * rows

    barrier = pltpu.get_barrier_semaphore()

    @pl.loop(1, ctx_count)
    def _(step):
        pl.semaphore_signal(
            barrier, inc=1, device_id={"ctx": lax.rem(me + step, ctx_count)}, device_id_type=MESH
        )

    pl.semaphore_wait(barrier, ctx_count - 1)

    def u_copy(part):
        cols = pl.ds(part * part_width, part_width)
        return pltpu.make_async_remote_copy(
            src_ref=u_ext.at[pl.ds(rows, rows), cols],
            dst_ref=u_ext.at[pl.ds(0, rows), cols],
            send_sem=u_send.at[part],
            recv_sem=u_recv.at[part],
            device_id={"ctx": lax.rem(me + 1, ctx_count)},
            device_id_type=MESH,
        )

    def g_copy(part):
        cols = pl.ds(part * part_width, part_width)
        return pltpu.make_async_remote_copy(
            src_ref=g_ext.at[pl.ds(0, rows), cols],
            dst_ref=g_ext.at[pl.ds(rows, rows), cols],
            send_sem=g_send.at[part],
            recv_sem=g_recv.at[part],
            device_id={"ctx": lax.rem(me + ctx_count - 1, ctx_count)},
            device_id_type=MESH,
        )

    def carry_copy(k, forward):
        src, dst, send, recv = (
            (carry_f, carry_f_in, cf_send, cf_recv)
            if forward
            else (carry_b, carry_b_in, cb_send, cb_recv)
        )
        peer = me + 1 + k if forward else me + ctx_count - 1 - k
        return pltpu.make_async_remote_copy(
            src_ref=src,
            dst_ref=dst.at[k],
            send_sem=send.at[k],
            recv_sem=recv.at[k],
            device_id={"ctx": lax.rem(peer, ctx_count)},
            device_id_type=MESH,
        )

    for part in range(halo_parts):
        cols = slice(part * part_width, (part + 1) * part_width)
        u_ext[rows:, cols] = (k_ref[:, cols].astype(F32) * v_ref[:, cols].astype(F32)).astype(BF16)

        @pl.when(me < ctx_count - 1)
        def _():
            u_copy(part).start()

    @pl.when(me == 0)
    def _():
        u_ext[:rows, :] = jnp.zeros((rows, width), BF16)

    @pl.when(me == ctx_count - 1)
    def _():
        g_ext[rows:, :] = jnp.zeros((rows, width), BF16)

    rate_all = rate_ref[...]
    scale[...] = residue_ref[...] * jnp.sqrt(one_minus_exp(2.0 * rate_all))
    row = lax.broadcasted_iota(jnp.int32, (rows, LANES), 0)
    seg = seg_of(lengths, first + row, total)
    sub = lax.rem(row, SUB)
    tile = row - sub
    for i, k in enumerate((1, 2, 4)):
        same = (seg == pltpu.roll(seg, k, 0)) & (sub >= k)
        scan_masks[i] = same.astype(F32)
        same = (seg == pltpu.roll(seg, rows - k, 0)) & (sub + k < SUB)
        scan_masks[4 + i] = same.astype(F32)
    scan_masks[3] = (seg == seg_of(lengths, first + tile - 1, total)).astype(F32)
    scan_masks[7] = (seg == seg_of(lengths, first + tile + SUB, total)).astype(F32)
    lane_one = jnp.zeros((1, LANES), jnp.int32)
    seg_before = seg_of(lengths, first - 1 + lane_one, total)
    seg_after = seg_of(lengths, first + rows + lane_one, total)
    scan_masks[8] = (seg == seg_before).astype(F32)
    scan_masks[9] = (seg == seg_after).astype(F32)
    lane = lax.broadcasted_iota(jnp.int32, (rows, LANES), 1)
    lane_row = lax.broadcasted_iota(jnp.int32, (1, LANES), 1)
    seg_prev = seg_of(lengths, first - rows + lane_row, total)
    seg_here = seg_of(lengths, first + lane_row, total)
    seg_next = seg_of(lengths, first + rows + lane_row, total)
    f_left = ((seg == seg_prev) & (lane > row)).astype(F32)
    f_right = ((seg == seg_here) & (lane <= row)).astype(F32)
    mask_f[:, :LANES] = f_left.astype(BF16)
    mask_f[:, LANES:] = f_right.astype(BF16)
    diag_seg[...] = f_left + f_right
    mask_b[:, :LANES] = ((seg == seg_here) & (lane >= row)).astype(F32).astype(BF16)
    mask_b[:, LANES:] = ((seg == seg_next) & (lane < row)).astype(F32).astype(BF16)
    flip = (lax.rem(row + lane, LANES) == 0).astype(F32)
    eye = (row == lane).astype(F32)
    over_taps = (((0,), (0,)), ((), ()))
    filt = filt_ref[...]
    taps[...] = lax.dot_general(filt, eye.astype(BF16), over_taps, preferred_element_type=F32)
    taps_rev[...] = lax.dot_general(filt, flip.astype(BF16), over_taps, preferred_element_type=F32)

    sub8 = lax.broadcasted_iota(jnp.int32, (SUB, LANES), 0).astype(F32)
    tiles = rows // SUB

    def chunk_cols(q):
        return pl.ds(pl.multiple_of(q * LANES, LANES), LANES)

    def scan_tiles(values, rate, forward):
        base = 0 if forward else 4
        steps = [jnp.exp(-k * rate) for k in (1.0, 2.0, 4.0)]
        far = jnp.exp(-((sub8 + 1.0) if forward else (SUB - sub8)) * rate)
        out = [None] * tiles
        carry = None
        for n in range(tiles) if forward else reversed(range(tiles)):
            here = slice(n * SUB, (n + 1) * SUB)
            x = values[here, :]
            for i, k in enumerate((1, 2, 4)):
                shifted = pltpu.roll(x, k if forward else SUB - k, 0)
                x = x + steps[i] * scan_masks[base + i, here, :] * shifted
            if carry is not None:
                x = x + far * scan_masks[base + 3, here, :] * carry
            carry = x[SUB - 1 : SUB, :] if forward else x[0:1, :]
            out[n] = x
        return out, carry

    def carried(slots, cols, rate, forward):
        value = slots[0, :, cols]
        for k in range(1, reach):
            edge = first - 1 - rows * k if forward else first + rows + rows * k
            there = seg_of(lengths, edge + lane_one, total)
            same = (there == (seg_before if forward else seg_after)).astype(F32)
            value = value + slots[k, :, cols] * same * jnp.exp(-float(rows * k) * rate)
        return value

    @pl.loop(0, chunks, unroll=4)
    def _(q):
        cols = chunk_cols(q)
        rate = rate_ref[:, cols]
        long = (scale[:, cols] * gate_ref[:, cols].astype(F32) * gout_ref[:, cols].astype(F32))
        out, carry = scan_tiles(long.astype(BF16).astype(F32), rate, False)
        for n in range(tiles):
            adj[n * SUB : (n + 1) * SUB, cols] = out[n]
        carry_b[:, cols] = carry

    for k in range(reach):

        @pl.when(me >= 1 + k)
        def _():
            carry_copy(k, False).start()

        @pl.when(me + 1 + k >= ctx_count)
        def _():
            carry_b_in[k] = jnp.zeros((1, width), F32)

    for k in range(reach):

        @pl.when(me + 1 + k < ctx_count)
        def _():
            carry_copy(k, False).wait_recv()

    for part in range(halo_parts):
        per_part = chunks // halo_parts

        @pl.loop(part * per_part, (part + 1) * per_part, unroll=4)
        def _(q):
            cols = chunk_cols(q)
            rate = rate_ref[:, cols]
            value = carried(carry_b_in, cols, rate, False)
            far = jnp.exp(-(SUB - sub8) * rate)
            eighth = jnp.exp(-float(SUB) * rate)
            for n in reversed(range(tiles)):
                here = slice(n * SUB, (n + 1) * SUB)
                x = adj[here, cols] + far * scan_masks[9, here, :] * value
                adj[here, cols] = x
                value = value * eighth
            g_ext[:rows, cols] = adj[:, cols].astype(BF16)

        @pl.when(me > 0)
        def _():
            g_copy(part).start()

    def bands(tap_rows, mask):
        blocks = []
        for g in range(per_chunk):
            skew = pltpu.roll(
                jnp.broadcast_to(tap_rows[g : g + 1, :], (SUB, LANES)), 0, 1,
                stride=1, stride_axis=0,
            )
            circ = jnp.concatenate(
                [skew] + [pltpu.roll(skew, n * SUB, 1) for n in range(1, tiles)], axis=0
            ).astype(BF16)
            blocks.append(
                jnp.concatenate([circ * mask[:, :LANES], circ * mask[:, LANES:]], axis=1)
            )
        return jnp.concatenate(blocks, axis=0)

    group_of_lane = lane // per_group

    for part in range(halo_parts):

        @pl.when(me > 0)
        def _():
            u_copy(part).wait_recv()

        @pl.loop(part * per_part, (part + 1) * per_part, unroll=2)
        def _(q):
            cols = chunk_cols(q)
            window = u_ext[:, cols]
            grads = g_ext[:rows, cols]
            group_rows = pl.ds(pl.multiple_of(q * per_chunk, per_chunk), per_chunk)
            all_y = jnp.dot(
                bands(taps_rev[group_rows, :], mask_f), window,
                preferred_element_type=F32,
            )
            y = all_y[:rows, :]
            for g in range(1, per_chunk):
                y = jnp.where(group_of_lane == g, all_y[g * rows : (g + 1) * rows, :], y)
            own = jnp.concatenate(
                [jnp.where(group_of_lane == g, grads, jnp.zeros_like(grads)) for g in range(per_chunk)],
                axis=0,
            )
            all_prod = lax.dot_general(
                own, window, (((1,), (1,)), ((), ())), preferred_element_type=F32
            )
            for g in range(per_chunk):
                prod = all_prod[g * rows : (g + 1) * rows, :]
                prod = jnp.where(lane <= row, prod[:, LANES:], prod[:, :LANES]) * diag_seg[...]
                folded = prod[:SUB, :]
                for n in range(1, tiles):
                    folded = folded + pltpu.roll(
                        prod[n * SUB : (n + 1) * SUB, :], LANES - n * SUB, 1
                    )
                acc[pl.ds(pl.multiple_of((q * per_chunk + g) * SUB, SUB), SUB), :] = folded
            out, carry = scan_tiles(y.astype(BF16).astype(F32), rate_ref[:, cols], True)
            for n in range(tiles):
                state[n * SUB : (n + 1) * SUB, cols] = out[n]
            carry_f[:, cols] = carry

    for k in range(reach):

        @pl.when(me + 1 + k < ctx_count)
        def _():
            carry_copy(k, True).start()

        @pl.when(me < 1 + k)
        def _():
            carry_f_in[k] = jnp.zeros((1, width), F32)

    skewed = acc[pl.ds(0, groups, stride=SUB), :]
    for r in range(1, SUB):
        skewed = skewed + pltpu.roll(acc[pl.ds(r, groups, stride=SUB), :], LANES - r, 1)
    by_tap = lax.dot_general(
        flip, skewed, (((1,), (1,)), ((), ())),
        precision=lax.Precision.HIGHEST, preferred_element_type=F32,
    )
    piece = rows // ctx_count
    for i in range(ctx_count):
        partial[i] = by_tap[i * piece : (i + 1) * piece, :]

    def gf_copy(step):
        peer = lax.rem(me + step, ctx_count)
        return pltpu.make_async_remote_copy(
            src_ref=partial.at[peer],
            dst_ref=gf_slots.at[step - 1],
            send_sem=gf_send.at[step - 1],
            recv_sem=gf_recv.at[step - 1],
            device_id={"ctx": peer},
            device_id_type=MESH,
        )

    @pl.loop(1, ctx_count)
    def _(step):
        gf_copy(step).start()

    def finish_forward():
        for k in range(reach):

            @pl.when(me >= 1 + k)
            def _():
                carry_copy(k, True).wait_recv()

        @pl.loop(0, chunks, unroll=4)
        def _(q):
            cols = chunk_cols(q)
            rate = rate_ref[:, cols]
            value = carried(carry_f_in, cols, rate, True)
            far = jnp.exp(-(sub8 + 1.0) * rate)
            eighth = jnp.exp(-float(SUB) * rate)
            for n in range(tiles):
                here = slice(n * SUB, (n + 1) * SUB)
                x = state[here, cols] + far * scan_masks[8, here, :] * value
                state[here, cols] = x
                value = value * eighth
            z_long = (scale[:, cols] * state[:, cols]).astype(BF16)
            mixed_ref[:, cols] = (gate_ref[:, cols].astype(F32) * z_long.astype(F32)).astype(BF16)

    for part in range(halo_parts):

        @pl.when(me < ctx_count - 1)
        def _():
            g_copy(part).wait_recv()

        @pl.loop(part * per_part, (part + 1) * per_part, unroll=2)
        def _(q):
            cols = chunk_cols(q)
            window = g_ext[:, cols]
            group_rows = pl.ds(pl.multiple_of(q * per_chunk, per_chunk), per_chunk)
            all_u = jnp.dot(
                bands(taps[group_rows, :], mask_b), window,
                preferred_element_type=F32,
            )
            grad_u = all_u[:rows, :]
            for g in range(1, per_chunk):
                grad_u = jnp.where(group_of_lane == g, all_u[g * rows : (g + 1) * rows, :], grad_u)
            gv_ref[:, cols] = (k_ref[:, cols].astype(F32) * grad_u).astype(BF16)

        if part == (halo_parts - 1) // 2:
            finish_forward()

    own = partial[me]

    def add_slot(step, value):
        gf_copy(step).wait_recv()
        return value + gf_slots[step - 1]

    gf_ref[...] = lax.fori_loop(1, ctx_count, add_slot, own)

    @pl.loop(1, ctx_count)
    def _(step):
        gf_copy(step).wait_send()

    for k in range(reach):

        @pl.when(me >= 1 + k)
        def _():
            carry_copy(k, False).wait_send()

        @pl.when(me + 1 + k < ctx_count)
        def _():
            carry_copy(k, True).wait_send()

    for part in range(halo_parts):

        @pl.when(me < ctx_count - 1)
        def _():
            u_copy(part).wait_send()

        @pl.when(me > 0)
        def _():
            g_copy(part).wait_send()


def crossing(lengths_ref, edge):
    offset = jnp.int32(0)
    before = jnp.int32(0)
    after = jnp.int32(0)
    for i in range(lengths_ref.shape[0]):
        end = offset + lengths_ref[i]
        inside = (offset < edge) & (end > edge)
        before = jnp.where(inside, edge - offset, before)
        after = jnp.where(inside, end - edge, after)
        offset = end
    return before, after


def short_kernel(
    ctx_count, halo_parts,
    lengths, k_ref, v_ref, filt_ref, rate_ref, residue_ref, gate_ref, gout_ref,
    mixed_ref, gv_ref, gf_ref,
    u_own, g_own, u_out, g_out, u_in, g_in, adj, y_own, gu_own, circ_f, circ_b,
    scale, taps, taps_rev, mask_f, mask_b, diag_seg, scan_masks, even_odd, pair_lanes,
    right_rows, left_rows, quad_u, quad_g, acc, acc_t, partial, gf_slots,
    carry_f, carry_b, carry_f_in, carry_b_in,
    u_send, u_recv, g_send, g_recv, cf_send, cf_recv, cb_send, cb_recv, gf_send, gf_recv,
):
    rows, width = k_ref.shape
    groups = filt_ref.shape[1]
    half = rows // 2
    per_group = width // groups
    per_chunk = LANES // per_group
    pairs = per_chunk // 2
    chunks = width // LANES
    per_part = chunks // halo_parts
    part_width = width // halo_parts
    total = rows * ctx_count
    tiles = rows // SUB
    me = lax.axis_index("ctx")
    first = me * rows
    has_next = me < ctx_count - 1
    has_prev = me > 0

    barrier = pltpu.get_barrier_semaphore()

    @pl.loop(1, ctx_count)
    def _(step):
        pl.semaphore_signal(
            barrier, inc=1, device_id={"ctx": lax.rem(me + step, ctx_count)}, device_id_type=MESH
        )

    def halo_copy(part, forward):
        src, dst, send, recv = (
            (u_out, u_in, u_send, u_recv) if forward else (g_out, g_in, g_send, g_recv)
        )
        cols = pl.ds(part * part_width, part_width)
        peer = me + 1 if forward else me + ctx_count - 1
        return pltpu.make_async_remote_copy(
            src_ref=src.at[:, cols],
            dst_ref=dst.at[:, cols],
            send_sem=send.at[part],
            recv_sem=recv.at[part],
            device_id={"ctx": lax.rem(peer, ctx_count)},
            device_id_type=MESH,
        )

    def carry_copy(forward):
        src, dst, send, recv = (
            (carry_f, carry_f_in, cf_send, cf_recv)
            if forward
            else (carry_b, carry_b_in, cb_send, cb_recv)
        )
        peer = me + 1 if forward else me + ctx_count - 1
        return pltpu.make_async_remote_copy(
            src_ref=src,
            dst_ref=dst,
            send_sem=send.at[0],
            recv_sem=recv.at[0],
            device_id={"ctx": lax.rem(peer, ctx_count)},
            device_id_type=MESH,
        )

    @pl.when(jnp.logical_not(has_prev))
    def _():
        u_in[...] = jnp.zeros(u_in.shape, BF16)
        carry_f_in[...] = jnp.zeros(carry_f_in.shape, F32)

    @pl.when(jnp.logical_not(has_next))
    def _():
        g_in[...] = jnp.zeros(g_in.shape, BF16)
        carry_b_in[...] = jnp.zeros(carry_b_in.shape, F32)

    left_a, left_b = crossing(lengths, first)
    right_a, right_b = crossing(lengths, first + rows)

    rate_all = rate_ref[...]
    scale[...] = residue_ref[...] * jnp.sqrt(one_minus_exp(2.0 * rate_all))
    row = lax.broadcasted_iota(jnp.int32, (rows, LANES), 0)
    lane = lax.broadcasted_iota(jnp.int32, (rows, LANES), 1)
    lane_row = lax.broadcasted_iota(jnp.int32, (1, LANES), 1)
    row_half = lax.broadcasted_iota(jnp.int32, (half, LANES), 0)
    lane_half = lax.broadcasted_iota(jnp.int32, (half, LANES), 1)
    seg = seg_of(lengths, first + row, total)
    sub = lax.rem(row, SUB)
    tile = row - sub
    for i, k in enumerate((1, 2, 4)):
        same = (seg == pltpu.roll(seg, k, 0)) & (sub >= k)
        scan_masks[i] = same.astype(F32)
        same = (seg == pltpu.roll(seg, rows - k, 0)) & (sub + k < SUB)
        scan_masks[4 + i] = same.astype(F32)
    scan_masks[3] = (seg == seg_of(lengths, first + tile - 1, total)).astype(F32)
    scan_masks[7] = (seg == seg_of(lengths, first + tile + SUB, total)).astype(F32)
    lane_one = jnp.zeros((1, LANES), jnp.int32)
    scan_masks[8] = (seg == seg_of(lengths, first + rows - 1 + lane_one, total)).astype(F32)
    scan_masks[9] = (seg == seg_of(lengths, first + rows + lane_one, total)).astype(F32)
    seg_here = seg_of(lengths, first + lane_row, total)
    own = ((seg == seg_here) & (lane <= row)).astype(F32)
    mask_f[...] = own.astype(BF16)
    diag_seg[...] = own
    mask_b[...] = ((seg == seg_here) & (lane >= row)).astype(F32).astype(BF16)

    group_of_lane = lane // per_group
    pair_of_lane = group_of_lane // 2
    send_u = right_a <= half
    send_gpart = left_a <= half
    for e in range(2):
        lanes = lax.rem(group_of_lane, 2) == e
        even_odd[e * rows : (e + 1) * rows, :] = lanes.astype(F32).astype(BF16)
        right_rows[e * rows : (e + 1) * rows, :] = (
            (lanes & (row >= rows - right_a)).astype(F32).astype(BF16)
        )
        left_rows[e * rows : (e + 1) * rows, :] = (
            (lanes & (row < left_b)).astype(F32).astype(BF16)
        )
    for p in range(pairs):
        pair_lanes[p] = (pair_of_lane == p).astype(F32).astype(BF16)
    group_half = lane_half // per_group
    for e in range(4):
        lanes = lax.rem(group_half, 4) == e
        quad_u[e * half : (e + 1) * half, :] = (
            jnp.where(send_gpart, lanes.astype(F32), 0.0).astype(BF16)
        )
        quad_g[e * half : (e + 1) * half, :] = (
            jnp.where(send_u, 0.0, lanes.astype(F32)).astype(BF16)
        )

    flip = (lax.rem(row + lane, LANES) == 0).astype(F32)
    eye = (row == lane).astype(F32)
    over_taps = (((0,), (0,)), ((), ()))
    filt = filt_ref[...]
    taps[...] = lax.dot_general(filt, eye.astype(BF16), over_taps, preferred_element_type=F32)
    taps_rev[...] = lax.dot_general(filt, flip.astype(BF16), over_taps, preferred_element_type=F32)
    sub8 = lax.broadcasted_iota(jnp.int32, (SUB, LANES), 0).astype(F32)

    def chunk_cols(q):
        return pl.ds(pl.multiple_of(q * LANES, LANES), LANES)

    def group_rows(q, g):
        return pl.ds(pl.multiple_of((q * per_chunk + g) * rows, rows), rows)

    def scan_tiles(values, rate, forward, carry=None):
        base = 0 if forward else 4
        steps = [jnp.exp(-k * rate) for k in (1.0, 2.0, 4.0)]
        far = jnp.exp(-((sub8 + 1.0) if forward else (SUB - sub8)) * rate)
        out = [None] * tiles
        for n in range(tiles) if forward else reversed(range(tiles)):
            here = slice(n * SUB, (n + 1) * SUB)
            x = values[here, :]
            for i, k in enumerate((1, 2, 4)):
                shifted = pltpu.roll(x, k if forward else SUB - k, 0)
                x = x + steps[i] * scan_masks[base + i, here, :] * shifted
            if carry is not None:
                x = x + far * scan_masks[base + 3, here, :] * carry
            carry = x[SUB - 1 : SUB, :] if forward else x[0:1, :]
            out[n] = x
        return out, carry

    def circulant(tap_rows, g):
        skew = pltpu.roll(
            jnp.broadcast_to(tap_rows[g : g + 1, :], (SUB, LANES)), 0, 1, stride=1, stride_axis=0
        )
        return jnp.concatenate(
            [skew] + [pltpu.roll(skew, n * SUB, 1) for n in range(1, tiles)], axis=0
        ).astype(BF16)

    def pick(outs, n_rows, index):
        value = outs[:n_rows, :]
        for p in range(1, outs.shape[0] // n_rows):
            value = jnp.where(index == p, outs[p * n_rows : (p + 1) * n_rows, :], value)
        return value

    def twice(x):
        return jnp.concatenate([x, x], axis=0)

    def fold(prod, sign):
        folded = prod[:SUB, :]
        for n in range(1, prod.shape[0] // SUB):
            folded = folded + pltpu.roll(prod[n * SUB : (n + 1) * SUB, :], LANES - n * SUB, 1)
        return folded

    pair_half = lane_half // (2 * per_group)
    across = (((1,), (1,)), ((), ()))

    pl.semaphore_wait(barrier, ctx_count - 1)

    for part in range(halo_parts):

        @pl.loop(part * per_part, (part + 1) * per_part, unroll=4)
        def _(q):
            cols = chunk_cols(q)
            u = (k_ref[:, cols].astype(F32) * v_ref[:, cols].astype(F32)).astype(BF16)
            u_own[:, cols] = u
            rate = rate_ref[:, cols]
            long = scale[:, cols] * gate_ref[:, cols].astype(F32) * gout_ref[:, cols].astype(F32)
            out, carry = scan_tiles(long.astype(BF16).astype(F32), rate, False)
            for n in range(tiles):
                adj[n * SUB : (n + 1) * SUB, cols] = out[n]
            carry_b[:, cols] = carry
            g = jnp.concatenate(out, axis=0).astype(BF16)
            tap_rows = pl.ds(pl.multiple_of(q * per_chunk, per_chunk), per_chunk)
            f_rows, b_rows = taps_rev[tap_rows, :], taps[tap_rows, :]
            top, bottom = [], []
            for i in range(per_chunk):
                f, b = circulant(f_rows, i), circulant(b_rows, i)
                circ_f[group_rows(q, i), :] = f
                circ_b[group_rows(q, i), :] = b
                top.append(f[:half, :])
                bottom.append(b[half:, :])
            join = lambda xs: jnp.concatenate(
                [jnp.concatenate(xs[2 * p : 2 * p + 2], axis=1) for p in range(pairs)], axis=0
            )
            y_part = jnp.dot(join(top), twice(u) * right_rows[...], preferred_element_type=F32)
            y_part = pick(y_part, half, pair_half)
            g_part = jnp.dot(join(bottom), twice(g) * left_rows[...], preferred_element_type=F32)
            g_part = pick(g_part, half, pair_half)
            y_part = jnp.where(row_half < right_b, y_part, 0.0)
            g_part = jnp.where(row_half >= half - left_a, g_part, 0.0)
            u_tail = jnp.where(row_half >= half - right_a, u[half:, :].astype(F32), 0.0)
            g_head = jnp.where(row_half < left_b, g[:half, :].astype(F32), 0.0)
            u_out[:, cols] = jnp.where(send_u, u_tail, y_part).astype(BF16)
            g_out[:, cols] = jnp.where(send_gpart, g_part, g_head).astype(BF16)

        @pl.when(has_next)
        def _():
            halo_copy(part, True).start()

        @pl.when(has_prev)
        def _():
            halo_copy(part, False).start()

    @pl.when(has_prev)
    def _():
        carry_copy(False).start()

    def pair_bands(circ, q, mask):
        return jnp.concatenate(
            [
                jnp.concatenate(
                    [circ[group_rows(q, 2 * p + e), :] * mask for e in range(2)], axis=1
                )
                for p in range(pairs)
            ],
            axis=0,
        )

    @pl.loop(0, chunks, unroll=4)
    def _(q):
        cols = chunk_cols(q)
        rate = rate_ref[:, cols]
        y = jnp.dot(
            pair_bands(circ_f, q, mask_f[...]), twice(u_own[:, cols]) * even_odd[...],
            preferred_element_type=F32,
        )
        y = pick(y, rows, pair_of_lane)
        y_own[:, cols] = y
        last = y.astype(BF16).astype(F32) * scan_masks[8]
        eighth = jnp.exp(-float(SUB) * rate)
        run = last[:SUB, :]
        for n in range(1, tiles):
            run = run * eighth + last[n * SUB : (n + 1) * SUB, :]
        carry_f[:, cols] = jnp.sum(
            run * jnp.exp(-(SUB - 1.0 - sub8) * rate), axis=0, keepdims=True
        )

    @pl.when(has_next)
    def _():
        carry_copy(True).start()
        carry_copy(False).wait_recv()

    @pl.loop(0, chunks, unroll=4)
    def _(q):
        cols = chunk_cols(q)
        rate = rate_ref[:, cols]
        value = carry_b_in[:, cols]
        far = jnp.exp(-(SUB - sub8) * rate)
        eighth = jnp.exp(-float(SUB) * rate)
        out = [None] * tiles
        for n in reversed(range(tiles)):
            here = slice(n * SUB, (n + 1) * SUB)
            out[n] = adj[here, cols] + far * scan_masks[9, here, :] * value
            value = value * eighth
        g = jnp.concatenate(out, axis=0).astype(BF16)
        g_own[:, cols] = g
        gu = jnp.dot(
            pair_bands(circ_b, q, mask_b[...]), twice(g) * even_odd[...],
            preferred_element_type=F32,
        )
        gu_own[:, cols] = pick(gu, rows, pair_of_lane)
        by_pair = jnp.concatenate([g * pair_lanes[p] for p in range(pairs)], axis=0)
        prods = lax.dot_general(
            by_pair, twice(u_own[:, cols]) * even_odd[...], across, preferred_element_type=F32
        )
        for p in range(pairs):
            for e in range(2):
                prod = prods[p * rows : (p + 1) * rows, e * LANES : (e + 1) * LANES]
                at = pl.multiple_of((q * per_chunk + 2 * p + e) * SUB, SUB)
                acc[pl.ds(at, SUB), :] = fold(prod * diag_seg[...], 1)

    low_lanes = lane < half

    def quad_bands(circ, q, forward):
        quads = []
        for g in range(0, per_chunk, 4):
            halves = []
            for e in (0, 2):
                one = circ[group_rows(q, g + e), :]
                two = circ[group_rows(q, g + e + 1), :]
                if forward:
                    one = jnp.concatenate([one[half:, :], one[:half, :]], axis=0)
                else:
                    two = jnp.concatenate([two[half:, :], two[:half, :]], axis=0)
                halves.append(jnp.where(low_lanes, one, two))
            quads.append(jnp.concatenate(halves, axis=1))
        return jnp.concatenate(quads, axis=0)

    def four(x):
        return jnp.concatenate([x, x, x, x], axis=0)

    quad_of_lane = lane // (4 * per_group)

    for part in range(halo_parts):

        @pl.when(has_prev)
        def _():
            halo_copy(part, True).wait_recv()

        @pl.when(has_next)
        def _():
            halo_copy(part, False).wait_recv()

        @pl.loop(part * per_part, (part + 1) * per_part, unroll=4)
        def _(q):
            cols = chunk_cols(q)
            u_msg, g_msg = u_in[:, cols], g_in[:, cols]
            lhs = jnp.concatenate(
                [u_msg * (pair_lanes[p, :half, :]) for p in range(pairs)], axis=0
            )
            prods = lax.dot_general(
                lhs, twice(g_own[:, cols]) * left_rows[...], across, preferred_element_type=F32
            )
            prods = jnp.where(send_gpart, prods, 0.0)
            lhs = jnp.concatenate(
                [g_msg * (pair_lanes[p, :half, :]) for p in range(pairs)], axis=0
            )
            prods2 = lax.dot_general(
                lhs, twice(u_own[:, cols]) * right_rows[...], across, preferred_element_type=F32
            )
            prods2 = jnp.where(send_u, 0.0, prods2)
            for p in range(pairs):
                for e in range(2):
                    at = pl.ds(pl.multiple_of((q * per_chunk + 2 * p + e) * SUB, SUB), SUB)
                    cut = (slice(p * half, (p + 1) * half), slice(e * LANES, (e + 1) * LANES))
                    acc_t[at, :] = fold(prods[cut], 1)
                    acc[at, :] = acc[at, :] + fold(prods2[cut], 1)

        if part == halo_parts - 1:
            skewed = acc[pl.ds(0, groups, stride=SUB), :]
            skewed_t = acc_t[pl.ds(0, groups, stride=SUB), :]
            for r in range(1, SUB):
                turn = LANES - r
                skewed = skewed + pltpu.roll(acc[pl.ds(r, groups, stride=SUB), :], turn, 1)
                skewed_t = skewed_t + pltpu.roll(acc_t[pl.ds(r, groups, stride=SUB), :], turn, 1)
            skewed_t = pltpu.roll(skewed_t, half, 1)
            by_tap = lax.dot_general(
                flip, skewed, across, precision=lax.Precision.HIGHEST, preferred_element_type=F32
            ) + lax.dot_general(
                eye, skewed_t, across, precision=lax.Precision.HIGHEST, preferred_element_type=F32
            )
            piece = rows // ctx_count
            for i in range(ctx_count):
                partial[i] = by_tap[i * piece : (i + 1) * piece, :]

            def gf_copy(step):
                peer = lax.rem(me + step, ctx_count)
                return pltpu.make_async_remote_copy(
                    src_ref=partial.at[peer],
                    dst_ref=gf_slots.at[step - 1],
                    send_sem=gf_send.at[step - 1],
                    recv_sem=gf_recv.at[step - 1],
                    device_id={"ctx": peer},
                    device_id_type=MESH,
                )

            @pl.loop(1, ctx_count)
            def _(step):
                gf_copy(step).start()

        if part == 0:

            @pl.when(has_prev)
            def _():
                carry_copy(True).wait_recv()

        @pl.loop(part * per_part, (part + 1) * per_part, unroll=4)
        def _(q):
            cols = chunk_cols(q)
            rate = rate_ref[:, cols]
            u_msg, g_msg = u_in[:, cols], g_in[:, cols]
            y = jnp.dot(
                quad_bands(circ_f, q, True), four(u_msg) * quad_u[...], preferred_element_type=F32
            )
            y = pick(y, rows, quad_of_lane)
            y_part = jnp.where(send_gpart, 0.0, u_msg.astype(F32))
            y = y + jnp.concatenate([y_part, jnp.zeros_like(y_part)], axis=0)
            y = y_own[:, cols] + jnp.where(row < left_b, y, 0.0)
            out, _ = scan_tiles(
                y.astype(BF16).astype(F32), rate, True, carry_f_in[:, cols]
            )
            z_long = (scale[:, cols] * jnp.concatenate(out, axis=0)).astype(BF16)
            mixed_ref[:, cols] = (gate_ref[:, cols].astype(F32) * z_long.astype(F32)).astype(BF16)
            gu = jnp.dot(
                quad_bands(circ_b, q, False), four(g_msg) * quad_g[...], preferred_element_type=F32
            )
            gu = pick(gu, rows, quad_of_lane)
            g_part = jnp.where(send_u, g_msg.astype(F32), 0.0)
            gu = gu + jnp.concatenate([jnp.zeros_like(g_part), g_part], axis=0)
            gu = gu_own[:, cols] + jnp.where(row >= rows - right_a, gu, 0.0)
            gv_ref[:, cols] = (k_ref[:, cols].astype(F32) * gu).astype(BF16)

    def add_slot(step, value):
        gf_copy(step).wait_recv()
        return value + gf_slots[step - 1]

    gf_ref[...] = lax.fori_loop(1, ctx_count, add_slot, partial[me])

    @pl.loop(1, ctx_count)
    def _(step):
        gf_copy(step).wait_send()

    @pl.when(has_prev)
    def _():
        carry_copy(False).wait_send()
        for part in range(halo_parts):
            halo_copy(part, False).wait_send()

    @pl.when(has_next)
    def _():
        carry_copy(True).wait_send()
        for part in range(halo_parts):
            halo_copy(part, True).wait_send()


def short_call(args, ctx_count):
    rows, width = args[1].shape
    taps, groups = args[3].shape
    halo_parts = 4
    half = rows // 2
    vmem = pl.BlockSpec(memory_space=pltpu.VMEM)
    dma = pltpu.SemaphoreType.DMA
    piece = taps // ctx_count
    pairs = LANES // (width // groups) // 2
    wide = lambda r, t: pltpu.VMEM((r, width), t)
    square = lambda n, t: pltpu.VMEM((n, LANES), t)
    return pl.pallas_call(
        functools.partial(short_kernel, ctx_count, halo_parts),
        out_shape=(
            jax.ShapeDtypeStruct((rows, width), BF16),
            jax.ShapeDtypeStruct((rows, width), BF16),
            jax.ShapeDtypeStruct((piece, groups), F32),
        ),
        in_specs=[pl.BlockSpec(memory_space=pltpu.SMEM)] + [vmem] * 7,
        out_specs=(vmem, vmem, vmem),
        scratch_shapes=[
            wide(rows, BF16), wide(rows, BF16),
            wide(half, BF16), wide(half, BF16), wide(half, BF16), wide(half, BF16),
            wide(rows, F32), wide(rows, F32), wide(rows, F32),
            square(groups * rows, BF16), square(groups * rows, BF16),
            wide(1, F32), pltpu.VMEM((groups, taps), F32), pltpu.VMEM((groups, taps), F32),
            square(rows, BF16), square(rows, BF16), square(rows, F32),
            pltpu.VMEM((10, rows, LANES), F32),
            square(2 * rows, BF16), pltpu.VMEM((pairs, rows, LANES), BF16),
            square(2 * rows, BF16), square(2 * rows, BF16),
            square(2 * rows, BF16), square(2 * rows, BF16),
            square(SUB * groups, F32), square(SUB * groups, F32),
            pltpu.VMEM((ctx_count, piece, groups), F32),
            pltpu.VMEM((ctx_count - 1, piece, groups), F32),
            wide(1, F32), wide(1, F32), wide(1, F32), wide(1, F32),
            dma((halo_parts,)), dma((halo_parts,)), dma((halo_parts,)), dma((halo_parts,)),
            dma((1,)), dma((1,)), dma((1,)), dma((1,)),
            dma((ctx_count - 1,)), dma((ctx_count - 1,)),
        ],
        compiler_params=pltpu.CompilerParams(
            collective_id=1, has_side_effects=True, vmem_limit_bytes=60 * 1024 * 1024
        ),
        name="hyena_mixers_short",
    )(*args)


def on_device(k_short, v_short, mr_filter, li_rate, li_residue, gate_out, contig_lengths, grad_out):
    rows, width = k_short.shape
    taps, groups = mr_filter.shape
    ctx_count = lax.axis_size("ctx")
    total = rows * ctx_count
    reach = min(ctx_count - 1, -(-(total // 4) // rows))
    args = (
        contig_lengths, k_short, v_short, mr_filter, li_rate[None], li_residue[None],
        gate_out, grad_out,
    )
    if total // 4 <= rows == taps == LANES:
        return short_call(args, ctx_count)
    halo_parts = 4
    vmem = pl.BlockSpec(memory_space=pltpu.VMEM)
    dma = pltpu.SemaphoreType.DMA
    piece = taps // ctx_count
    return pl.pallas_call(
        functools.partial(kernel, ctx_count, reach, halo_parts),
        out_shape=(
            jax.ShapeDtypeStruct((rows, width), BF16),
            jax.ShapeDtypeStruct((rows, width), BF16),
            jax.ShapeDtypeStruct((piece, groups), F32),
        ),
        in_specs=[pl.BlockSpec(memory_space=pltpu.SMEM)] + [vmem] * 7,
        out_specs=(vmem, vmem, vmem),
        scratch_shapes=[
            pltpu.VMEM((2 * rows, width), BF16),
            pltpu.VMEM((2 * rows, width), BF16),
            pltpu.VMEM((rows, width), F32),
            pltpu.VMEM((rows, width), F32),
            pltpu.VMEM((1, width), F32),
            pltpu.VMEM((groups, taps), F32),
            pltpu.VMEM((groups, taps), F32),
            pltpu.VMEM((rows, 2 * LANES), BF16),
            pltpu.VMEM((rows, 2 * LANES), BF16),
            pltpu.VMEM((rows, LANES), F32),
            pltpu.VMEM((10, rows, LANES), F32),
            pltpu.VMEM((SUB * groups, taps), F32),
            pltpu.VMEM((ctx_count, piece, groups), F32),
            pltpu.VMEM((ctx_count - 1, piece, groups), F32),
            pltpu.VMEM((1, width), F32),
            pltpu.VMEM((1, width), F32),
            pltpu.VMEM((reach, 1, width), F32),
            pltpu.VMEM((reach, 1, width), F32),
            dma((halo_parts,)), dma((halo_parts,)), dma((halo_parts,)), dma((halo_parts,)),
            dma((reach,)), dma((reach,)), dma((reach,)), dma((reach,)),
            dma((ctx_count - 1,)), dma((ctx_count - 1,)),
        ],
        compiler_params=pltpu.CompilerParams(collective_id=0, has_side_effects=True),
        name="hyena_mixers",
    )(*args)


def solution(mesh):
    in_specs = (
        P(("dp", "ctx"), "tp"),
        P(("dp", "ctx"), "tp"),
        P(None, "tp"),
        P("tp"),
        P("tp"),
        P(("dp", "ctx"), "tp"),
        P("dp"),
        P(("dp", "ctx"), "tp"),
    )
    out_specs = (P(("dp", "ctx"), "tp"), P(("dp", "ctx"), "tp"), P(("dp", "ctx"), "tp"))
    return jax.shard_map(
        on_device, mesh=mesh, in_specs=in_specs, out_specs=out_specs, check_vma=False
    )
```

```python
import functools

import jax
import jax.numpy as jnp
from jax import lax
from jax.experimental import pallas as pl
from jax.experimental.pallas import tpu as pltpu
from jax.sharding import PartitionSpec as P

MESH = pl.DeviceIdType.MESH
LANES = 128
SUB = 8
HALO_PARTS = 8
F32 = jnp.float32
BF16 = jnp.bfloat16


def seg_of(lengths_ref, places, total):
    offset = jnp.int32(0)
    seg = jnp.zeros(places.shape, jnp.int32)
    for i in range(lengths_ref.shape[0]):
        seg = seg + (places >= offset).astype(jnp.int32)
        offset = offset + lengths_ref[i]
    return seg + (places >= total).astype(jnp.int32)


def one_minus_exp(x):
    series = jnp.ones_like(x)
    for n in range(9, 1, -1):
        series = 1.0 - x / n * series
    return jnp.where(x < 0.5, x * series, 1.0 - jnp.exp(-x))


def kernel(
    ctx_count, reach, halo_parts,
    lengths, k_ref, v_ref, filt_ref, rate_ref, residue_ref, gate_ref, gout_ref,
    mixed_ref, gv_ref, gf_ref,
    u_ext, g_ext, adj, state, scale, taps, taps_rev, mask_f, mask_b, diag_seg,
    scan_masks, acc, partial, gf_slots, carry_f, carry_b, carry_f_in, carry_b_in,
    u_send, u_recv, g_send, g_recv, cf_send, cf_recv, cb_send, cb_recv, gf_send, gf_recv,
):
    rows, width = k_ref.shape
    groups = filt_ref.shape[1]
    per_group = width // groups
    per_chunk = LANES // per_group
    chunks = width // LANES
    part_width = width // halo_parts
    total = rows * ctx_count
    me = lax.axis_index("ctx")
    first = me * rows

    barrier = pltpu.get_barrier_semaphore()

    @pl.loop(1, ctx_count)
    def _(step):
        pl.semaphore_signal(
            barrier, inc=1, device_id={"ctx": lax.rem(me + step, ctx_count)}, device_id_type=MESH
        )

    pl.semaphore_wait(barrier, ctx_count - 1)

    def u_copy(part):
        cols = pl.ds(part * part_width, part_width)
        return pltpu.make_async_remote_copy(
            src_ref=u_ext.at[pl.ds(rows, rows), cols],
            dst_ref=u_ext.at[pl.ds(0, rows), cols],
            send_sem=u_send.at[part],
            recv_sem=u_recv.at[part],
            device_id={"ctx": lax.rem(me + 1, ctx_count)},
            device_id_type=MESH,
        )

    def g_copy(part):
        cols = pl.ds(part * part_width, part_width)
        return pltpu.make_async_remote_copy(
            src_ref=g_ext.at[pl.ds(0, rows), cols],
            dst_ref=g_ext.at[pl.ds(rows, rows), cols],
            send_sem=g_send.at[part],
            recv_sem=g_recv.at[part],
            device_id={"ctx": lax.rem(me + ctx_count - 1, ctx_count)},
            device_id_type=MESH,
        )

    def carry_copy(k, forward):
        src, dst, send, recv = (
            (carry_f, carry_f_in, cf_send, cf_recv)
            if forward
            else (carry_b, carry_b_in, cb_send, cb_recv)
        )
        peer = me + 1 + k if forward else me + ctx_count - 1 - k
        return pltpu.make_async_remote_copy(
            src_ref=src,
            dst_ref=dst.at[k],
            send_sem=send.at[k],
            recv_sem=recv.at[k],
            device_id={"ctx": lax.rem(peer, ctx_count)},
            device_id_type=MESH,
        )

    for part in range(halo_parts):
        cols = slice(part * part_width, (part + 1) * part_width)
        u_ext[rows:, cols] = (k_ref[:, cols].astype(F32) * v_ref[:, cols].astype(F32)).astype(BF16)

        @pl.when(me < ctx_count - 1)
        def _():
            u_copy(part).start()

    @pl.when(me == 0)
    def _():
        u_ext[:rows, :] = jnp.zeros((rows, width), BF16)

    @pl.when(me == ctx_count - 1)
    def _():
        g_ext[rows:, :] = jnp.zeros((rows, width), BF16)

    rate_all = rate_ref[...]
    scale[...] = residue_ref[...] * jnp.sqrt(one_minus_exp(2.0 * rate_all))
    row = lax.broadcasted_iota(jnp.int32, (rows, LANES), 0)
    seg = seg_of(lengths, first + row, total)
    sub = lax.rem(row, SUB)
    tile = row - sub
    for i, k in enumerate((1, 2, 4)):
        same = (seg == pltpu.roll(seg, k, 0)) & (sub >= k)
        scan_masks[i] = same.astype(F32)
        same = (seg == pltpu.roll(seg, rows - k, 0)) & (sub + k < SUB)
        scan_masks[4 + i] = same.astype(F32)
    scan_masks[3] = (seg == seg_of(lengths, first + tile - 1, total)).astype(F32)
    scan_masks[7] = (seg == seg_of(lengths, first + tile + SUB, total)).astype(F32)
    lane_one = jnp.zeros((1, LANES), jnp.int32)
    seg_before = seg_of(lengths, first - 1 + lane_one, total)
    seg_after = seg_of(lengths, first + rows + lane_one, total)
    scan_masks[8] = (seg == seg_before).astype(F32)
    scan_masks[9] = (seg == seg_after).astype(F32)
    lane = lax.broadcasted_iota(jnp.int32, (rows, LANES), 1)
    lane_row = lax.broadcasted_iota(jnp.int32, (1, LANES), 1)
    seg_prev = seg_of(lengths, first - rows + lane_row, total)
    seg_here = seg_of(lengths, first + lane_row, total)
    seg_next = seg_of(lengths, first + rows + lane_row, total)
    f_left = ((seg == seg_prev) & (lane > row)).astype(F32)
    f_right = ((seg == seg_here) & (lane <= row)).astype(F32)
    mask_f[:, :LANES] = f_left.astype(BF16)
    mask_f[:, LANES:] = f_right.astype(BF16)
    diag_seg[...] = f_left + f_right
    mask_b[:, :LANES] = ((seg == seg_here) & (lane >= row)).astype(F32).astype(BF16)
    mask_b[:, LANES:] = ((seg == seg_next) & (lane < row)).astype(F32).astype(BF16)
    flip = (lax.rem(row + lane, LANES) == 0).astype(F32)
    eye = (row == lane).astype(F32)
    over_taps = (((0,), (0,)), ((), ()))
    filt = filt_ref[...]
    taps[...] = lax.dot_general(filt, eye.astype(BF16), over_taps, preferred_element_type=F32)
    taps_rev[...] = lax.dot_general(filt, flip.astype(BF16), over_taps, preferred_element_type=F32)

    sub8 = lax.broadcasted_iota(jnp.int32, (SUB, LANES), 0).astype(F32)
    tiles = rows // SUB

    def chunk_cols(q):
        return pl.ds(pl.multiple_of(q * LANES, LANES), LANES)

    def scan_tiles(values, rate, forward):
        base = 0 if forward else 4
        steps = [jnp.exp(-k * rate) for k in (1.0, 2.0, 4.0)]
        far = jnp.exp(-((sub8 + 1.0) if forward else (SUB - sub8)) * rate)
        out = [None] * tiles
        carry = None
        for n in range(tiles) if forward else reversed(range(tiles)):
            here = slice(n * SUB, (n + 1) * SUB)
            x = values[here, :]
            for i, k in enumerate((1, 2, 4)):
                shifted = pltpu.roll(x, k if forward else SUB - k, 0)
                x = x + steps[i] * scan_masks[base + i, here, :] * shifted
            if carry is not None:
                x = x + far * scan_masks[base + 3, here, :] * carry
            carry = x[SUB - 1 : SUB, :] if forward else x[0:1, :]
            out[n] = x
        return out, carry

    def carried(slots, cols, rate, forward):
        value = slots[0, :, cols]
        for k in range(1, reach):
            edge = first - 1 - rows * k if forward else first + rows + rows * k
            there = seg_of(lengths, edge + lane_one, total)
            same = (there == (seg_before if forward else seg_after)).astype(F32)
            value = value + slots[k, :, cols] * same * jnp.exp(-float(rows * k) * rate)
        return value

    @pl.loop(0, chunks, unroll=4)
    def _(q):
        cols = chunk_cols(q)
        rate = rate_ref[:, cols]
        long = (scale[:, cols] * gate_ref[:, cols].astype(F32) * gout_ref[:, cols].astype(F32))
        out, carry = scan_tiles(long.astype(BF16).astype(F32), rate, False)
        for n in range(tiles):
            adj[n * SUB : (n + 1) * SUB, cols] = out[n]
        carry_b[:, cols] = carry

    for k in range(reach):

        @pl.when(me >= 1 + k)
        def _():
            carry_copy(k, False).start()

        @pl.when(me + 1 + k >= ctx_count)
        def _():
            carry_b_in[k] = jnp.zeros((1, width), F32)

    for k in range(reach):

        @pl.when(me + 1 + k < ctx_count)
        def _():
            carry_copy(k, False).wait_recv()

    for part in range(halo_parts):
        per_part = chunks // halo_parts

        @pl.loop(part * per_part, (part + 1) * per_part, unroll=4)
        def _(q):
            cols = chunk_cols(q)
            rate = rate_ref[:, cols]
            value = carried(carry_b_in, cols, rate, False)
            far = jnp.exp(-(SUB - sub8) * rate)
            eighth = jnp.exp(-float(SUB) * rate)
            for n in reversed(range(tiles)):
                here = slice(n * SUB, (n + 1) * SUB)
                x = adj[here, cols] + far * scan_masks[9, here, :] * value
                adj[here, cols] = x
                value = value * eighth
            g_ext[:rows, cols] = adj[:, cols].astype(BF16)

        @pl.when(me > 0)
        def _():
            g_copy(part).start()

    def bands(tap_rows, mask):
        blocks = []
        for g in range(per_chunk):
            skew = pltpu.roll(
                jnp.broadcast_to(tap_rows[g : g + 1, :], (SUB, LANES)), 0, 1,
                stride=1, stride_axis=0,
            )
            circ = jnp.concatenate(
                [skew] + [pltpu.roll(skew, n * SUB, 1) for n in range(1, tiles)], axis=0
            ).astype(BF16)
            blocks.append(
                jnp.concatenate([circ * mask[:, :LANES], circ * mask[:, LANES:]], axis=1)
            )
        return jnp.concatenate(blocks, axis=0)

    group_of_lane = lane // per_group

    for part in range(halo_parts):

        @pl.when(me > 0)
        def _():
            u_copy(part).wait_recv()

        @pl.loop(part * per_part, (part + 1) * per_part, unroll=2)
        def _(q):
            cols = chunk_cols(q)
            window = u_ext[:, cols]
            grads = g_ext[:rows, cols]
            group_rows = pl.ds(pl.multiple_of(q * per_chunk, per_chunk), per_chunk)
            all_y = jnp.dot(
                bands(taps_rev[group_rows, :], mask_f), window,
                preferred_element_type=F32,
            )
            y = all_y[:rows, :]
            for g in range(1, per_chunk):
                y = jnp.where(group_of_lane == g, all_y[g * rows : (g + 1) * rows, :], y)
            own = jnp.concatenate(
                [jnp.where(group_of_lane == g, grads, jnp.zeros_like(grads)) for g in range(per_chunk)],
                axis=0,
            )
            all_prod = lax.dot_general(
                own, window, (((1,), (1,)), ((), ())), preferred_element_type=F32
            )
            for g in range(per_chunk):
                prod = all_prod[g * rows : (g + 1) * rows, :]
                prod = jnp.where(lane <= row, prod[:, LANES:], prod[:, :LANES]) * diag_seg[...]
                folded = prod[:SUB, :]
                for n in range(1, tiles):
                    folded = folded + pltpu.roll(
                        prod[n * SUB : (n + 1) * SUB, :], LANES - n * SUB, 1
                    )
                acc[pl.ds(pl.multiple_of((q * per_chunk + g) * SUB, SUB), SUB), :] = folded
            out, carry = scan_tiles(y.astype(BF16).astype(F32), rate_ref[:, cols], True)
            for n in range(tiles):
                state[n * SUB : (n + 1) * SUB, cols] = out[n]
            carry_f[:, cols] = carry

    for k in range(reach):

        @pl.when(me + 1 + k < ctx_count)
        def _():
            carry_copy(k, True).start()

        @pl.when(me < 1 + k)
        def _():
            carry_f_in[k] = jnp.zeros((1, width), F32)

    skewed = acc[pl.ds(0, groups, stride=SUB), :]
    for r in range(1, SUB):
        skewed = skewed + pltpu.roll(acc[pl.ds(r, groups, stride=SUB), :], LANES - r, 1)
    by_tap = lax.dot_general(
        flip, skewed, (((1,), (1,)), ((), ())),
        precision=lax.Precision.HIGHEST, preferred_element_type=F32,
    )
    piece = rows // ctx_count
    for i in range(ctx_count):
        partial[i] = by_tap[i * piece : (i + 1) * piece, :]

    def gf_copy(step):
        peer = lax.rem(me + step, ctx_count)
        return pltpu.make_async_remote_copy(
            src_ref=partial.at[peer],
            dst_ref=gf_slots.at[step - 1],
            send_sem=gf_send.at[step - 1],
            recv_sem=gf_recv.at[step - 1],
            device_id={"ctx": peer},
            device_id_type=MESH,
        )

    @pl.loop(1, ctx_count)
    def _(step):
        gf_copy(step).start()

    def finish_forward():
        for k in range(reach):

            @pl.when(me >= 1 + k)
            def _():
                carry_copy(k, True).wait_recv()

        @pl.loop(0, chunks, unroll=4)
        def _(q):
            cols = chunk_cols(q)
            rate = rate_ref[:, cols]
            value = carried(carry_f_in, cols, rate, True)
            far = jnp.exp(-(sub8 + 1.0) * rate)
            eighth = jnp.exp(-float(SUB) * rate)
            for n in range(tiles):
                here = slice(n * SUB, (n + 1) * SUB)
                x = state[here, cols] + far * scan_masks[8, here, :] * value
                state[here, cols] = x
                value = value * eighth
            z_long = (scale[:, cols] * state[:, cols]).astype(BF16)
            mixed_ref[:, cols] = (gate_ref[:, cols].astype(F32) * z_long.astype(F32)).astype(BF16)

    for part in range(halo_parts):

        @pl.when(me < ctx_count - 1)
        def _():
            g_copy(part).wait_recv()

        @pl.loop(part * per_part, (part + 1) * per_part, unroll=2)
        def _(q):
            cols = chunk_cols(q)
            window = g_ext[:, cols]
            group_rows = pl.ds(pl.multiple_of(q * per_chunk, per_chunk), per_chunk)
            all_u = jnp.dot(
                bands(taps[group_rows, :], mask_b), window,
                preferred_element_type=F32,
            )
            grad_u = all_u[:rows, :]
            for g in range(1, per_chunk):
                grad_u = jnp.where(group_of_lane == g, all_u[g * rows : (g + 1) * rows, :], grad_u)
            gv_ref[:, cols] = (k_ref[:, cols].astype(F32) * grad_u).astype(BF16)

        if part == (halo_parts - 1) // 2:
            finish_forward()

    own = partial[me]

    def add_slot(step, value):
        gf_copy(step).wait_recv()
        return value + gf_slots[step - 1]

    gf_ref[...] = lax.fori_loop(1, ctx_count, add_slot, own)

    @pl.loop(1, ctx_count)
    def _(step):
        gf_copy(step).wait_send()

    for k in range(reach):

        @pl.when(me >= 1 + k)
        def _():
            carry_copy(k, False).wait_send()

        @pl.when(me + 1 + k < ctx_count)
        def _():
            carry_copy(k, True).wait_send()

    for part in range(halo_parts):

        @pl.when(me < ctx_count - 1)
        def _():
            u_copy(part).wait_send()

        @pl.when(me > 0)
        def _():
            g_copy(part).wait_send()


def crossing(lengths_ref, edge):
    offset = jnp.int32(0)
    before = jnp.int32(0)
    after = jnp.int32(0)
    for i in range(lengths_ref.shape[0]):
        end = offset + lengths_ref[i]
        inside = (offset < edge) & (end > edge)
        before = jnp.where(inside, edge - offset, before)
        after = jnp.where(inside, end - edge, after)
        offset = end
    return before, after


def short_kernel(
    ctx_count, halo_parts,
    lengths, k_hbm, v_hbm, filt_ref, rate_ref, residue_ref, gate_hbm, gout_hbm,
    mixed_ref, gv_ref, gf_ref,
    k_ref, v_ref, gate_ref, gout_ref, load,
    u_own, g_own, u_out, g_out, u_in, g_in, relay, adj, y_own, gu_own, circ_f, circ_b,
    scale, taps, taps_rev, mask_f, mask_b, diag_seg, scan_masks, even_odd, pair_lanes,
    right_rows, left_rows, even_odd_t, left_t, right_t, quad_u, quad_g, u_t, g_t, acc, acc_t, partial, gf_slots,
    carry_f, carry_b, carry_f_in, carry_b_in,
    u_send, u_recv, g_send, g_recv, cf_send, cf_recv, cb_send, cb_recv,
    relay_send, relay_recv, gf_send, gf_recv,
):
    rows, width = k_ref.shape
    groups = filt_ref.shape[1]
    half = rows // 2
    per_group = width // groups
    per_chunk = LANES // per_group
    pairs = per_chunk // 2
    chunks = width // LANES
    per_part = chunks // halo_parts
    part_width = width // halo_parts
    total = rows * ctx_count
    tiles = rows // SUB
    me = lax.axis_index("ctx")
    first = me * rows
    has_next = me < ctx_count - 1
    has_prev = me > 0

    loads = [
        pltpu.make_async_copy(src, dst, load.at[n])
        for n, (src, dst) in enumerate(
            ((gate_hbm, gate_ref), (gout_hbm, gout_ref), (k_hbm, k_ref), (v_hbm, v_ref))
        )
    ]
    for one in loads:
        one.start()

    barrier = pltpu.get_barrier_semaphore()

    @pl.loop(1, ctx_count)
    def _(step):
        pl.semaphore_signal(
            barrier, inc=1, device_id={"ctx": lax.rem(me + step, ctx_count)}, device_id_type=MESH
        )

    def halo_copy(part, forward):
        src, dst, send, recv = (
            (u_out, u_in, u_send, u_recv) if forward else (g_out, g_in, g_send, g_recv)
        )
        cols = pl.ds(pl.multiple_of(part * part_width, LANES), part_width)
        peer = me + 1 if forward else me + ctx_count - 1
        return pltpu.make_async_remote_copy(
            src_ref=src.at[:, cols],
            dst_ref=dst.at[:, cols],
            send_sem=send.at[part],
            recv_sem=recv.at[part],
            device_id={"ctx": lax.rem(peer, ctx_count)},
            device_id_type=MESH,
        )

    def carry_b_copy():
        return pltpu.make_async_remote_copy(
            src_ref=carry_b,
            dst_ref=carry_b_in,
            send_sem=cb_send.at[0],
            recv_sem=cb_recv.at[0],
            device_id={"ctx": lax.rem(me + ctx_count - 1, ctx_count)},
            device_id_type=MESH,
        )

    def carry_f_copy(part):
        cols = pl.ds(pl.multiple_of(part * part_width, LANES), part_width)
        return pltpu.make_async_remote_copy(
            src_ref=carry_f.at[:, cols],
            dst_ref=carry_f_in.at[:, cols],
            send_sem=cf_send.at[part],
            recv_sem=cf_recv.at[part],
            device_id={"ctx": lax.rem(me + 1, ctx_count)},
            device_id_type=MESH,
        )

    relays = False

    def relay_copy(part, forward):
        cols = pl.ds(pl.multiple_of(part * part_width, LANES), part_width)
        src, send = (u_out, u_send) if forward else (g_out, g_send)
        return pltpu.make_async_remote_copy(
            src_ref=src.at[:, cols],
            dst_ref=relay.at[:, cols],
            send_sem=send.at[part],
            recv_sem=relay_recv.at[part],
            device_id={"ctx": 3 if forward else 0},
            device_id_type=MESH,
        )

    def onward_copy(part, forward):
        cols = pl.ds(pl.multiple_of(part * part_width, LANES), part_width)
        dst, recv = (u_in, u_recv) if forward else (g_in, g_recv)
        return pltpu.make_async_remote_copy(
            src_ref=relay.at[:, cols],
            dst_ref=dst.at[:, cols],
            send_sem=relay_send.at[part],
            recv_sem=recv.at[part],
            device_id={"ctx": 2 if forward else 1},
            device_id_type=MESH,
        )

    @pl.when(jnp.logical_not(has_prev))
    def _():
        u_in[...] = jnp.zeros(u_in.shape, BF16)
        carry_f_in[...] = jnp.zeros(carry_f_in.shape, F32)

    @pl.when(jnp.logical_not(has_next))
    def _():
        g_in[...] = jnp.zeros(g_in.shape, BF16)
        carry_b_in[...] = jnp.zeros(carry_b_in.shape, F32)

    left_a, left_b = crossing(lengths, first)
    right_a, right_b = crossing(lengths, first + rows)

    rate_all = rate_ref[...]
    scale[...] = residue_ref[...] * jnp.sqrt(one_minus_exp(2.0 * rate_all))
    row = lax.broadcasted_iota(jnp.int32, (rows, LANES), 0)
    lane = lax.broadcasted_iota(jnp.int32, (rows, LANES), 1)
    lane_row = lax.broadcasted_iota(jnp.int32, (1, LANES), 1)
    row_half = lax.broadcasted_iota(jnp.int32, (half, LANES), 0)
    lane_half = lax.broadcasted_iota(jnp.int32, (half, LANES), 1)
    seg = seg_of(lengths, first + row, total)
    sub = lax.rem(row, SUB)
    tile = row - sub
    for i, k in enumerate((1, 2, 4)):
        same = (seg == pltpu.roll(seg, k, 0)) & (sub >= k)
        scan_masks[i] = same.astype(F32)
        same = (seg == pltpu.roll(seg, rows - k, 0)) & (sub + k < SUB)
        scan_masks[4 + i] = same.astype(F32)
    scan_masks[3] = (seg == seg_of(lengths, first + tile - 1, total)).astype(F32)
    scan_masks[7] = (seg == seg_of(lengths, first + tile + SUB, total)).astype(F32)
    lane_one = jnp.zeros((1, LANES), jnp.int32)
    scan_masks[8] = (seg == seg_of(lengths, first + rows - 1 + lane_one, total)).astype(F32)
    scan_masks[9] = (seg == seg_of(lengths, first + rows + lane_one, total)).astype(F32)
    seg_here = seg_of(lengths, first + lane_row, total)
    own = ((seg == seg_here) & (lane <= row)).astype(F32)
    mask_f[...] = own.astype(BF16)
    diag_seg[...] = own
    mask_b[...] = ((seg == seg_here) & (lane >= row)).astype(F32).astype(BF16)

    group_of_lane = lane // per_group
    pair_of_lane = group_of_lane // 2
    send_u = right_a <= half
    send_gpart = left_a <= half
    for e in range(2):
        lanes = lax.rem(group_of_lane, 2) == e
        even_odd[e * rows : (e + 1) * rows, :] = lanes.astype(F32).astype(BF16)
        right_rows[e * rows : (e + 1) * rows, :] = (
            (lanes & (row >= rows - right_a)).astype(F32).astype(BF16)
        )
        left_rows[e * rows : (e + 1) * rows, :] = (
            (lanes & (row < left_b)).astype(F32).astype(BF16)
        )
    group_of_row = row // per_group
    for e in range(2):
        rows_e = lax.rem(group_of_row, 2) == e
        at = slice(e * LANES, (e + 1) * LANES)
        even_odd_t[:, at] = rows_e.astype(F32).astype(BF16)
        left_t[:, at] = jnp.where(
            send_gpart, (rows_e & (lane < left_b)).astype(F32), 0.0
        ).astype(BF16)
        right_t[:, at] = jnp.where(
            send_u, 0.0, (rows_e & (lane >= rows - right_a)).astype(F32)
        ).astype(BF16)
    for p in range(pairs):
        pair_lanes[p] = (pair_of_lane == p).astype(F32).astype(BF16)
    group_half = lane_half // per_group
    for e in range(4):
        lanes = lax.rem(group_half, 4) == e
        quad_u[e * half : (e + 1) * half, :] = (
            jnp.where(send_gpart, lanes.astype(F32), 0.0).astype(BF16)
        )
        quad_g[e * half : (e + 1) * half, :] = (
            jnp.where(send_u, 0.0, lanes.astype(F32)).astype(BF16)
        )

    flip = (lax.rem(row + lane, LANES) == 0).astype(F32)
    eye = (row == lane).astype(F32)
    over_taps = (((0,), (0,)), ((), ()))
    filt = filt_ref[...]
    taps[...] = lax.dot_general(filt, eye.astype(BF16), over_taps, preferred_element_type=F32)
    taps_rev[...] = lax.dot_general(filt, flip.astype(BF16), over_taps, preferred_element_type=F32)
    sub8 = lax.broadcasted_iota(jnp.int32, (SUB, LANES), 0).astype(F32)

    def chunk_cols(q):
        return pl.ds(pl.multiple_of(q * LANES, LANES), LANES)

    def group_rows(q, g):
        return pl.ds(pl.multiple_of((q * per_chunk + g) * rows, rows), rows)

    def scan_tiles(values, rate, forward, carry=None):
        base = 0 if forward else 4
        steps = [jnp.exp(-k * rate) for k in (1.0, 2.0, 4.0)]
        far = jnp.exp(-((sub8 + 1.0) if forward else (SUB - sub8)) * rate)
        out = [None] * tiles
        for n in range(tiles) if forward else reversed(range(tiles)):
            here = slice(n * SUB, (n + 1) * SUB)
            x = values[here, :]
            for i, k in enumerate((1, 2, 4)):
                shifted = pltpu.roll(x, k if forward else SUB - k, 0)
                x = x + steps[i] * scan_masks[base + i, here, :] * shifted
            if carry is not None:
                x = x + far * scan_masks[base + 3, here, :] * carry
            carry = x[SUB - 1 : SUB, :] if forward else x[0:1, :]
            out[n] = x
        return out, carry

    def circulant(tap_rows, g):
        skew = pltpu.roll(
            jnp.broadcast_to(tap_rows[g : g + 1, :], (2 * SUB, LANES)), 0, 1,
            stride=1, stride_axis=0,
        ).astype(BF16)
        return jnp.concatenate(
            [skew] + [pltpu.roll(skew, 2 * n * SUB, 1) for n in range(1, tiles // 2)], axis=0
        )

    def pick(outs, n_rows, index):
        value = outs[:n_rows, :]
        for p in range(1, outs.shape[0] // n_rows):
            value = jnp.where(index == p, outs[p * n_rows : (p + 1) * n_rows, :], value)
        return value

    def beside(x):
        return jnp.concatenate([x, x], axis=1)

    def twice(x):
        return jnp.concatenate([x, x], axis=0)

    def fold(prod):
        folded = prod[:SUB, :]
        for n in range(1, prod.shape[0] // SUB):
            folded = folded + pltpu.roll(prod[n * SUB : (n + 1) * SUB, :], LANES - n * SUB, 1)
        return folded

    pair_half = lane_half // (2 * per_group)
    across = (((1,), (1,)), ((), ()))

    for one in loads:
        one.wait()

    @pl.loop(0, halo_parts)
    def _(part):
        for c in range(per_part):
            cols = chunk_cols(part * per_part + c)
            long = scale[:, cols] * gate_ref[:, cols].astype(F32) * gout_ref[:, cols].astype(F32)
            out, carry = scan_tiles(long.astype(BF16).astype(F32), rate_ref[:, cols], False)
            for n in range(tiles):
                adj[n * SUB : (n + 1) * SUB, cols] = out[n]
            carry_b[:, cols] = carry
            u_own[:, cols] = (k_ref[:, cols].astype(F32) * v_ref[:, cols].astype(F32)).astype(BF16)

    pl.semaphore_wait(barrier, ctx_count - 1)

    @pl.when(has_prev)
    def _():
        carry_b_copy().start()

    def join(xs):
        return jnp.concatenate(
            [jnp.concatenate(xs[2 * p : 2 * p + 2], axis=1) for p in range(pairs)], axis=0
        )

    def pair_bands(circ, q, mask):
        return jnp.concatenate(
            [
                jnp.concatenate(
                    [circ[group_rows(q, 2 * p + e), :] * mask for e in range(2)], axis=1
                )
                for p in range(pairs)
            ],
            axis=0,
        )

    def own_y(q):
        cols = chunk_cols(q)
        rate = rate_ref[:, cols]
        y = jnp.dot(
            pair_bands(circ_f, q, mask_f[...]), twice(u_own[:, cols]) * even_odd[...],
            preferred_element_type=F32,
        )
        y = pick(y, rows, pair_of_lane)
        y_own[:, cols] = y
        last = y.astype(BF16).astype(F32) * scan_masks[8]
        eighth = jnp.exp(-float(SUB) * rate)
        run = last[:SUB, :]
        for n in range(1, tiles):
            run = run * eighth + last[n * SUB : (n + 1) * SUB, :]
        carry_f[:, cols] = jnp.sum(
            run * jnp.exp(-(SUB - 1.0 - sub8) * rate), axis=0, keepdims=True
        )

    @pl.loop(0, halo_parts)
    def _(part):
        for c in range(per_part):
            q = part * per_part + c
            cols = chunk_cols(q)
            u = u_own[:, cols]
            g = adj[:, cols].astype(BF16)
            tap_rows = pl.ds(pl.multiple_of(q * per_chunk, per_chunk), per_chunk)
            f_rows, b_rows = taps_rev[tap_rows, :], taps[tap_rows, :]
            top, bottom = [], []
            for i in range(per_chunk):
                f, b = circulant(f_rows, i), circulant(b_rows, i)
                circ_f[group_rows(q, i), :] = f
                circ_b[group_rows(q, i), :] = b
                top.append(f[:half, :])
                bottom.append(b[half:, :])
            y_part = jnp.dot(join(top), twice(u) * right_rows[...], preferred_element_type=F32)
            y_part = pick(y_part, half, pair_half)
            g_part = jnp.dot(join(bottom), twice(g) * left_rows[...], preferred_element_type=F32)
            g_part = pick(g_part, half, pair_half)
            y_part = jnp.where(row_half < right_b, y_part, 0.0)
            g_part = jnp.where(row_half >= half - left_a, g_part, 0.0)
            u_tail = jnp.where(row_half >= half - right_a, u[half:, :].astype(F32), 0.0)
            g_head = jnp.where(row_half < left_b, g[:half, :].astype(F32), 0.0)
            u_out[:, cols] = jnp.where(send_u, u_tail, y_part).astype(BF16)
            g_out[:, cols] = jnp.where(send_gpart, g_part, g_head).astype(BF16)
            own_y(q)

        by_relay = lax.rem(part, 2) == 1 if relays else False

        @pl.when(has_next)
        def _():
            carry_f_copy(part).start()
            if relays:
                pl.when((me == 1) & by_relay)(lambda: relay_copy(part, True).start())
                pl.when((me != 1) | jnp.logical_not(by_relay))(
                    lambda: halo_copy(part, True).start()
                )
            else:
                halo_copy(part, True).start()

        @pl.when(has_prev)
        def _():
            if relays:
                pl.when((me == 2) & by_relay)(lambda: relay_copy(part, False).start())
                pl.when((me != 2) | jnp.logical_not(by_relay))(
                    lambda: halo_copy(part, False).start()
                )
            else:
                halo_copy(part, False).start()

    @pl.when(has_next)
    def _():
        carry_b_copy().wait_recv()

    def own_terms(q):
        cols = chunk_cols(q)
        rate = rate_ref[:, cols]
        value = carry_b_in[:, cols]
        far = jnp.exp(-(SUB - sub8) * rate)
        eighth = jnp.exp(-float(SUB) * rate)
        out = [None] * tiles
        for n in reversed(range(tiles)):
            here = slice(n * SUB, (n + 1) * SUB)
            out[n] = adj[here, cols] + far * scan_masks[9, here, :] * value
            value = value * eighth
        g = jnp.concatenate(out, axis=0).astype(BF16)
        g_own[:, cols] = g
        gu = jnp.dot(
            pair_bands(circ_b, q, mask_b[...]), twice(g) * even_odd[...],
            preferred_element_type=F32,
        )
        gu_own[:, cols] = pick(gu, rows, pair_of_lane)
        by_pair = jnp.concatenate([g * pair_lanes[p] for p in range(pairs)], axis=0)
        ut, gt = u_own[:, cols].T, g.T
        t_rows = pl.ds(pl.multiple_of(q * LANES, LANES), LANES)
        u_t[t_rows, :] = ut
        g_t[t_rows, :] = gt
        prods = jnp.dot(by_pair, beside(ut) * even_odd_t[...], preferred_element_type=F32)
        for p in range(pairs):
            for e in range(2):
                prod = prods[p * rows : (p + 1) * rows, e * LANES : (e + 1) * LANES]
                at = pl.multiple_of((q * per_chunk + 2 * p + e) * SUB, SUB)
                acc[pl.ds(at, SUB), :] = fold(prod * diag_seg[...])

    @pl.loop(0, halo_parts)
    def _(part):
        if relays:
            for forward, by in ((True, 3), (False, 0)):

                @pl.when((me == by) & (lax.rem(part, 2) == 1))
                def _():
                    relay_copy(part, forward).wait_recv()
                    onward_copy(part, forward).start()

        for c in range(per_part):
            own_terms(part * per_part + c)

    low_lanes = lane < half

    def quad_bands(circ, q, forward):
        quads = []
        for g in range(0, per_chunk, 4):
            halves = []
            for e in (0, 2):
                one = circ[group_rows(q, g + e), :]
                two = circ[group_rows(q, g + e + 1), :]
                if forward:
                    one = jnp.concatenate([one[half:, :], one[:half, :]], axis=0)
                else:
                    two = jnp.concatenate([two[half:, :], two[:half, :]], axis=0)
                halves.append(jnp.where(low_lanes, one, two))
            quads.append(jnp.concatenate(halves, axis=1))
        return jnp.concatenate(quads, axis=0)

    def four(x):
        return jnp.concatenate([x, x, x, x], axis=0)

    quad_of_lane = lane // (4 * per_group)

    def cross_terms(q):
        cols = chunk_cols(q)
        u_msg, g_msg = u_in[:, cols], g_in[:, cols]
        t_rows = pl.ds(pl.multiple_of(q * LANES, LANES), LANES)
        lhs = jnp.concatenate([u_msg * pair_lanes[p, :half, :] for p in range(pairs)], axis=0)
        prods = jnp.dot(lhs, beside(g_t[t_rows, :]) * left_t[...], preferred_element_type=F32)
        lhs = jnp.concatenate([g_msg * pair_lanes[p, :half, :] for p in range(pairs)], axis=0)
        prods2 = jnp.dot(lhs, beside(u_t[t_rows, :]) * right_t[...], preferred_element_type=F32)
        for p in range(pairs):
            for e in range(2):
                at = pl.ds(pl.multiple_of((q * per_chunk + 2 * p + e) * SUB, SUB), SUB)
                cut = (slice(p * half, (p + 1) * half), slice(e * LANES, (e + 1) * LANES))
                acc_t[at, :] = fold(prods[cut])
                acc[at, :] = acc[at, :] + fold(prods2[cut])

    def finish(q):
        cols = chunk_cols(q)
        u_msg, g_msg = u_in[:, cols], g_in[:, cols]
        rate = rate_ref[:, cols]
        y = jnp.dot(
            quad_bands(circ_f, q, True), four(u_msg) * quad_u[...], preferred_element_type=F32
        )
        y = pick(y, rows, quad_of_lane)
        y_part = jnp.where(send_gpart, 0.0, u_msg.astype(F32))
        y = y + jnp.concatenate([y_part, jnp.zeros_like(y_part)], axis=0)
        y = y_own[:, cols] + jnp.where(row < left_b, y, 0.0)
        out, _ = scan_tiles(
            y.astype(BF16).astype(F32), rate, True, carry_f_in[:, cols]
        )
        z_long = (scale[:, cols] * jnp.concatenate(out, axis=0)).astype(BF16)
        mixed_ref[:, cols] = (gate_ref[:, cols].astype(F32) * z_long.astype(F32)).astype(BF16)
        gu = jnp.dot(
            quad_bands(circ_b, q, False), four(g_msg) * quad_g[...], preferred_element_type=F32
        )
        gu = pick(gu, rows, quad_of_lane)
        g_part = jnp.where(send_u, g_msg.astype(F32), 0.0)
        gu = gu + jnp.concatenate([jnp.zeros_like(g_part), g_part], axis=0)
        gu = gu_own[:, cols] + jnp.where(row >= rows - right_a, gu, 0.0)
        gv_ref[:, cols] = (k_ref[:, cols].astype(F32) * gu).astype(BF16)

    @pl.loop(0, halo_parts)
    def _(part):
        @pl.when(has_prev)
        def _():
            carry_f_copy(part).wait_recv()
            halo_copy(part, True).wait_recv()

        @pl.when(has_next)
        def _():
            halo_copy(part, False).wait_recv()

        for c in range(per_part):
            cross_terms(part * per_part + c)

    skewed = acc[pl.ds(0, groups, stride=SUB), :]
    skewed_t = acc_t[pl.ds(0, groups, stride=SUB), :]
    for r in range(1, SUB):
        turn = LANES - r
        skewed = skewed + pltpu.roll(acc[pl.ds(r, groups, stride=SUB), :], turn, 1)
        skewed_t = skewed_t + pltpu.roll(acc_t[pl.ds(r, groups, stride=SUB), :], turn, 1)
    skewed_t = pltpu.roll(skewed_t, half, 1)
    by_tap = lax.dot_general(
        flip, skewed, across, precision=lax.Precision.HIGHEST, preferred_element_type=F32
    ) + lax.dot_general(
        eye, skewed_t, across, precision=lax.Precision.HIGHEST, preferred_element_type=F32
    )
    piece = rows // ctx_count
    for i in range(ctx_count):
        partial[i] = by_tap[i * piece : (i + 1) * piece, :]

    def gf_copy(step):
        peer = lax.rem(me + step, ctx_count)
        return pltpu.make_async_remote_copy(
            src_ref=partial.at[peer],
            dst_ref=gf_slots.at[step - 1],
            send_sem=gf_send.at[step - 1],
            recv_sem=gf_recv.at[step - 1],
            device_id={"ctx": peer},
            device_id_type=MESH,
        )

    @pl.loop(1, ctx_count)
    def _(step):
        gf_copy(step).start()

    @pl.loop(0, halo_parts)
    def _(part):
        for c in range(per_part):
            finish(part * per_part + c)

    def add_slot(step, value):
        gf_copy(step).wait_recv()
        return value + gf_slots[step - 1]

    gf_ref[...] = lax.fori_loop(1, ctx_count, add_slot, partial[me])

    @pl.loop(1, ctx_count)
    def _(step):
        gf_copy(step).wait_send()

    if relays:
        for forward, by in ((True, 3), (False, 0)):

            @pl.when(me == by)
            def _():
                for part in range(1, halo_parts, 2):
                    onward_copy(part, forward).wait_send()

    @pl.when(has_prev)
    def _():
        carry_b_copy().wait_send()
        for part in range(halo_parts):
            halo_copy(part, False).wait_send()

    @pl.when(has_next)
    def _():
        for part in range(halo_parts):
            carry_f_copy(part).wait_send()
            halo_copy(part, True).wait_send()


def write_out(*refs):
    copies = [
        pltpu.make_async_copy(refs[n], refs[3 + n], refs[6].at[n]) for n in range(3)
    ]
    for one in copies:
        one.start()
    for one in copies:
        one.wait()


def short_call(args, ctx_count):
    rows, width = args[1].shape
    taps, groups = args[3].shape
    halo_parts = HALO_PARTS
    half = rows // 2
    vmem = pl.BlockSpec(memory_space=pltpu.VMEM)
    hbm = pl.BlockSpec(memory_space=pltpu.HBM)
    dma = pltpu.SemaphoreType.DMA
    piece = taps // ctx_count
    pairs = LANES // (width // groups) // 2
    wide = lambda r, t: pltpu.VMEM((r, width), t)
    square = lambda n, t: pltpu.VMEM((n, LANES), t)
    keep = pltpu.with_memory_space_constraint
    args = [keep(x, pltpu.HBM) for x in args]
    results = pl.pallas_call(
        functools.partial(short_kernel, ctx_count, halo_parts),
        out_shape=(
            pltpu.VMEM((rows, width), BF16),
            pltpu.VMEM((rows, width), BF16),
            pltpu.VMEM((piece, groups), F32),
        ),
        in_specs=[pl.BlockSpec(memory_space=pltpu.SMEM)] + [hbm] * 2 + [vmem] * 3 + [hbm] * 2,
        out_specs=(vmem, vmem, vmem),
        scratch_shapes=[
            wide(rows, BF16), wide(rows, BF16), wide(rows, BF16), wide(rows, BF16), dma((4,)),
            wide(rows, BF16), wide(rows, BF16),
            wide(half, BF16), wide(half, BF16), wide(half, BF16), wide(half, BF16),
            wide(half, BF16),
            wide(rows, F32), wide(rows, F32), wide(rows, F32),
            square(groups * rows, BF16), square(groups * rows, BF16),
            wide(1, F32), pltpu.VMEM((groups, taps), F32), pltpu.VMEM((groups, taps), F32),
            square(rows, BF16), square(rows, BF16), square(rows, F32),
            pltpu.VMEM((10, rows, LANES), F32),
            square(2 * rows, BF16), pltpu.VMEM((pairs, rows, LANES), BF16),
            square(2 * rows, BF16), square(2 * rows, BF16),
            pltpu.VMEM((rows, 2 * LANES), BF16), pltpu.VMEM((rows, 2 * LANES), BF16),
            pltpu.VMEM((rows, 2 * LANES), BF16),
            square(2 * rows, BF16), square(2 * rows, BF16),
            square(width, BF16), square(width, BF16),
            square(SUB * groups, F32), square(SUB * groups, F32),
            pltpu.VMEM((ctx_count, piece, groups), F32),
            pltpu.VMEM((ctx_count - 1, piece, groups), F32),
            wide(1, F32), wide(1, F32), wide(1, F32), wide(1, F32),
            dma((halo_parts,)), dma((halo_parts,)), dma((halo_parts,)), dma((halo_parts,)),
            dma((halo_parts,)), dma((halo_parts,)), dma((1,)), dma((1,)),
            dma((halo_parts,)), dma((halo_parts,)),
            dma((ctx_count - 1,)), dma((ctx_count - 1,)),
        ],
        compiler_params=pltpu.CompilerParams(
            collective_id=1, has_side_effects=True, vmem_limit_bytes=48 * 1024 * 1024
        ),
        name="hyena_mixers_short",
    )(*args)
    return pl.pallas_call(
        write_out,
        out_shape=tuple(jax.ShapeDtypeStruct(x.shape, x.dtype) for x in results),
        in_specs=[vmem] * 3,
        out_specs=(hbm,) * 3,
        scratch_shapes=[dma((3,))],
        name="write_out",
    )(*[keep(x, pltpu.VMEM) for x in results])


def on_device(k_short, v_short, mr_filter, li_rate, li_residue, gate_out, contig_lengths, grad_out):
    rows, width = k_short.shape
    taps, groups = mr_filter.shape
    ctx_count = lax.axis_size("ctx")
    total = rows * ctx_count
    reach = min(ctx_count - 1, -(-(total // 4) // rows))
    args = (
        contig_lengths, k_short, v_short, mr_filter, li_rate[None], li_residue[None],
        gate_out, grad_out,
    )
    if total // 4 <= rows == taps == LANES:
        return short_call(args, ctx_count)
    halo_parts = 4
    vmem = pl.BlockSpec(memory_space=pltpu.VMEM)
    dma = pltpu.SemaphoreType.DMA
    piece = taps // ctx_count
    return pl.pallas_call(
        functools.partial(kernel, ctx_count, reach, halo_parts),
        out_shape=(
            jax.ShapeDtypeStruct((rows, width), BF16),
            jax.ShapeDtypeStruct((rows, width), BF16),
            jax.ShapeDtypeStruct((piece, groups), F32),
        ),
        in_specs=[pl.BlockSpec(memory_space=pltpu.SMEM)] + [vmem] * 7,
        out_specs=(vmem, vmem, vmem),
        scratch_shapes=[
            pltpu.VMEM((2 * rows, width), BF16),
            pltpu.VMEM((2 * rows, width), BF16),
            pltpu.VMEM((rows, width), F32),
            pltpu.VMEM((rows, width), F32),
            pltpu.VMEM((1, width), F32),
            pltpu.VMEM((groups, taps), F32),
            pltpu.VMEM((groups, taps), F32),
            pltpu.VMEM((rows, 2 * LANES), BF16),
            pltpu.VMEM((rows, 2 * LANES), BF16),
            pltpu.VMEM((rows, LANES), F32),
            pltpu.VMEM((10, rows, LANES), F32),
            pltpu.VMEM((SUB * groups, taps), F32),
            pltpu.VMEM((ctx_count, piece, groups), F32),
            pltpu.VMEM((ctx_count - 1, piece, groups), F32),
            pltpu.VMEM((1, width), F32),
            pltpu.VMEM((1, width), F32),
            pltpu.VMEM((reach, 1, width), F32),
            pltpu.VMEM((reach, 1, width), F32),
            dma((halo_parts,)), dma((halo_parts,)), dma((halo_parts,)), dma((halo_parts,)),
            dma((reach,)), dma((reach,)), dma((reach,)), dma((reach,)),
            dma((ctx_count - 1,)), dma((ctx_count - 1,)),
        ],
        compiler_params=pltpu.CompilerParams(collective_id=0, has_side_effects=True),
        name="hyena_mixers",
    )(*args)


def solution(mesh):
    in_specs = (
        P(("dp", "ctx"), "tp"),
        P(("dp", "ctx"), "tp"),
        P(None, "tp"),
        P("tp"),
        P("tp"),
        P(("dp", "ctx"), "tp"),
        P("dp"),
        P(("dp", "ctx"), "tp"),
    )
    out_specs = (P(("dp", "ctx"), "tp"), P(("dp", "ctx"), "tp"), P(("dp", "ctx"), "tp"))
    return jax.shard_map(
        on_device, mesh=mesh, in_specs=in_specs, out_specs=out_specs, check_vma=False
    )
```

```python
import functools

import jax
import jax.numpy as jnp
from jax import lax
from jax.experimental import pallas as pl
from jax.experimental.pallas import tpu as pltpu
from jax.sharding import PartitionSpec as P

MESH = pl.DeviceIdType.MESH
LANES = 128
SUB = 8
HALO_PARTS = 8
F32 = jnp.float32
BF16 = jnp.bfloat16


def seg_of(lengths_ref, places, total):
    offset = jnp.int32(0)
    seg = jnp.zeros(places.shape, jnp.int32)
    for i in range(lengths_ref.shape[0]):
        seg = seg + (places >= offset).astype(jnp.int32)
        offset = offset + lengths_ref[i]
    return seg + (places >= total).astype(jnp.int32)


def one_minus_exp(x):
    series = jnp.ones_like(x)
    for n in range(9, 1, -1):
        series = 1.0 - x / n * series
    return jnp.where(x < 0.5, x * series, 1.0 - jnp.exp(-x))


def kernel(
    ctx_count, reach, halo_parts,
    lengths, k_ref, v_ref, filt_ref, rate_ref, residue_ref, gate_ref, gout_ref,
    mixed_ref, gv_ref, gf_ref,
    u_ext, g_ext, adj, state, scale, taps, taps_rev, mask_f, mask_b, diag_seg,
    scan_masks, acc, partial, gf_slots, carry_f, carry_b, carry_f_in, carry_b_in,
    u_send, u_recv, g_send, g_recv, cf_send, cf_recv, cb_send, cb_recv, gf_send, gf_recv,
):
    rows, width = k_ref.shape
    groups = filt_ref.shape[1]
    per_group = width // groups
    per_chunk = LANES // per_group
    chunks = width // LANES
    part_width = width // halo_parts
    total = rows * ctx_count
    me = lax.axis_index("ctx")
    first = me * rows

    barrier = pltpu.get_barrier_semaphore()

    @pl.loop(1, ctx_count)
    def _(step):
        pl.semaphore_signal(
            barrier, inc=1, device_id={"ctx": lax.rem(me + step, ctx_count)}, device_id_type=MESH
        )

    pl.semaphore_wait(barrier, ctx_count - 1)

    def u_copy(part):
        cols = pl.ds(part * part_width, part_width)
        return pltpu.make_async_remote_copy(
            src_ref=u_ext.at[pl.ds(rows, rows), cols],
            dst_ref=u_ext.at[pl.ds(0, rows), cols],
            send_sem=u_send.at[part],
            recv_sem=u_recv.at[part],
            device_id={"ctx": lax.rem(me + 1, ctx_count)},
            device_id_type=MESH,
        )

    def g_copy(part):
        cols = pl.ds(part * part_width, part_width)
        return pltpu.make_async_remote_copy(
            src_ref=g_ext.at[pl.ds(0, rows), cols],
            dst_ref=g_ext.at[pl.ds(rows, rows), cols],
            send_sem=g_send.at[part],
            recv_sem=g_recv.at[part],
            device_id={"ctx": lax.rem(me + ctx_count - 1, ctx_count)},
            device_id_type=MESH,
        )

    def carry_copy(k, forward):
        src, dst, send, recv = (
            (carry_f, carry_f_in, cf_send, cf_recv)
            if forward
            else (carry_b, carry_b_in, cb_send, cb_recv)
        )
        peer = me + 1 + k if forward else me + ctx_count - 1 - k
        return pltpu.make_async_remote_copy(
            src_ref=src,
            dst_ref=dst.at[k],
            send_sem=send.at[k],
            recv_sem=recv.at[k],
            device_id={"ctx": lax.rem(peer, ctx_count)},
            device_id_type=MESH,
        )

    for part in range(halo_parts):
        cols = slice(part * part_width, (part + 1) * part_width)
        u_ext[rows:, cols] = (k_ref[:, cols].astype(F32) * v_ref[:, cols].astype(F32)).astype(BF16)

        @pl.when(me < ctx_count - 1)
        def _():
            u_copy(part).start()

    @pl.when(me == 0)
    def _():
        u_ext[:rows, :] = jnp.zeros((rows, width), BF16)

    @pl.when(me == ctx_count - 1)
    def _():
        g_ext[rows:, :] = jnp.zeros((rows, width), BF16)

    rate_all = rate_ref[...]
    scale[...] = residue_ref[...] * jnp.sqrt(one_minus_exp(2.0 * rate_all))
    row = lax.broadcasted_iota(jnp.int32, (rows, LANES), 0)
    seg = seg_of(lengths, first + row, total)
    sub = lax.rem(row, SUB)
    tile = row - sub
    for i, k in enumerate((1, 2, 4)):
        same = (seg == pltpu.roll(seg, k, 0)) & (sub >= k)
        scan_masks[i] = same.astype(F32)
        same = (seg == pltpu.roll(seg, rows - k, 0)) & (sub + k < SUB)
        scan_masks[4 + i] = same.astype(F32)
    scan_masks[3] = (seg == seg_of(lengths, first + tile - 1, total)).astype(F32)
    scan_masks[7] = (seg == seg_of(lengths, first + tile + SUB, total)).astype(F32)
    lane_one = jnp.zeros((1, LANES), jnp.int32)
    seg_before = seg_of(lengths, first - 1 + lane_one, total)
    seg_after = seg_of(lengths, first + rows + lane_one, total)
    scan_masks[8] = (seg == seg_before).astype(F32)
    scan_masks[9] = (seg == seg_after).astype(F32)
    lane = lax.broadcasted_iota(jnp.int32, (rows, LANES), 1)
    lane_row = lax.broadcasted_iota(jnp.int32, (1, LANES), 1)
    seg_prev = seg_of(lengths, first - rows + lane_row, total)
    seg_here = seg_of(lengths, first + lane_row, total)
    seg_next = seg_of(lengths, first + rows + lane_row, total)
    f_left = ((seg == seg_prev) & (lane > row)).astype(F32)
    f_right = ((seg == seg_here) & (lane <= row)).astype(F32)
    mask_f[:, :LANES] = f_left.astype(BF16)
    mask_f[:, LANES:] = f_right.astype(BF16)
    diag_seg[...] = f_left + f_right
    mask_b[:, :LANES] = ((seg == seg_here) & (lane >= row)).astype(F32).astype(BF16)
    mask_b[:, LANES:] = ((seg == seg_next) & (lane < row)).astype(F32).astype(BF16)
    flip = (lax.rem(row + lane, LANES) == 0).astype(F32)
    eye = (row == lane).astype(F32)
    over_taps = (((0,), (0,)), ((), ()))
    filt = filt_ref[...]
    taps[...] = lax.dot_general(filt, eye.astype(BF16), over_taps, preferred_element_type=F32)
    taps_rev[...] = lax.dot_general(filt, flip.astype(BF16), over_taps, preferred_element_type=F32)

    sub8 = lax.broadcasted_iota(jnp.int32, (SUB, LANES), 0).astype(F32)
    tiles = rows // SUB

    def chunk_cols(q):
        return pl.ds(pl.multiple_of(q * LANES, LANES), LANES)

    def scan_tiles(values, rate, forward):
        base = 0 if forward else 4
        steps = [jnp.exp(-k * rate) for k in (1.0, 2.0, 4.0)]
        far = jnp.exp(-((sub8 + 1.0) if forward else (SUB - sub8)) * rate)
        out = [None] * tiles
        carry = None
        for n in range(tiles) if forward else reversed(range(tiles)):
            here = slice(n * SUB, (n + 1) * SUB)
            x = values[here, :]
            for i, k in enumerate((1, 2, 4)):
                shifted = pltpu.roll(x, k if forward else SUB - k, 0)
                x = x + steps[i] * scan_masks[base + i, here, :] * shifted
            if carry is not None:
                x = x + far * scan_masks[base + 3, here, :] * carry
            carry = x[SUB - 1 : SUB, :] if forward else x[0:1, :]
            out[n] = x
        return out, carry

    def carried(slots, cols, rate, forward):
        value = slots[0, :, cols]
        for k in range(1, reach):
            edge = first - 1 - rows * k if forward else first + rows + rows * k
            there = seg_of(lengths, edge + lane_one, total)
            same = (there == (seg_before if forward else seg_after)).astype(F32)
            value = value + slots[k, :, cols] * same * jnp.exp(-float(rows * k) * rate)
        return value

    @pl.loop(0, chunks, unroll=4)
    def _(q):
        cols = chunk_cols(q)
        rate = rate_ref[:, cols]
        long = (scale[:, cols] * gate_ref[:, cols].astype(F32) * gout_ref[:, cols].astype(F32))
        out, carry = scan_tiles(long.astype(BF16).astype(F32), rate, False)
        for n in range(tiles):
            adj[n * SUB : (n + 1) * SUB, cols] = out[n]
        carry_b[:, cols] = carry

    for k in range(reach):

        @pl.when(me >= 1 + k)
        def _():
            carry_copy(k, False).start()

        @pl.when(me + 1 + k >= ctx_count)
        def _():
            carry_b_in[k] = jnp.zeros((1, width), F32)

    for k in range(reach):

        @pl.when(me + 1 + k < ctx_count)
        def _():
            carry_copy(k, False).wait_recv()

    for part in range(halo_parts):
        per_part = chunks // halo_parts

        @pl.loop(part * per_part, (part + 1) * per_part, unroll=4)
        def _(q):
            cols = chunk_cols(q)
            rate = rate_ref[:, cols]
            value = carried(carry_b_in, cols, rate, False)
            far = jnp.exp(-(SUB - sub8) * rate)
            eighth = jnp.exp(-float(SUB) * rate)
            for n in reversed(range(tiles)):
                here = slice(n * SUB, (n + 1) * SUB)
                x = adj[here, cols] + far * scan_masks[9, here, :] * value
                adj[here, cols] = x
                value = value * eighth
            g_ext[:rows, cols] = adj[:, cols].astype(BF16)

        @pl.when(me > 0)
        def _():
            g_copy(part).start()

    def bands(tap_rows, mask):
        blocks = []
        for g in range(per_chunk):
            skew = pltpu.roll(
                jnp.broadcast_to(tap_rows[g : g + 1, :], (SUB, LANES)), 0, 1,
                stride=1, stride_axis=0,
            )
            circ = jnp.concatenate(
                [skew] + [pltpu.roll(skew, n * SUB, 1) for n in range(1, tiles)], axis=0
            ).astype(BF16)
            blocks.append(
                jnp.concatenate([circ * mask[:, :LANES], circ * mask[:, LANES:]], axis=1)
            )
        return jnp.concatenate(blocks, axis=0)

    group_of_lane = lane // per_group

    for part in range(halo_parts):

        @pl.when(me > 0)
        def _():
            u_copy(part).wait_recv()

        @pl.loop(part * per_part, (part + 1) * per_part, unroll=2)
        def _(q):
            cols = chunk_cols(q)
            window = u_ext[:, cols]
            grads = g_ext[:rows, cols]
            group_rows = pl.ds(pl.multiple_of(q * per_chunk, per_chunk), per_chunk)
            all_y = jnp.dot(
                bands(taps_rev[group_rows, :], mask_f), window,
                preferred_element_type=F32,
            )
            y = all_y[:rows, :]
            for g in range(1, per_chunk):
                y = jnp.where(group_of_lane == g, all_y[g * rows : (g + 1) * rows, :], y)
            own = jnp.concatenate(
                [jnp.where(group_of_lane == g, grads, jnp.zeros_like(grads)) for g in range(per_chunk)],
                axis=0,
            )
            all_prod = lax.dot_general(
                own, window, (((1,), (1,)), ((), ())), preferred_element_type=F32
            )
            for g in range(per_chunk):
                prod = all_prod[g * rows : (g + 1) * rows, :]
                prod = jnp.where(lane <= row, prod[:, LANES:], prod[:, :LANES]) * diag_seg[...]
                folded = prod[:SUB, :]
                for n in range(1, tiles):
                    folded = folded + pltpu.roll(
                        prod[n * SUB : (n + 1) * SUB, :], LANES - n * SUB, 1
                    )
                acc[pl.ds(pl.multiple_of((q * per_chunk + g) * SUB, SUB), SUB), :] = folded
            out, carry = scan_tiles(y.astype(BF16).astype(F32), rate_ref[:, cols], True)
            for n in range(tiles):
                state[n * SUB : (n + 1) * SUB, cols] = out[n]
            carry_f[:, cols] = carry

    for k in range(reach):

        @pl.when(me + 1 + k < ctx_count)
        def _():
            carry_copy(k, True).start()

        @pl.when(me < 1 + k)
        def _():
            carry_f_in[k] = jnp.zeros((1, width), F32)

    skewed = acc[pl.ds(0, groups, stride=SUB), :]
    for r in range(1, SUB):
        skewed = skewed + pltpu.roll(acc[pl.ds(r, groups, stride=SUB), :], LANES - r, 1)
    by_tap = lax.dot_general(
        flip, skewed, (((1,), (1,)), ((), ())),
        precision=lax.Precision.HIGHEST, preferred_element_type=F32,
    )
    piece = rows // ctx_count
    for i in range(ctx_count):
        partial[i] = by_tap[i * piece : (i + 1) * piece, :]

    def gf_copy(step):
        peer = lax.rem(me + step, ctx_count)
        return pltpu.make_async_remote_copy(
            src_ref=partial.at[peer],
            dst_ref=gf_slots.at[step - 1],
            send_sem=gf_send.at[step - 1],
            recv_sem=gf_recv.at[step - 1],
            device_id={"ctx": peer},
            device_id_type=MESH,
        )

    @pl.loop(1, ctx_count)
    def _(step):
        gf_copy(step).start()

    def finish_forward():
        for k in range(reach):

            @pl.when(me >= 1 + k)
            def _():
                carry_copy(k, True).wait_recv()

        @pl.loop(0, chunks, unroll=4)
        def _(q):
            cols = chunk_cols(q)
            rate = rate_ref[:, cols]
            value = carried(carry_f_in, cols, rate, True)
            far = jnp.exp(-(sub8 + 1.0) * rate)
            eighth = jnp.exp(-float(SUB) * rate)
            for n in range(tiles):
                here = slice(n * SUB, (n + 1) * SUB)
                x = state[here, cols] + far * scan_masks[8, here, :] * value
                state[here, cols] = x
                value = value * eighth
            z_long = (scale[:, cols] * state[:, cols]).astype(BF16)
            mixed_ref[:, cols] = (gate_ref[:, cols].astype(F32) * z_long.astype(F32)).astype(BF16)

    for part in range(halo_parts):

        @pl.when(me < ctx_count - 1)
        def _():
            g_copy(part).wait_recv()

        @pl.loop(part * per_part, (part + 1) * per_part, unroll=2)
        def _(q):
            cols = chunk_cols(q)
            window = g_ext[:, cols]
            group_rows = pl.ds(pl.multiple_of(q * per_chunk, per_chunk), per_chunk)
            all_u = jnp.dot(
                bands(taps[group_rows, :], mask_b), window,
                preferred_element_type=F32,
            )
            grad_u = all_u[:rows, :]
            for g in range(1, per_chunk):
                grad_u = jnp.where(group_of_lane == g, all_u[g * rows : (g + 1) * rows, :], grad_u)
            gv_ref[:, cols] = (k_ref[:, cols].astype(F32) * grad_u).astype(BF16)

        if part == (halo_parts - 1) // 2:
            finish_forward()

    own = partial[me]

    def add_slot(step, value):
        gf_copy(step).wait_recv()
        return value + gf_slots[step - 1]

    gf_ref[...] = lax.fori_loop(1, ctx_count, add_slot, own)

    @pl.loop(1, ctx_count)
    def _(step):
        gf_copy(step).wait_send()

    for k in range(reach):

        @pl.when(me >= 1 + k)
        def _():
            carry_copy(k, False).wait_send()

        @pl.when(me + 1 + k < ctx_count)
        def _():
            carry_copy(k, True).wait_send()

    for part in range(halo_parts):

        @pl.when(me < ctx_count - 1)
        def _():
            u_copy(part).wait_send()

        @pl.when(me > 0)
        def _():
            g_copy(part).wait_send()


def crossing(lengths_ref, edge):
    offset = jnp.int32(0)
    before = jnp.int32(0)
    after = jnp.int32(0)
    for i in range(lengths_ref.shape[0]):
        end = offset + lengths_ref[i]
        inside = (offset < edge) & (end > edge)
        before = jnp.where(inside, edge - offset, before)
        after = jnp.where(inside, end - edge, after)
        offset = end
    return before, after


def short_kernel(
    ctx_count, halo_parts,
    lengths, k_hbm, v_hbm, filt_ref, rate_ref, residue_ref, gate_hbm, gout_hbm,
    mixed_ref, gv_ref, gf_ref,
    k_ref, v_ref, gate_ref, gout_ref, load,
    u_own, g_own, u_out, g_out, u_in, g_in, relay, adj, y_own, gu_own, circ_f, circ_b,
    scale, taps, taps_rev, mask_f, mask_b, diag_seg, scan_masks, even_odd, pair_lanes,
    right_rows, left_rows, even_odd_t, left_t, right_t, quad_u, quad_g, u_t, g_t, acc, acc_t, partial, gf_slots,
    carry_f, carry_b, carry_f_in, carry_b_in,
    u_send, u_recv, g_send, g_recv, cf_send, cf_recv, cb_send, cb_recv,
    relay_send, relay_recv, gf_send, gf_recv,
):
    rows, width = k_ref.shape
    groups = filt_ref.shape[1]
    half = rows // 2
    per_group = width // groups
    per_chunk = LANES // per_group
    pairs = per_chunk // 2
    chunks = width // LANES
    per_part = chunks // halo_parts
    part_width = width // halo_parts
    total = rows * ctx_count
    tiles = rows // SUB
    me = lax.axis_index("ctx")
    first = me * rows
    has_next = me < ctx_count - 1
    has_prev = me > 0

    loads = [
        pltpu.make_async_copy(src, dst, load.at[n])
        for n, (src, dst) in enumerate(
            ((gate_hbm, gate_ref), (gout_hbm, gout_ref), (k_hbm, k_ref), (v_hbm, v_ref))
        )
    ]
    for one in loads:
        one.start()

    barrier = pltpu.get_barrier_semaphore()

    @pl.loop(1, ctx_count)
    def _(step):
        pl.semaphore_signal(
            barrier, inc=1, device_id={"ctx": lax.rem(me + step, ctx_count)}, device_id_type=MESH
        )

    def halo_copy(part, forward):
        src, dst, send, recv = (
            (u_out, u_in, u_send, u_recv) if forward else (g_out, g_in, g_send, g_recv)
        )
        cols = pl.ds(pl.multiple_of(part * part_width, LANES), part_width)
        peer = me + 1 if forward else me + ctx_count - 1
        return pltpu.make_async_remote_copy(
            src_ref=src.at[:, cols],
            dst_ref=dst.at[:, cols],
            send_sem=send.at[part],
            recv_sem=recv.at[part],
            device_id={"ctx": lax.rem(peer, ctx_count)},
            device_id_type=MESH,
        )

    def carry_b_copy():
        return pltpu.make_async_remote_copy(
            src_ref=carry_b,
            dst_ref=carry_b_in,
            send_sem=cb_send.at[0],
            recv_sem=cb_recv.at[0],
            device_id={"ctx": lax.rem(me + ctx_count - 1, ctx_count)},
            device_id_type=MESH,
        )

    def carry_f_copy():
        return pltpu.make_async_remote_copy(
            src_ref=carry_f,
            dst_ref=carry_f_in,
            send_sem=cf_send.at[0],
            recv_sem=cf_recv.at[0],
            device_id={"ctx": lax.rem(me + 1, ctx_count)},
            device_id_type=MESH,
        )

    relays = ctx_count == 4

    def relay_copy(part, forward):
        cols = pl.ds(pl.multiple_of(part * part_width, LANES), part_width)
        src, send = (u_out, u_send) if forward else (g_out, g_send)
        return pltpu.make_async_remote_copy(
            src_ref=src.at[:, cols],
            dst_ref=relay.at[:, cols],
            send_sem=send.at[part],
            recv_sem=relay_recv.at[part],
            device_id={"ctx": 3 if forward else 0},
            device_id_type=MESH,
        )

    def onward_copy(part, forward):
        cols = pl.ds(pl.multiple_of(part * part_width, LANES), part_width)
        dst, recv = (u_in, u_recv) if forward else (g_in, g_recv)
        return pltpu.make_async_remote_copy(
            src_ref=relay.at[:, cols],
            dst_ref=dst.at[:, cols],
            send_sem=relay_send.at[part],
            recv_sem=recv.at[part],
            device_id={"ctx": 2 if forward else 1},
            device_id_type=MESH,
        )

    @pl.when(jnp.logical_not(has_prev))
    def _():
        u_in[...] = jnp.zeros(u_in.shape, BF16)
        carry_f_in[...] = jnp.zeros(carry_f_in.shape, F32)

    @pl.when(jnp.logical_not(has_next))
    def _():
        g_in[...] = jnp.zeros(g_in.shape, BF16)
        carry_b_in[...] = jnp.zeros(carry_b_in.shape, F32)

    left_a, left_b = crossing(lengths, first)
    right_a, right_b = crossing(lengths, first + rows)

    rate_all = rate_ref[...]
    scale[...] = residue_ref[...] * jnp.sqrt(one_minus_exp(2.0 * rate_all))
    row = lax.broadcasted_iota(jnp.int32, (rows, LANES), 0)
    lane = lax.broadcasted_iota(jnp.int32, (rows, LANES), 1)
    lane_row = lax.broadcasted_iota(jnp.int32, (1, LANES), 1)
    row_half = lax.broadcasted_iota(jnp.int32, (half, LANES), 0)
    lane_half = lax.broadcasted_iota(jnp.int32, (half, LANES), 1)
    seg = seg_of(lengths, first + row, total)
    sub = lax.rem(row, SUB)
    tile = row - sub
    for i, k in enumerate((1, 2, 4)):
        same = (seg == pltpu.roll(seg, rows - k, 0)) & (sub + k < SUB)
        scan_masks[4 + i] = same.astype(F32)
    scan_masks[7] = (seg == seg_of(lengths, first + tile + SUB, total)).astype(F32)
    lane_one = jnp.zeros((1, LANES), jnp.int32)
    scan_masks[10] = (seg == seg_of(lengths, first + lane_one, total)).astype(F32)
    group_of_lane = lane // per_group
    pair_of_lane = group_of_lane // 2
    send_u = right_a <= half
    send_gpart = left_a <= half
    for e in range(2):
        lanes = lax.rem(group_of_lane, 2) == e
        right_rows[e * rows : (e + 1) * rows, :] = (
            (lanes & (row >= rows - right_a)).astype(F32).astype(BF16)
        )
        left_rows[e * rows : (e + 1) * rows, :] = (
            (lanes & (row < left_b)).astype(F32).astype(BF16)
        )
    flip = (lax.rem(row + lane, LANES) == 0).astype(F32)
    eye = (row == lane).astype(F32)
    over_taps = (((0,), (0,)), ((), ()))
    filt = filt_ref[...]
    taps[...] = lax.dot_general(filt, eye.astype(BF16), over_taps, preferred_element_type=F32)
    taps_rev[...] = lax.dot_general(filt, flip.astype(BF16), over_taps, preferred_element_type=F32)
    sub8 = lax.broadcasted_iota(jnp.int32, (SUB, LANES), 0).astype(F32)

    def chunk_cols(q):
        return pl.ds(pl.multiple_of(q * LANES, LANES), LANES)

    def group_rows(q, g):
        return pl.ds(pl.multiple_of((q * per_chunk + g) * rows, rows), rows)

    def scan_tiles(values, rate, forward, carry=None):
        base = 0 if forward else 4
        steps = [jnp.exp(-k * rate) for k in (1.0, 2.0, 4.0)]
        far = jnp.exp(-((sub8 + 1.0) if forward else (SUB - sub8)) * rate)
        out = [None] * tiles
        for n in range(tiles) if forward else reversed(range(tiles)):
            here = slice(n * SUB, (n + 1) * SUB)
            x = values[here, :]
            for i, k in enumerate((1, 2, 4)):
                shifted = pltpu.roll(x, k if forward else SUB - k, 0)
                x = x + steps[i] * scan_masks[base + i, here, :] * shifted
            if carry is not None:
                x = x + far * scan_masks[base + 3, here, :] * carry
            carry = x[SUB - 1 : SUB, :] if forward else x[0:1, :]
            out[n] = x
        return out, carry

    def circulant(tap_rows, g):
        skew = pltpu.roll(
            jnp.broadcast_to(tap_rows[g : g + 1, :], (2 * SUB, LANES)), 0, 1,
            stride=1, stride_axis=0,
        ).astype(BF16)
        return jnp.concatenate(
            [skew] + [pltpu.roll(skew, 2 * n * SUB, 1) for n in range(1, tiles // 2)], axis=0
        )

    def pick(outs, n_rows, index):
        value = outs[:n_rows, :]
        for p in range(1, outs.shape[0] // n_rows):
            value = jnp.where(index == p, outs[p * n_rows : (p + 1) * n_rows, :], value)
        return value

    def beside(x):
        return jnp.concatenate([x, x], axis=1)

    def twice(x):
        return jnp.concatenate([x, x], axis=0)

    def fold(prod):
        folded = prod[:SUB, :]
        for n in range(1, prod.shape[0] // SUB):
            folded = folded + pltpu.roll(prod[n * SUB : (n + 1) * SUB, :], LANES - n * SUB, 1)
        return folded

    pair_half = lane_half // (2 * per_group)
    across = (((1,), (1,)), ((), ()))

    for one in loads:
        one.wait()

    @pl.loop(0, halo_parts)
    def _(part):
        for c in range(per_part):
            cols = chunk_cols(part * per_part + c)
            rate = rate_ref[:, cols]
            long = scale[:, cols] * gate_ref[:, cols].astype(F32) * gout_ref[:, cols].astype(F32)
            long = long.astype(BF16).astype(F32) * scan_masks[10]
            eighth = jnp.exp(-float(SUB) * rate)
            run = long[rows - SUB :, :]
            for n in reversed(range(tiles - 1)):
                run = run * eighth + long[n * SUB : (n + 1) * SUB, :]
            carry_b[:, cols] = jnp.sum(run * jnp.exp(-sub8 * rate), axis=0, keepdims=True)

    pl.semaphore_wait(barrier, ctx_count - 1)

    @pl.when(has_prev)
    def _():
        carry_b_copy().start()

    def join(xs):
        return jnp.concatenate(
            [jnp.concatenate(xs[2 * p : 2 * p + 2], axis=1) for p in range(pairs)], axis=0
        )

    def pair_bands(circ, q, mask):
        return jnp.concatenate(
            [
                jnp.concatenate(
                    [circ[group_rows(q, 2 * p + e), :] * mask for e in range(2)], axis=1
                )
                for p in range(pairs)
            ],
            axis=0,
        )

    def own_y(q):
        cols = chunk_cols(q)
        rate = rate_ref[:, cols]
        y = jnp.dot(
            pair_bands(circ_f, q, mask_f[...]), twice(u_own[:, cols]) * even_odd[...],
            preferred_element_type=F32,
        )
        y = pick(y, rows, pair_of_lane)
        y_own[:, cols] = y
        last = y.astype(BF16).astype(F32) * scan_masks[8]
        eighth = jnp.exp(-float(SUB) * rate)
        run = last[:SUB, :]
        for n in range(1, tiles):
            run = run * eighth + last[n * SUB : (n + 1) * SUB, :]
        carry_f[:, cols] = jnp.sum(
            run * jnp.exp(-(SUB - 1.0 - sub8) * rate), axis=0, keepdims=True
        )

    @pl.loop(0, halo_parts)
    def _(part):
        for c in range(per_part):
            q = part * per_part + c
            cols = chunk_cols(q)
            u = (k_ref[:, cols].astype(F32) * v_ref[:, cols].astype(F32)).astype(BF16)
            u_own[:, cols] = u
            long = scale[:, cols] * gate_ref[:, cols].astype(F32) * gout_ref[:, cols].astype(F32)
            out, _ = scan_tiles(long.astype(BF16).astype(F32), rate_ref[:, cols], False)
            for n in range(tiles):
                adj[n * SUB : (n + 1) * SUB, cols] = out[n]
            g = jnp.concatenate(out, axis=0).astype(BF16)
            tap_rows = pl.ds(pl.multiple_of(q * per_chunk, per_chunk), per_chunk)
            f_rows, b_rows = taps_rev[tap_rows, :], taps[tap_rows, :]
            top, bottom = [], []
            for i in range(per_chunk):
                f, b = circulant(f_rows, i), circulant(b_rows, i)
                circ_f[group_rows(q, i), :] = f
                circ_b[group_rows(q, i), :] = b
                top.append(f[:half, :])
                bottom.append(b[half:, :])
            y_part = jnp.dot(join(top), twice(u) * right_rows[...], preferred_element_type=F32)
            y_part = pick(y_part, half, pair_half)
            g_part = jnp.dot(join(bottom), twice(g) * left_rows[...], preferred_element_type=F32)
            g_part = pick(g_part, half, pair_half)
            y_part = jnp.where(row_half < right_b, y_part, 0.0)
            g_part = jnp.where(row_half >= half - left_a, g_part, 0.0)
            u_tail = jnp.where(row_half >= half - right_a, u[half:, :].astype(F32), 0.0)
            g_head = jnp.where(row_half < left_b, g[:half, :].astype(F32), 0.0)
            u_out[:, cols] = jnp.where(send_u, u_tail, y_part).astype(BF16)
            g_out[:, cols] = jnp.where(send_gpart, g_part, g_head).astype(BF16)

        by_relay = lax.rem(part, 2) == 1 if relays else False

        @pl.when(has_next)
        def _():
            if relays:
                pl.when((me == 1) & by_relay)(lambda: relay_copy(part, True).start())
                pl.when((me != 1) | jnp.logical_not(by_relay))(
                    lambda: halo_copy(part, True).start()
                )
            else:
                halo_copy(part, True).start()

        @pl.when(has_prev)
        def _():
            if relays:
                pl.when((me == 2) & by_relay)(lambda: relay_copy(part, False).start())
                pl.when((me != 2) | jnp.logical_not(by_relay))(
                    lambda: halo_copy(part, False).start()
                )
            else:
                halo_copy(part, False).start()

    def own_terms(q):
        cols = chunk_cols(q)
        rate = rate_ref[:, cols]
        value = carry_b_in[:, cols]
        far = jnp.exp(-(SUB - sub8) * rate)
        eighth = jnp.exp(-float(SUB) * rate)
        out = [None] * tiles
        for n in reversed(range(tiles)):
            here = slice(n * SUB, (n + 1) * SUB)
            out[n] = adj[here, cols] + far * scan_masks[9, here, :] * value
            value = value * eighth
        g = jnp.concatenate(out, axis=0).astype(BF16)
        g_own[:, cols] = g
        gu = jnp.dot(
            pair_bands(circ_b, q, mask_b[...]), twice(g) * even_odd[...],
            preferred_element_type=F32,
        )
        gu_own[:, cols] = pick(gu, rows, pair_of_lane)
        by_pair = jnp.concatenate([g * pair_lanes[p] for p in range(pairs)], axis=0)
        ut, gt = u_own[:, cols].T, g.T
        t_rows = pl.ds(pl.multiple_of(q * LANES, LANES), LANES)
        u_t[t_rows, :] = ut
        g_t[t_rows, :] = gt
        prods = jnp.dot(by_pair, beside(ut) * even_odd_t[...], preferred_element_type=F32)
        for p in range(pairs):
            for e in range(2):
                prod = prods[p * rows : (p + 1) * rows, e * LANES : (e + 1) * LANES]
                at = pl.multiple_of((q * per_chunk + 2 * p + e) * SUB, SUB)
                acc[pl.ds(at, SUB), :] = fold(prod * diag_seg[...])

    seg = seg_of(lengths, first + row, total)
    for i, k in enumerate((1, 2, 4)):
        same = (seg == pltpu.roll(seg, k, 0)) & (sub >= k)
        scan_masks[i] = same.astype(F32)
    scan_masks[3] = (seg == seg_of(lengths, first + tile - 1, total)).astype(F32)
    lane_one = jnp.zeros((1, LANES), jnp.int32)
    scan_masks[8] = (seg == seg_of(lengths, first + rows - 1 + lane_one, total)).astype(F32)
    scan_masks[9] = (seg == seg_of(lengths, first + rows + lane_one, total)).astype(F32)
    seg_here = seg_of(lengths, first + lane_row, total)
    own = ((seg == seg_here) & (lane <= row)).astype(F32)
    mask_f[...] = own.astype(BF16)
    diag_seg[...] = own
    mask_b[...] = ((seg == seg_here) & (lane >= row)).astype(F32).astype(BF16)
    for e in range(2):
        even_odd[e * rows : (e + 1) * rows, :] = (
            (lax.rem(group_of_lane, 2) == e).astype(F32).astype(BF16)
        )
    group_of_row = row // per_group
    for e in range(2):
        rows_e = lax.rem(group_of_row, 2) == e
        at = slice(e * LANES, (e + 1) * LANES)
        even_odd_t[:, at] = rows_e.astype(F32).astype(BF16)
        left_t[:, at] = jnp.where(
            send_gpart, (rows_e & (lane < left_b)).astype(F32), 0.0
        ).astype(BF16)
        right_t[:, at] = jnp.where(
            send_u, 0.0, (rows_e & (lane >= rows - right_a)).astype(F32)
        ).astype(BF16)
    for p in range(pairs):
        pair_lanes[p] = (pair_of_lane == p).astype(F32).astype(BF16)
    group_half = lane_half // per_group
    for e in range(4):
        lanes = lax.rem(group_half, 4) == e
        quad_u[e * half : (e + 1) * half, :] = (
            jnp.where(send_gpart, lanes.astype(F32), 0.0).astype(BF16)
        )
        quad_g[e * half : (e + 1) * half, :] = (
            jnp.where(send_u, 0.0, lanes.astype(F32)).astype(BF16)
        )

    @pl.when(has_next)
    def _():
        carry_b_copy().wait_recv()

    @pl.loop(0, chunks // 4)
    def _(step):
        if relays:
            for forward, by in ((True, 3), (False, 0)):

                @pl.when(me == by)
                def _():
                    relay_copy(2 * step + 1, forward).wait_recv()
                    onward_copy(2 * step + 1, forward).start()

        for c in range(4):
            own_y(step * 4 + c)
            own_terms(step * 4 + c)

    @pl.when(has_next)
    def _():
        carry_f_copy().start()

    low_lanes = lane < half

    def quad_bands(circ, q, forward):
        quads = []
        for g in range(0, per_chunk, 4):
            halves = []
            for e in (0, 2):
                one = circ[group_rows(q, g + e), :]
                two = circ[group_rows(q, g + e + 1), :]
                if forward:
                    one = jnp.concatenate([one[half:, :], one[:half, :]], axis=0)
                else:
                    two = jnp.concatenate([two[half:, :], two[:half, :]], axis=0)
                halves.append(jnp.where(low_lanes, one, two))
            quads.append(jnp.concatenate(halves, axis=1))
        return jnp.concatenate(quads, axis=0)

    def four(x):
        return jnp.concatenate([x, x, x, x], axis=0)

    quad_of_lane = lane // (4 * per_group)

    def cross_terms(q):
        cols = chunk_cols(q)
        u_msg, g_msg = u_in[:, cols], g_in[:, cols]
        t_rows = pl.ds(pl.multiple_of(q * LANES, LANES), LANES)
        lhs = jnp.concatenate([u_msg * pair_lanes[p, :half, :] for p in range(pairs)], axis=0)
        prods = jnp.dot(lhs, beside(g_t[t_rows, :]) * left_t[...], preferred_element_type=F32)
        lhs = jnp.concatenate([g_msg * pair_lanes[p, :half, :] for p in range(pairs)], axis=0)
        prods2 = jnp.dot(lhs, beside(u_t[t_rows, :]) * right_t[...], preferred_element_type=F32)
        for p in range(pairs):
            for e in range(2):
                at = pl.ds(pl.multiple_of((q * per_chunk + 2 * p + e) * SUB, SUB), SUB)
                cut = (slice(p * half, (p + 1) * half), slice(e * LANES, (e + 1) * LANES))
                acc_t[at, :] = fold(prods[cut])
                acc[at, :] = acc[at, :] + fold(prods2[cut])

    def finish(q):
        cols = chunk_cols(q)
        u_msg, g_msg = u_in[:, cols], g_in[:, cols]
        rate = rate_ref[:, cols]
        y = jnp.dot(
            quad_bands(circ_f, q, True), four(u_msg) * quad_u[...], preferred_element_type=F32
        )
        y = pick(y, rows, quad_of_lane)
        y_part = jnp.where(send_gpart, 0.0, u_msg.astype(F32))
        y = y + jnp.concatenate([y_part, jnp.zeros_like(y_part)], axis=0)
        y = y_own[:, cols] + jnp.where(row < left_b, y, 0.0)
        out, _ = scan_tiles(
            y.astype(BF16).astype(F32), rate, True, carry_f_in[:, cols]
        )
        z_long = (scale[:, cols] * jnp.concatenate(out, axis=0)).astype(BF16)
        mixed_ref[:, cols] = (gate_ref[:, cols].astype(F32) * z_long.astype(F32)).astype(BF16)
        gu = jnp.dot(
            quad_bands(circ_b, q, False), four(g_msg) * quad_g[...], preferred_element_type=F32
        )
        gu = pick(gu, rows, quad_of_lane)
        g_part = jnp.where(send_u, g_msg.astype(F32), 0.0)
        gu = gu + jnp.concatenate([jnp.zeros_like(g_part), g_part], axis=0)
        gu = gu_own[:, cols] + jnp.where(row >= rows - right_a, gu, 0.0)
        gv_ref[:, cols] = (k_ref[:, cols].astype(F32) * gu).astype(BF16)

    @pl.loop(0, chunks // 4)
    def _(step):
        @pl.when(has_prev)
        def _():
            for n in range(2):
                halo_copy(step * 2 + n, True).wait_recv()

        @pl.when(has_next)
        def _():
            for n in range(2):
                halo_copy(step * 2 + n, False).wait_recv()

        for c in range(4):
            cross_terms(step * 4 + c)

    skewed = acc[pl.ds(0, groups, stride=SUB), :]
    skewed_t = acc_t[pl.ds(0, groups, stride=SUB), :]
    for r in range(1, SUB):
        turn = LANES - r
        skewed = skewed + pltpu.roll(acc[pl.ds(r, groups, stride=SUB), :], turn, 1)
        skewed_t = skewed_t + pltpu.roll(acc_t[pl.ds(r, groups, stride=SUB), :], turn, 1)
    skewed_t = pltpu.roll(skewed_t, half, 1)
    by_tap = lax.dot_general(
        flip, skewed, across, precision=lax.Precision.HIGHEST, preferred_element_type=F32
    ) + lax.dot_general(
        eye, skewed_t, across, precision=lax.Precision.HIGHEST, preferred_element_type=F32
    )
    piece = rows // ctx_count
    for i in range(ctx_count):
        partial[i] = by_tap[i * piece : (i + 1) * piece, :]

    def gf_copy(step):
        peer = lax.rem(me + step, ctx_count)
        return pltpu.make_async_remote_copy(
            src_ref=partial.at[peer],
            dst_ref=gf_slots.at[step - 1],
            send_sem=gf_send.at[step - 1],
            recv_sem=gf_recv.at[step - 1],
            device_id={"ctx": peer},
            device_id_type=MESH,
        )

    @pl.loop(1, ctx_count)
    def _(step):
        gf_copy(step).start()

    @pl.when(has_prev)
    def _():
        carry_f_copy().wait_recv()

    @pl.loop(0, chunks // 4)
    def _(step):
        for c in range(4):
            finish(step * 4 + c)

    def add_slot(step, value):
        gf_copy(step).wait_recv()
        return value + gf_slots[step - 1]

    gf_ref[...] = lax.fori_loop(1, ctx_count, add_slot, partial[me])

    @pl.loop(1, ctx_count)
    def _(step):
        gf_copy(step).wait_send()

    if relays:
        for forward, by in ((True, 3), (False, 0)):

            @pl.when(me == by)
            def _():
                for part in range(1, halo_parts, 2):
                    onward_copy(part, forward).wait_send()

    @pl.when(has_prev)
    def _():
        carry_b_copy().wait_send()
        for part in range(halo_parts):
            halo_copy(part, False).wait_send()

    @pl.when(has_next)
    def _():
        carry_f_copy().wait_send()
        for part in range(halo_parts):
            halo_copy(part, True).wait_send()


def write_out(*refs):
    copies = [
        pltpu.make_async_copy(refs[n], refs[3 + n], refs[6].at[n]) for n in range(3)
    ]
    for one in copies:
        one.start()
    for one in copies:
        one.wait()


def short_call(args, ctx_count):
    rows, width = args[1].shape
    taps, groups = args[3].shape
    halo_parts = HALO_PARTS
    half = rows // 2
    vmem = pl.BlockSpec(memory_space=pltpu.VMEM)
    hbm = pl.BlockSpec(memory_space=pltpu.HBM)
    dma = pltpu.SemaphoreType.DMA
    piece = taps // ctx_count
    pairs = LANES // (width // groups) // 2
    wide = lambda r, t: pltpu.VMEM((r, width), t)
    square = lambda n, t: pltpu.VMEM((n, LANES), t)
    keep = pltpu.with_memory_space_constraint
    args = [keep(x, pltpu.HBM) for x in args]
    results = pl.pallas_call(
        functools.partial(short_kernel, ctx_count, halo_parts),
        out_shape=(
            pltpu.VMEM((rows, width), BF16),
            pltpu.VMEM((rows, width), BF16),
            pltpu.VMEM((piece, groups), F32),
        ),
        in_specs=[pl.BlockSpec(memory_space=pltpu.SMEM)] + [hbm] * 2 + [vmem] * 3 + [hbm] * 2,
        out_specs=(vmem, vmem, vmem),
        scratch_shapes=[
            wide(rows, BF16), wide(rows, BF16), wide(rows, BF16), wide(rows, BF16), dma((4,)),
            wide(rows, BF16), wide(rows, BF16),
            wide(half, BF16), wide(half, BF16), wide(half, BF16), wide(half, BF16),
            wide(half, BF16),
            wide(rows, F32), wide(rows, F32), wide(rows, F32),
            square(groups * rows, BF16), square(groups * rows, BF16),
            wide(1, F32), pltpu.VMEM((groups, taps), F32), pltpu.VMEM((groups, taps), F32),
            square(rows, BF16), square(rows, BF16), square(rows, F32),
            pltpu.VMEM((11, rows, LANES), F32),
            square(2 * rows, BF16), pltpu.VMEM((pairs, rows, LANES), BF16),
            square(2 * rows, BF16), square(2 * rows, BF16),
            pltpu.VMEM((rows, 2 * LANES), BF16), pltpu.VMEM((rows, 2 * LANES), BF16),
            pltpu.VMEM((rows, 2 * LANES), BF16),
            square(2 * rows, BF16), square(2 * rows, BF16),
            square(width, BF16), square(width, BF16),
            square(SUB * groups, F32), square(SUB * groups, F32),
            pltpu.VMEM((ctx_count, piece, groups), F32),
            pltpu.VMEM((ctx_count - 1, piece, groups), F32),
            wide(1, F32), wide(1, F32), wide(1, F32), wide(1, F32),
            dma((halo_parts,)), dma((halo_parts,)), dma((halo_parts,)), dma((halo_parts,)),
            dma((1,)), dma((1,)), dma((1,)), dma((1,)),
            dma((halo_parts,)), dma((halo_parts,)),
            dma((ctx_count - 1,)), dma((ctx_count - 1,)),
        ],
        compiler_params=pltpu.CompilerParams(
            collective_id=1, has_side_effects=True, vmem_limit_bytes=48 * 1024 * 1024
        ),
        name="hyena_mixers_short",
    )(*args)
    return pl.pallas_call(
        write_out,
        out_shape=tuple(jax.ShapeDtypeStruct(x.shape, x.dtype) for x in results),
        in_specs=[vmem] * 3,
        out_specs=(hbm,) * 3,
        scratch_shapes=[dma((3,))],
        name="write_out",
    )(*[keep(x, pltpu.VMEM) for x in results])


def on_device(k_short, v_short, mr_filter, li_rate, li_residue, gate_out, contig_lengths, grad_out):
    rows, width = k_short.shape
    taps, groups = mr_filter.shape
    ctx_count = lax.axis_size("ctx")
    total = rows * ctx_count
    reach = min(ctx_count - 1, -(-(total // 4) // rows))
    args = (
        contig_lengths, k_short, v_short, mr_filter, li_rate[None], li_residue[None],
        gate_out, grad_out,
    )
    if total // 4 <= rows == taps == LANES:
        return short_call(args, ctx_count)
    halo_parts = 4
    vmem = pl.BlockSpec(memory_space=pltpu.VMEM)
    dma = pltpu.SemaphoreType.DMA
    piece = taps // ctx_count
    return pl.pallas_call(
        functools.partial(kernel, ctx_count, reach, halo_parts),
        out_shape=(
            jax.ShapeDtypeStruct((rows, width), BF16),
            jax.ShapeDtypeStruct((rows, width), BF16),
            jax.ShapeDtypeStruct((piece, groups), F32),
        ),
        in_specs=[pl.BlockSpec(memory_space=pltpu.SMEM)] + [vmem] * 7,
        out_specs=(vmem, vmem, vmem),
        scratch_shapes=[
            pltpu.VMEM((2 * rows, width), BF16),
            pltpu.VMEM((2 * rows, width), BF16),
            pltpu.VMEM((rows, width), F32),
            pltpu.VMEM((rows, width), F32),
            pltpu.VMEM((1, width), F32),
            pltpu.VMEM((groups, taps), F32),
            pltpu.VMEM((groups, taps), F32),
            pltpu.VMEM((rows, 2 * LANES), BF16),
            pltpu.VMEM((rows, 2 * LANES), BF16),
            pltpu.VMEM((rows, LANES), F32),
            pltpu.VMEM((10, rows, LANES), F32),
            pltpu.VMEM((SUB * groups, taps), F32),
            pltpu.VMEM((ctx_count, piece, groups), F32),
            pltpu.VMEM((ctx_count - 1, piece, groups), F32),
            pltpu.VMEM((1, width), F32),
            pltpu.VMEM((1, width), F32),
            pltpu.VMEM((reach, 1, width), F32),
            pltpu.VMEM((reach, 1, width), F32),
            dma((halo_parts,)), dma((halo_parts,)), dma((halo_parts,)), dma((halo_parts,)),
            dma((reach,)), dma((reach,)), dma((reach,)), dma((reach,)),
            dma((ctx_count - 1,)), dma((ctx_count - 1,)),
        ],
        compiler_params=pltpu.CompilerParams(collective_id=0, has_side_effects=True),
        name="hyena_mixers",
    )(*args)


def solution(mesh):
    in_specs = (
        P(("dp", "ctx"), "tp"),
        P(("dp", "ctx"), "tp"),
        P(None, "tp"),
        P("tp"),
        P("tp"),
        P(("dp", "ctx"), "tp"),
        P("dp"),
        P(("dp", "ctx"), "tp"),
    )
    out_specs = (P(("dp", "ctx"), "tp"), P(("dp", "ctx"), "tp"), P(("dp", "ctx"), "tp"))
    return jax.shard_map(
        on_device, mesh=mesh, in_specs=in_specs, out_specs=out_specs, check_vma=False
    )
```

```python
import functools

import jax
import jax.numpy as jnp
from jax import lax
from jax.experimental import pallas as pl
from jax.experimental.pallas import tpu as pltpu
from jax.sharding import PartitionSpec as P

MESH = pl.DeviceIdType.MESH
LANES = 128
SUB = 8
HALO_PARTS = 8
F32 = jnp.float32
BF16 = jnp.bfloat16


def seg_of(lengths_ref, places, total):
    offset = jnp.int32(0)
    seg = jnp.zeros(places.shape, jnp.int32)
    for i in range(lengths_ref.shape[0]):
        seg = seg + (places >= offset).astype(jnp.int32)
        offset = offset + lengths_ref[i]
    return seg + (places >= total).astype(jnp.int32)


def one_minus_exp(x):
    series = jnp.ones_like(x)
    for n in range(9, 1, -1):
        series = 1.0 - x / n * series
    return jnp.where(x < 0.5, x * series, 1.0 - jnp.exp(-x))


def kernel(
    ctx_count, reach, halo_parts,
    lengths, k_ref, v_ref, filt_ref, rate_ref, residue_ref, gate_ref, gout_ref,
    mixed_ref, gv_ref, gf_ref,
    u_ext, g_ext, adj, state, scale, taps, taps_rev, mask_f, mask_b, diag_seg,
    scan_masks, acc, partial, gf_slots, carry_f, carry_b, carry_f_in, carry_b_in,
    u_send, u_recv, g_send, g_recv, cf_send, cf_recv, cb_send, cb_recv, gf_send, gf_recv,
):
    rows, width = k_ref.shape
    groups = filt_ref.shape[1]
    per_group = width // groups
    per_chunk = LANES // per_group
    chunks = width // LANES
    part_width = width // halo_parts
    total = rows * ctx_count
    me = lax.axis_index("ctx")
    first = me * rows

    barrier = pltpu.get_barrier_semaphore()

    @pl.loop(1, ctx_count)
    def _(step):
        pl.semaphore_signal(
            barrier, inc=1, device_id={"ctx": lax.rem(me + step, ctx_count)}, device_id_type=MESH
        )

    pl.semaphore_wait(barrier, ctx_count - 1)

    def u_copy(part):
        cols = pl.ds(part * part_width, part_width)
        return pltpu.make_async_remote_copy(
            src_ref=u_ext.at[pl.ds(rows, rows), cols],
            dst_ref=u_ext.at[pl.ds(0, rows), cols],
            send_sem=u_send.at[part],
            recv_sem=u_recv.at[part],
            device_id={"ctx": lax.rem(me + 1, ctx_count)},
            device_id_type=MESH,
        )

    def g_copy(part):
        cols = pl.ds(part * part_width, part_width)
        return pltpu.make_async_remote_copy(
            src_ref=g_ext.at[pl.ds(0, rows), cols],
            dst_ref=g_ext.at[pl.ds(rows, rows), cols],
            send_sem=g_send.at[part],
            recv_sem=g_recv.at[part],
            device_id={"ctx": lax.rem(me + ctx_count - 1, ctx_count)},
            device_id_type=MESH,
        )

    def carry_copy(k, forward):
        src, dst, send, recv = (
            (carry_f, carry_f_in, cf_send, cf_recv)
            if forward
            else (carry_b, carry_b_in, cb_send, cb_recv)
        )
        peer = me + 1 + k if forward else me + ctx_count - 1 - k
        return pltpu.make_async_remote_copy(
            src_ref=src,
            dst_ref=dst.at[k],
            send_sem=send.at[k],
            recv_sem=recv.at[k],
            device_id={"ctx": lax.rem(peer, ctx_count)},
            device_id_type=MESH,
        )

    for part in range(halo_parts):
        cols = slice(part * part_width, (part + 1) * part_width)
        u_ext[rows:, cols] = (k_ref[:, cols].astype(F32) * v_ref[:, cols].astype(F32)).astype(BF16)

        @pl.when(me < ctx_count - 1)
        def _():
            u_copy(part).start()

    @pl.when(me == 0)
    def _():
        u_ext[:rows, :] = jnp.zeros((rows, width), BF16)

    @pl.when(me == ctx_count - 1)
    def _():
        g_ext[rows:, :] = jnp.zeros((rows, width), BF16)

    rate_all = rate_ref[...]
    scale[...] = residue_ref[...] * jnp.sqrt(one_minus_exp(2.0 * rate_all))
    row = lax.broadcasted_iota(jnp.int32, (rows, LANES), 0)
    seg = seg_of(lengths, first + row, total)
    sub = lax.rem(row, SUB)
    tile = row - sub
    for i, k in enumerate((1, 2, 4)):
        same = (seg == pltpu.roll(seg, k, 0)) & (sub >= k)
        scan_masks[i] = same.astype(F32)
        same = (seg == pltpu.roll(seg, rows - k, 0)) & (sub + k < SUB)
        scan_masks[4 + i] = same.astype(F32)
    scan_masks[3] = (seg == seg_of(lengths, first + tile - 1, total)).astype(F32)
    scan_masks[7] = (seg == seg_of(lengths, first + tile + SUB, total)).astype(F32)
    lane_one = jnp.zeros((1, LANES), jnp.int32)
    seg_before = seg_of(lengths, first - 1 + lane_one, total)
    seg_after = seg_of(lengths, first + rows + lane_one, total)
    scan_masks[8] = (seg == seg_before).astype(F32)
    scan_masks[9] = (seg == seg_after).astype(F32)
    lane = lax.broadcasted_iota(jnp.int32, (rows, LANES), 1)
    lane_row = lax.broadcasted_iota(jnp.int32, (1, LANES), 1)
    seg_prev = seg_of(lengths, first - rows + lane_row, total)
    seg_here = seg_of(lengths, first + lane_row, total)
    seg_next = seg_of(lengths, first + rows + lane_row, total)
    f_left = ((seg == seg_prev) & (lane > row)).astype(F32)
    f_right = ((seg == seg_here) & (lane <= row)).astype(F32)
    mask_f[:, :LANES] = f_left.astype(BF16)
    mask_f[:, LANES:] = f_right.astype(BF16)
    diag_seg[...] = f_left + f_right
    mask_b[:, :LANES] = ((seg == seg_here) & (lane >= row)).astype(F32).astype(BF16)
    mask_b[:, LANES:] = ((seg == seg_next) & (lane < row)).astype(F32).astype(BF16)
    flip = (lax.rem(row + lane, LANES) == 0).astype(F32)
    eye = (row == lane).astype(F32)
    over_taps = (((0,), (0,)), ((), ()))
    filt = filt_ref[...]
    taps[...] = lax.dot_general(filt, eye.astype(BF16), over_taps, preferred_element_type=F32)
    taps_rev[...] = lax.dot_general(filt, flip.astype(BF16), over_taps, preferred_element_type=F32)

    sub8 = lax.broadcasted_iota(jnp.int32, (SUB, LANES), 0).astype(F32)
    tiles = rows // SUB

    def chunk_cols(q):
        return pl.ds(pl.multiple_of(q * LANES, LANES), LANES)

    def scan_tiles(values, rate, forward):
        base = 0 if forward else 4
        steps = [jnp.exp(-k * rate) for k in (1.0, 2.0, 4.0)]
        far = jnp.exp(-((sub8 + 1.0) if forward else (SUB - sub8)) * rate)
        out = [None] * tiles
        carry = None
        for n in range(tiles) if forward else reversed(range(tiles)):
            here = slice(n * SUB, (n + 1) * SUB)
            x = values[here, :]
            for i, k in enumerate((1, 2, 4)):
                shifted = pltpu.roll(x, k if forward else SUB - k, 0)
                x = x + steps[i] * scan_masks[base + i, here, :] * shifted
            if carry is not None:
                x = x + far * scan_masks[base + 3, here, :] * carry
            carry = x[SUB - 1 : SUB, :] if forward else x[0:1, :]
            out[n] = x
        return out, carry

    def carried(slots, cols, rate, forward):
        value = slots[0, :, cols]
        for k in range(1, reach):
            edge = first - 1 - rows * k if forward else first + rows + rows * k
            there = seg_of(lengths, edge + lane_one, total)
            same = (there == (seg_before if forward else seg_after)).astype(F32)
            value = value + slots[k, :, cols] * same * jnp.exp(-float(rows * k) * rate)
        return value

    @pl.loop(0, chunks, unroll=4)
    def _(q):
        cols = chunk_cols(q)
        rate = rate_ref[:, cols]
        long = (scale[:, cols] * gate_ref[:, cols].astype(F32) * gout_ref[:, cols].astype(F32))
        out, carry = scan_tiles(long.astype(BF16).astype(F32), rate, False)
        for n in range(tiles):
            adj[n * SUB : (n + 1) * SUB, cols] = out[n]
        carry_b[:, cols] = carry

    for k in range(reach):

        @pl.when(me >= 1 + k)
        def _():
            carry_copy(k, False).start()

        @pl.when(me + 1 + k >= ctx_count)
        def _():
            carry_b_in[k] = jnp.zeros((1, width), F32)

    for k in range(reach):

        @pl.when(me + 1 + k < ctx_count)
        def _():
            carry_copy(k, False).wait_recv()

    for part in range(halo_parts):
        per_part = chunks // halo_parts

        @pl.loop(part * per_part, (part + 1) * per_part, unroll=4)
        def _(q):
            cols = chunk_cols(q)
            rate = rate_ref[:, cols]
            value = carried(carry_b_in, cols, rate, False)
            far = jnp.exp(-(SUB - sub8) * rate)
            eighth = jnp.exp(-float(SUB) * rate)
            for n in reversed(range(tiles)):
                here = slice(n * SUB, (n + 1) * SUB)
                x = adj[here, cols] + far * scan_masks[9, here, :] * value
                adj[here, cols] = x
                value = value * eighth
            g_ext[:rows, cols] = adj[:, cols].astype(BF16)

        @pl.when(me > 0)
        def _():
            g_copy(part).start()

    def bands(tap_rows, mask):
        blocks = []
        for g in range(per_chunk):
            skew = pltpu.roll(
                jnp.broadcast_to(tap_rows[g : g + 1, :], (SUB, LANES)), 0, 1,
                stride=1, stride_axis=0,
            )
            circ = jnp.concatenate(
                [skew] + [pltpu.roll(skew, n * SUB, 1) for n in range(1, tiles)], axis=0
            ).astype(BF16)
            blocks.append(
                jnp.concatenate([circ * mask[:, :LANES], circ * mask[:, LANES:]], axis=1)
            )
        return jnp.concatenate(blocks, axis=0)

    group_of_lane = lane // per_group

    for part in range(halo_parts):

        @pl.when(me > 0)
        def _():
            u_copy(part).wait_recv()

        @pl.loop(part * per_part, (part + 1) * per_part, unroll=2)
        def _(q):
            cols = chunk_cols(q)
            window = u_ext[:, cols]
            grads = g_ext[:rows, cols]
            group_rows = pl.ds(pl.multiple_of(q * per_chunk, per_chunk), per_chunk)
            all_y = jnp.dot(
                bands(taps_rev[group_rows, :], mask_f), window,
                preferred_element_type=F32,
            )
            y = all_y[:rows, :]
            for g in range(1, per_chunk):
                y = jnp.where(group_of_lane == g, all_y[g * rows : (g + 1) * rows, :], y)
            own = jnp.concatenate(
                [jnp.where(group_of_lane == g, grads, jnp.zeros_like(grads)) for g in range(per_chunk)],
                axis=0,
            )
            all_prod = lax.dot_general(
                own, window, (((1,), (1,)), ((), ())), preferred_element_type=F32
            )
            for g in range(per_chunk):
                prod = all_prod[g * rows : (g + 1) * rows, :]
                prod = jnp.where(lane <= row, prod[:, LANES:], prod[:, :LANES]) * diag_seg[...]
                folded = prod[:SUB, :]
                for n in range(1, tiles):
                    folded = folded + pltpu.roll(
                        prod[n * SUB : (n + 1) * SUB, :], LANES - n * SUB, 1
                    )
                acc[pl.ds(pl.multiple_of((q * per_chunk + g) * SUB, SUB), SUB), :] = folded
            out, carry = scan_tiles(y.astype(BF16).astype(F32), rate_ref[:, cols], True)
            for n in range(tiles):
                state[n * SUB : (n + 1) * SUB, cols] = out[n]
            carry_f[:, cols] = carry

    for k in range(reach):

        @pl.when(me + 1 + k < ctx_count)
        def _():
            carry_copy(k, True).start()

        @pl.when(me < 1 + k)
        def _():
            carry_f_in[k] = jnp.zeros((1, width), F32)

    skewed = acc[pl.ds(0, groups, stride=SUB), :]
    for r in range(1, SUB):
        skewed = skewed + pltpu.roll(acc[pl.ds(r, groups, stride=SUB), :], LANES - r, 1)
    by_tap = lax.dot_general(
        flip, skewed, (((1,), (1,)), ((), ())),
        precision=lax.Precision.HIGHEST, preferred_element_type=F32,
    )
    piece = rows // ctx_count
    for i in range(ctx_count):
        partial[i] = by_tap[i * piece : (i + 1) * piece, :]

    def gf_copy(step):
        peer = lax.rem(me + step, ctx_count)
        return pltpu.make_async_remote_copy(
            src_ref=partial.at[peer],
            dst_ref=gf_slots.at[step - 1],
            send_sem=gf_send.at[step - 1],
            recv_sem=gf_recv.at[step - 1],
            device_id={"ctx": peer},
            device_id_type=MESH,
        )

    @pl.loop(1, ctx_count)
    def _(step):
        gf_copy(step).start()

    def finish_forward():
        for k in range(reach):

            @pl.when(me >= 1 + k)
            def _():
                carry_copy(k, True).wait_recv()

        @pl.loop(0, chunks, unroll=4)
        def _(q):
            cols = chunk_cols(q)
            rate = rate_ref[:, cols]
            value = carried(carry_f_in, cols, rate, True)
            far = jnp.exp(-(sub8 + 1.0) * rate)
            eighth = jnp.exp(-float(SUB) * rate)
            for n in range(tiles):
                here = slice(n * SUB, (n + 1) * SUB)
                x = state[here, cols] + far * scan_masks[8, here, :] * value
                state[here, cols] = x
                value = value * eighth
            z_long = (scale[:, cols] * state[:, cols]).astype(BF16)
            mixed_ref[:, cols] = (gate_ref[:, cols].astype(F32) * z_long.astype(F32)).astype(BF16)

    for part in range(halo_parts):

        @pl.when(me < ctx_count - 1)
        def _():
            g_copy(part).wait_recv()

        @pl.loop(part * per_part, (part + 1) * per_part, unroll=2)
        def _(q):
            cols = chunk_cols(q)
            window = g_ext[:, cols]
            group_rows = pl.ds(pl.multiple_of(q * per_chunk, per_chunk), per_chunk)
            all_u = jnp.dot(
                bands(taps[group_rows, :], mask_b), window,
                preferred_element_type=F32,
            )
            grad_u = all_u[:rows, :]
            for g in range(1, per_chunk):
                grad_u = jnp.where(group_of_lane == g, all_u[g * rows : (g + 1) * rows, :], grad_u)
            gv_ref[:, cols] = (k_ref[:, cols].astype(F32) * grad_u).astype(BF16)

        if part == (halo_parts - 1) // 2:
            finish_forward()

    own = partial[me]

    def add_slot(step, value):
        gf_copy(step).wait_recv()
        return value + gf_slots[step - 1]

    gf_ref[...] = lax.fori_loop(1, ctx_count, add_slot, own)

    @pl.loop(1, ctx_count)
    def _(step):
        gf_copy(step).wait_send()

    for k in range(reach):

        @pl.when(me >= 1 + k)
        def _():
            carry_copy(k, False).wait_send()

        @pl.when(me + 1 + k < ctx_count)
        def _():
            carry_copy(k, True).wait_send()

    for part in range(halo_parts):

        @pl.when(me < ctx_count - 1)
        def _():
            u_copy(part).wait_send()

        @pl.when(me > 0)
        def _():
            g_copy(part).wait_send()


def crossing(lengths_ref, edge):
    offset = jnp.int32(0)
    before = jnp.int32(0)
    after = jnp.int32(0)
    for i in range(lengths_ref.shape[0]):
        end = offset + lengths_ref[i]
        inside = (offset < edge) & (end > edge)
        before = jnp.where(inside, edge - offset, before)
        after = jnp.where(inside, end - edge, after)
        offset = end
    return before, after


def short_kernel(
    ctx_count, halo_parts,
    lengths, k_hbm, v_hbm, filt_ref, rate_ref, residue_ref, gate_hbm, gout_hbm,
    mixed_ref, gv_ref, gf_ref,
    k_ref, v_ref, gate_ref, gout_ref, load,
    u_own, g_own, u_out, g_out, u_in, g_in, relay, adj, y_own, circ_f, circ_b,
    scale, taps, taps_rev, mask_f, mask_b, diag_seg, scan_masks, even_odd, pair_lanes,
    right_rows, left_rows, even_odd_t, left_t, right_t, quad_u, quad_g, u_t, g_t, acc, acc_t, partial, gf_slots,
    carry_f, carry_b, carry_f_in, carry_b_in,
    u_send, u_recv, g_send, g_recv, cf_send, cf_recv, cb_send, cb_recv,
    relay_send, relay_recv, gf_send, gf_recv,
):
    rows, width = k_ref.shape
    groups = filt_ref.shape[1]
    half = rows // 2
    per_group = width // groups
    per_chunk = LANES // per_group
    pairs = per_chunk // 2
    chunks = width // LANES
    per_part = chunks // halo_parts
    part_width = width // halo_parts
    total = rows * ctx_count
    tiles = rows // SUB
    me = lax.axis_index("ctx")
    first = me * rows
    has_next = me < ctx_count - 1
    has_prev = me > 0

    loads = [
        pltpu.make_async_copy(src, dst, load.at[n])
        for n, (src, dst) in enumerate(
            ((gate_hbm, gate_ref), (gout_hbm, gout_ref), (k_hbm, k_ref), (v_hbm, v_ref))
        )
    ]
    for one in loads:
        one.start()

    barrier = pltpu.get_barrier_semaphore()

    @pl.loop(1, ctx_count)
    def _(step):
        pl.semaphore_signal(
            barrier, inc=1, device_id={"ctx": lax.rem(me + step, ctx_count)}, device_id_type=MESH
        )

    def halo_copy(part, forward):
        src, dst, send, recv = (
            (u_out, u_in, u_send, u_recv) if forward else (g_out, g_in, g_send, g_recv)
        )
        cols = pl.ds(pl.multiple_of(part * part_width, LANES), part_width)
        peer = me + 1 if forward else me + ctx_count - 1
        return pltpu.make_async_remote_copy(
            src_ref=src.at[:, cols],
            dst_ref=dst.at[:, cols],
            send_sem=send.at[part],
            recv_sem=recv.at[part],
            device_id={"ctx": lax.rem(peer, ctx_count)},
            device_id_type=MESH,
        )

    def carry_b_copy():
        return pltpu.make_async_remote_copy(
            src_ref=carry_b,
            dst_ref=carry_b_in,
            send_sem=cb_send.at[0],
            recv_sem=cb_recv.at[0],
            device_id={"ctx": lax.rem(me + ctx_count - 1, ctx_count)},
            device_id_type=MESH,
        )

    def carry_f_copy():
        return pltpu.make_async_remote_copy(
            src_ref=carry_f,
            dst_ref=carry_f_in,
            send_sem=cf_send.at[0],
            recv_sem=cf_recv.at[0],
            device_id={"ctx": lax.rem(me + 1, ctx_count)},
            device_id_type=MESH,
        )

    relays = ctx_count == 4

    def relay_copy(part, forward):
        cols = pl.ds(pl.multiple_of(part * part_width, LANES), part_width)
        src, send = (u_out, u_send) if forward else (g_out, g_send)
        return pltpu.make_async_remote_copy(
            src_ref=src.at[:, cols],
            dst_ref=relay.at[:, cols],
            send_sem=send.at[part],
            recv_sem=relay_recv.at[part],
            device_id={"ctx": 3 if forward else 0},
            device_id_type=MESH,
        )

    def onward_copy(part, forward):
        cols = pl.ds(pl.multiple_of(part * part_width, LANES), part_width)
        dst, recv = (u_in, u_recv) if forward else (g_in, g_recv)
        return pltpu.make_async_remote_copy(
            src_ref=relay.at[:, cols],
            dst_ref=dst.at[:, cols],
            send_sem=relay_send.at[part],
            recv_sem=recv.at[part],
            device_id={"ctx": 2 if forward else 1},
            device_id_type=MESH,
        )

    @pl.when(jnp.logical_not(has_prev))
    def _():
        u_in[...] = jnp.zeros(u_in.shape, BF16)
        carry_f_in[...] = jnp.zeros(carry_f_in.shape, F32)

    @pl.when(jnp.logical_not(has_next))
    def _():
        g_in[...] = jnp.zeros(g_in.shape, BF16)
        carry_b_in[...] = jnp.zeros(carry_b_in.shape, F32)

    left_a, left_b = crossing(lengths, first)
    right_a, right_b = crossing(lengths, first + rows)

    rate_all = rate_ref[...]
    scale[...] = residue_ref[...] * jnp.sqrt(one_minus_exp(2.0 * rate_all))
    row = lax.broadcasted_iota(jnp.int32, (rows, LANES), 0)
    lane = lax.broadcasted_iota(jnp.int32, (rows, LANES), 1)
    lane_row = lax.broadcasted_iota(jnp.int32, (1, LANES), 1)
    row_half = lax.broadcasted_iota(jnp.int32, (half, LANES), 0)
    lane_half = lax.broadcasted_iota(jnp.int32, (half, LANES), 1)
    seg = seg_of(lengths, first + row, total)
    sub = lax.rem(row, SUB)
    tile = row - sub
    for i, k in enumerate((1, 2, 4)):
        same = (seg == pltpu.roll(seg, rows - k, 0)) & (sub + k < SUB)
        scan_masks[4 + i] = same.astype(F32)
    scan_masks[7] = (seg == seg_of(lengths, first + tile + SUB, total)).astype(F32)
    lane_one = jnp.zeros((1, LANES), jnp.int32)
    scan_masks[10] = (seg == seg_of(lengths, first + lane_one, total)).astype(F32)
    group_of_lane = lane // per_group
    pair_of_lane = group_of_lane // 2
    send_u = right_a <= half
    send_gpart = left_a <= half
    for e in range(2):
        lanes = lax.rem(group_of_lane, 2) == e
        right_rows[e * rows : (e + 1) * rows, :] = (
            (lanes & (row >= rows - right_a)).astype(F32).astype(BF16)
        )
        left_rows[e * rows : (e + 1) * rows, :] = (
            (lanes & (row < left_b)).astype(F32).astype(BF16)
        )
    flip = (lax.rem(row + lane, LANES) == 0).astype(F32)
    eye = (row == lane).astype(F32)
    over_taps = (((0,), (0,)), ((), ()))
    filt = filt_ref[...]
    taps[...] = lax.dot_general(filt, eye.astype(BF16), over_taps, preferred_element_type=F32)
    taps_rev[...] = lax.dot_general(filt, flip.astype(BF16), over_taps, preferred_element_type=F32)
    sub8 = lax.broadcasted_iota(jnp.int32, (SUB, LANES), 0).astype(F32)

    def chunk_cols(q):
        return pl.ds(pl.multiple_of(q * LANES, LANES), LANES)

    def group_rows(q, g):
        return pl.ds(pl.multiple_of((q * per_chunk + g) * rows, rows), rows)

    def scan_tiles(values, rate, forward, carry=None):
        base = 0 if forward else 4
        steps = [jnp.exp(-k * rate) for k in (1.0, 2.0, 4.0)]
        far = jnp.exp(-((sub8 + 1.0) if forward else (SUB - sub8)) * rate)
        out = [None] * tiles
        for n in range(tiles) if forward else reversed(range(tiles)):
            here = slice(n * SUB, (n + 1) * SUB)
            x = values[here, :]
            for i, k in enumerate((1, 2, 4)):
                shifted = pltpu.roll(x, k if forward else SUB - k, 0)
                x = x + steps[i] * scan_masks[base + i, here, :] * shifted
            if carry is not None:
                x = x + far * scan_masks[base + 3, here, :] * carry
            carry = x[SUB - 1 : SUB, :] if forward else x[0:1, :]
            out[n] = x
        return out, carry

    def circulant(tap_rows, g):
        skew = pltpu.roll(
            jnp.broadcast_to(tap_rows[g : g + 1, :], (2 * SUB, LANES)), 0, 1,
            stride=1, stride_axis=0,
        ).astype(BF16)
        return jnp.concatenate(
            [skew] + [pltpu.roll(skew, 2 * n * SUB, 1) for n in range(1, tiles // 2)], axis=0
        )

    def pick(outs, n_rows, index):
        value = outs[:n_rows, :]
        for p in range(1, outs.shape[0] // n_rows):
            value = jnp.where(index == p, outs[p * n_rows : (p + 1) * n_rows, :], value)
        return value

    def beside(x):
        return jnp.concatenate([x, x], axis=1)

    def twice(x):
        return jnp.concatenate([x, x], axis=0)

    def fold(prod):
        folded = prod[:SUB, :]
        for n in range(1, prod.shape[0] // SUB):
            folded = folded + pltpu.roll(prod[n * SUB : (n + 1) * SUB, :], LANES - n * SUB, 1)
        return folded

    pair_half = lane_half // (2 * per_group)
    across = (((1,), (1,)), ((), ()))

    for one in loads:
        one.wait()

    @pl.loop(0, chunks // 4)
    def _(step):
        for c in range(4):
            cols = chunk_cols(step * 4 + c)
            rate = rate_ref[:, cols]
            long = scale[:, cols] * gate_ref[:, cols].astype(F32) * gout_ref[:, cols].astype(F32)
            long = long.astype(BF16).astype(F32) * scan_masks[10]
            eighth = jnp.exp(-float(SUB) * rate)
            run = long[rows - SUB :, :]
            for n in reversed(range(tiles - 1)):
                run = run * eighth + long[n * SUB : (n + 1) * SUB, :]
            carry_b[:, cols] = jnp.sum(run * jnp.exp(-sub8 * rate), axis=0, keepdims=True)

    pl.semaphore_wait(barrier, ctx_count - 1)

    @pl.when(has_prev)
    def _():
        carry_b_copy().start()

    def join(xs):
        return jnp.concatenate(
            [jnp.concatenate(xs[2 * p : 2 * p + 2], axis=1) for p in range(pairs)], axis=0
        )

    def pair_bands(circ, q, mask):
        return jnp.concatenate(
            [
                jnp.concatenate(
                    [circ[group_rows(q, 2 * p + e), :] * mask for e in range(2)], axis=1
                )
                for p in range(pairs)
            ],
            axis=0,
        )

    def own_y(q):
        cols = chunk_cols(q)
        rate = rate_ref[:, cols]
        y = jnp.dot(
            pair_bands(circ_f, q, mask_f[...]), twice(u_own[:, cols]) * even_odd[...],
            preferred_element_type=F32,
        )
        y = pick(y, rows, pair_of_lane)
        y_own[:, cols] = y
        last = y.astype(BF16).astype(F32) * scan_masks[8]
        eighth = jnp.exp(-float(SUB) * rate)
        run = last[:SUB, :]
        for n in range(1, tiles):
            run = run * eighth + last[n * SUB : (n + 1) * SUB, :]
        carry_f[:, cols] = jnp.sum(
            run * jnp.exp(-(SUB - 1.0 - sub8) * rate), axis=0, keepdims=True
        )

    @pl.loop(0, halo_parts)
    def _(part):
        for c in range(per_part):
            q = part * per_part + c
            cols = chunk_cols(q)
            u = (k_ref[:, cols].astype(F32) * v_ref[:, cols].astype(F32)).astype(BF16)
            u_own[:, cols] = u
            long = scale[:, cols] * gate_ref[:, cols].astype(F32) * gout_ref[:, cols].astype(F32)
            out, _ = scan_tiles(long.astype(BF16).astype(F32), rate_ref[:, cols], False)
            for n in range(tiles):
                adj[n * SUB : (n + 1) * SUB, cols] = out[n]
            g = jnp.concatenate(out, axis=0).astype(BF16)
            tap_rows = pl.ds(pl.multiple_of(q * per_chunk, per_chunk), per_chunk)
            f_rows, b_rows = taps_rev[tap_rows, :], taps[tap_rows, :]
            top, bottom = [], []
            for i in range(per_chunk):
                f, b = circulant(f_rows, i), circulant(b_rows, i)
                circ_f[group_rows(q, i), :] = f
                circ_b[group_rows(q, i), :] = b
                top.append(f[:half, :])
                bottom.append(b[half:, :])
            y_part = jnp.dot(join(top), twice(u) * right_rows[...], preferred_element_type=F32)
            y_part = pick(y_part, half, pair_half)
            g_part = jnp.dot(join(bottom), twice(g) * left_rows[...], preferred_element_type=F32)
            g_part = pick(g_part, half, pair_half)
            y_part = jnp.where(row_half < right_b, y_part, 0.0)
            g_part = jnp.where(row_half >= half - left_a, g_part, 0.0)
            u_tail = jnp.where(row_half >= half - right_a, u[half:, :].astype(F32), 0.0)
            g_head = jnp.where(row_half < left_b, g[:half, :].astype(F32), 0.0)
            u_out[:, cols] = jnp.where(send_u, u_tail, y_part).astype(BF16)
            g_out[:, cols] = jnp.where(send_gpart, g_part, g_head).astype(BF16)

        by_relay = lax.rem(part, 2) == 1 if relays else False

        @pl.when(has_next)
        def _():
            if relays:
                pl.when((me == 1) & by_relay)(lambda: relay_copy(part, True).start())
                pl.when((me != 1) | jnp.logical_not(by_relay))(
                    lambda: halo_copy(part, True).start()
                )
            else:
                halo_copy(part, True).start()

        @pl.when(has_prev)
        def _():
            if relays:
                pl.when((me == 2) & by_relay)(lambda: relay_copy(part, False).start())
                pl.when((me != 2) | jnp.logical_not(by_relay))(
                    lambda: halo_copy(part, False).start()
                )
            else:
                halo_copy(part, False).start()

    def own_terms(q):
        cols = chunk_cols(q)
        rate = rate_ref[:, cols]
        value = carry_b_in[:, cols]
        far = jnp.exp(-(SUB - sub8) * rate)
        eighth = jnp.exp(-float(SUB) * rate)
        out = [None] * tiles
        for n in reversed(range(tiles)):
            here = slice(n * SUB, (n + 1) * SUB)
            out[n] = adj[here, cols] + far * scan_masks[9, here, :] * value
            value = value * eighth
        g = jnp.concatenate(out, axis=0).astype(BF16)
        g_own[:, cols] = g
        by_pair = jnp.concatenate([g * pair_lanes[p] for p in range(pairs)], axis=0)
        ut, gt = u_own[:, cols].T, g.T
        t_rows = pl.ds(pl.multiple_of(q * LANES, LANES), LANES)
        u_t[t_rows, :] = ut
        g_t[t_rows, :] = gt
        prods = jnp.dot(by_pair, beside(ut) * even_odd_t[...], preferred_element_type=F32)
        for p in range(pairs):
            for e in range(2):
                prod = prods[p * rows : (p + 1) * rows, e * LANES : (e + 1) * LANES]
                at = pl.multiple_of((q * per_chunk + 2 * p + e) * SUB, SUB)
                acc[pl.ds(at, SUB), :] = fold(prod * diag_seg[...])

    seg = seg_of(lengths, first + row, total)
    for i, k in enumerate((1, 2, 4)):
        same = (seg == pltpu.roll(seg, k, 0)) & (sub >= k)
        scan_masks[i] = same.astype(F32)
    scan_masks[3] = (seg == seg_of(lengths, first + tile - 1, total)).astype(F32)
    lane_one = jnp.zeros((1, LANES), jnp.int32)
    scan_masks[8] = (seg == seg_of(lengths, first + rows - 1 + lane_one, total)).astype(F32)
    scan_masks[9] = (seg == seg_of(lengths, first + rows + lane_one, total)).astype(F32)
    seg_here = seg_of(lengths, first + lane_row, total)
    own = ((seg == seg_here) & (lane <= row)).astype(F32)
    mask_f[...] = own.astype(BF16)
    diag_seg[...] = own
    mask_b[...] = ((seg == seg_here) & (lane >= row)).astype(F32).astype(BF16)
    for e in range(2):
        even_odd[e * rows : (e + 1) * rows, :] = (
            (lax.rem(group_of_lane, 2) == e).astype(F32).astype(BF16)
        )
    group_of_row = row // per_group
    for e in range(2):
        rows_e = lax.rem(group_of_row, 2) == e
        at = slice(e * LANES, (e + 1) * LANES)
        even_odd_t[:, at] = rows_e.astype(F32).astype(BF16)
        left_t[:, at] = jnp.where(
            send_gpart, (rows_e & (lane < left_b)).astype(F32), 0.0
        ).astype(BF16)
        right_t[:, at] = jnp.where(
            send_u, 0.0, (rows_e & (lane >= rows - right_a)).astype(F32)
        ).astype(BF16)
    for p in range(pairs):
        pair_lanes[p] = (pair_of_lane == p).astype(F32).astype(BF16)
    group_half = lane_half // per_group
    for e in range(4):
        lanes = lax.rem(group_half, 4) == e
        quad_u[e * half : (e + 1) * half, :] = (
            jnp.where(send_gpart, lanes.astype(F32), 0.0).astype(BF16)
        )
        quad_g[e * half : (e + 1) * half, :] = (
            jnp.where(send_u, 0.0, lanes.astype(F32)).astype(BF16)
        )

    @pl.when(has_next)
    def _():
        carry_b_copy().wait_recv()

    @pl.loop(0, chunks // 4)
    def _(step):
        if relays:
            for forward, by in ((True, 3), (False, 0)):

                @pl.when(me == by)
                def _():
                    relay_copy(2 * step + 1, forward).wait_recv()
                    onward_copy(2 * step + 1, forward).start()

        for c in range(4):
            own_y(step * 4 + c)
            own_terms(step * 4 + c)

    @pl.when(has_next)
    def _():
        carry_f_copy().start()

    low_lanes = lane < half

    def quad_bands(circ, q, forward):
        quads = []
        for g in range(0, per_chunk, 4):
            halves = []
            for e in (0, 2):
                one = circ[group_rows(q, g + e), :]
                two = circ[group_rows(q, g + e + 1), :]
                if forward:
                    one = jnp.concatenate([one[half:, :], one[:half, :]], axis=0)
                else:
                    two = jnp.concatenate([two[half:, :], two[:half, :]], axis=0)
                halves.append(jnp.where(low_lanes, one, two))
            quads.append(jnp.concatenate(halves, axis=1))
        return jnp.concatenate(quads, axis=0)

    def four(x):
        return jnp.concatenate([x, x, x, x], axis=0)

    quad_of_lane = lane // (4 * per_group)

    def cross_terms(q):
        cols = chunk_cols(q)
        u_msg, g_msg = u_in[:, cols], g_in[:, cols]
        t_rows = pl.ds(pl.multiple_of(q * LANES, LANES), LANES)
        lhs = jnp.concatenate([u_msg * pair_lanes[p, :half, :] for p in range(pairs)], axis=0)
        prods = jnp.dot(lhs, beside(g_t[t_rows, :]) * left_t[...], preferred_element_type=F32)
        lhs = jnp.concatenate([g_msg * pair_lanes[p, :half, :] for p in range(pairs)], axis=0)
        prods2 = jnp.dot(lhs, beside(u_t[t_rows, :]) * right_t[...], preferred_element_type=F32)
        for p in range(pairs):
            for e in range(2):
                at = pl.ds(pl.multiple_of((q * per_chunk + 2 * p + e) * SUB, SUB), SUB)
                cut = (slice(p * half, (p + 1) * half), slice(e * LANES, (e + 1) * LANES))
                acc_t[at, :] = fold(prods[cut])
                acc[at, :] = acc[at, :] + fold(prods2[cut])

    def finish(q):
        cols = chunk_cols(q)
        u_msg, g_msg = u_in[:, cols], g_in[:, cols]
        rate = rate_ref[:, cols]
        y = jnp.dot(
            quad_bands(circ_f, q, True), four(u_msg) * quad_u[...], preferred_element_type=F32
        )
        y = pick(y, rows, quad_of_lane)
        y_part = jnp.where(send_gpart, 0.0, u_msg.astype(F32))
        y = y + jnp.concatenate([y_part, jnp.zeros_like(y_part)], axis=0)
        y = y_own[:, cols] + jnp.where(row < left_b, y, 0.0)
        out, _ = scan_tiles(
            y.astype(BF16).astype(F32), rate, True, carry_f_in[:, cols]
        )
        z_long = (scale[:, cols] * jnp.concatenate(out, axis=0)).astype(BF16)
        mixed_ref[:, cols] = (gate_ref[:, cols].astype(F32) * z_long.astype(F32)).astype(BF16)
        gu = jnp.dot(
            quad_bands(circ_b, q, False), four(g_msg) * quad_g[...], preferred_element_type=F32
        )
        gu = pick(gu, rows, quad_of_lane)
        g_part = jnp.where(send_u, g_msg.astype(F32), 0.0)
        gu = gu + jnp.concatenate([jnp.zeros_like(g_part), g_part], axis=0)
        own = jnp.dot(
            pair_bands(circ_b, q, mask_b[...]), twice(g_own[:, cols]) * even_odd[...],
            preferred_element_type=F32,
        )
        gu = pick(own, rows, pair_of_lane) + jnp.where(row >= rows - right_a, gu, 0.0)
        gv_ref[:, cols] = (k_ref[:, cols].astype(F32) * gu).astype(BF16)

    @pl.loop(0, chunks // 4)
    def _(step):
        @pl.when(has_prev)
        def _():
            for n in range(2):
                halo_copy(step * 2 + n, True).wait_recv()

        @pl.when(has_next)
        def _():
            for n in range(2):
                halo_copy(step * 2 + n, False).wait_recv()

        for c in range(4):
            cross_terms(step * 4 + c)

    skewed = acc[pl.ds(0, groups, stride=SUB), :]
    skewed_t = acc_t[pl.ds(0, groups, stride=SUB), :]
    for r in range(1, SUB):
        turn = LANES - r
        skewed = skewed + pltpu.roll(acc[pl.ds(r, groups, stride=SUB), :], turn, 1)
        skewed_t = skewed_t + pltpu.roll(acc_t[pl.ds(r, groups, stride=SUB), :], turn, 1)
    skewed_t = pltpu.roll(skewed_t, half, 1)
    high = skewed.astype(BF16)
    rest = skewed - high.astype(F32)
    middle = rest.astype(BF16)
    low = (rest - middle.astype(F32)).astype(BF16)
    turned = jnp.dot(
        jnp.concatenate([high, middle, low], axis=0), flip.astype(BF16),
        preferred_element_type=F32,
    )
    by_group = skewed_t + turned[:groups, :]
    for n in range(1, 3):
        by_group = by_group + turned[n * groups : (n + 1) * groups, :]
    by_tap = by_group.T
    piece = rows // ctx_count
    for i in range(ctx_count):
        partial[i] = by_tap[i * piece : (i + 1) * piece, :]

    def gf_copy(step):
        peer = lax.rem(me + step, ctx_count)
        return pltpu.make_async_remote_copy(
            src_ref=partial.at[peer],
            dst_ref=gf_slots.at[step - 1],
            send_sem=gf_send.at[step - 1],
            recv_sem=gf_recv.at[step - 1],
            device_id={"ctx": peer},
            device_id_type=MESH,
        )

    @pl.loop(1, ctx_count)
    def _(step):
        gf_copy(step).start()

    @pl.when(has_prev)
    def _():
        carry_f_copy().wait_recv()

    @pl.loop(0, chunks // 4)
    def _(step):
        for c in range(4):
            finish(step * 4 + c)

    def add_slot(step, value):
        gf_copy(step).wait_recv()
        return value + gf_slots[step - 1]

    gf_ref[...] = lax.fori_loop(1, ctx_count, add_slot, partial[me])

    @pl.loop(1, ctx_count)
    def _(step):
        gf_copy(step).wait_send()

    if relays:
        for forward, by in ((True, 3), (False, 0)):

            @pl.when(me == by)
            def _():
                for part in range(1, halo_parts, 2):
                    onward_copy(part, forward).wait_send()

    @pl.when(has_prev)
    def _():
        carry_b_copy().wait_send()
        for part in range(halo_parts):
            halo_copy(part, False).wait_send()

    @pl.when(has_next)
    def _():
        carry_f_copy().wait_send()
        for part in range(halo_parts):
            halo_copy(part, True).wait_send()


def write_out(*refs):
    copies = [
        pltpu.make_async_copy(refs[n], refs[3 + n], refs[6].at[n]) for n in range(3)
    ]
    for one in copies:
        one.start()
    for one in copies:
        one.wait()


def short_call(args, ctx_count):
    rows, width = args[1].shape
    taps, groups = args[3].shape
    halo_parts = HALO_PARTS
    half = rows // 2
    vmem = pl.BlockSpec(memory_space=pltpu.VMEM)
    hbm = pl.BlockSpec(memory_space=pltpu.HBM)
    dma = pltpu.SemaphoreType.DMA
    piece = taps // ctx_count
    pairs = LANES // (width // groups) // 2
    wide = lambda r, t: pltpu.VMEM((r, width), t)
    square = lambda n, t: pltpu.VMEM((n, LANES), t)
    keep = pltpu.with_memory_space_constraint
    args = [keep(x, pltpu.HBM) for x in args]
    results = pl.pallas_call(
        functools.partial(short_kernel, ctx_count, halo_parts),
        out_shape=(
            pltpu.VMEM((rows, width), BF16),
            pltpu.VMEM((rows, width), BF16),
            pltpu.VMEM((piece, groups), F32),
        ),
        in_specs=[pl.BlockSpec(memory_space=pltpu.SMEM)] + [hbm] * 2 + [vmem] * 3 + [hbm] * 2,
        out_specs=(vmem, vmem, vmem),
        scratch_shapes=[
            wide(rows, BF16), wide(rows, BF16), wide(rows, BF16), wide(rows, BF16), dma((4,)),
            wide(rows, BF16), wide(rows, BF16),
            wide(half, BF16), wide(half, BF16), wide(half, BF16), wide(half, BF16),
            wide(half, BF16),
            wide(rows, F32), wide(rows, F32),
            square(groups * rows, BF16), square(groups * rows, BF16),
            wide(1, F32), pltpu.VMEM((groups, taps), F32), pltpu.VMEM((groups, taps), F32),
            square(rows, BF16), square(rows, BF16), square(rows, F32),
            pltpu.VMEM((11, rows, LANES), F32),
            square(2 * rows, BF16), pltpu.VMEM((pairs, rows, LANES), BF16),
            square(2 * rows, BF16), square(2 * rows, BF16),
            pltpu.VMEM((rows, 2 * LANES), BF16), pltpu.VMEM((rows, 2 * LANES), BF16),
            pltpu.VMEM((rows, 2 * LANES), BF16),
            square(2 * rows, BF16), square(2 * rows, BF16),
            square(width, BF16), square(width, BF16),
            square(SUB * groups, F32), square(SUB * groups, F32),
            pltpu.VMEM((ctx_count, piece, groups), F32),
            pltpu.VMEM((ctx_count - 1, piece, groups), F32),
            wide(1, F32), wide(1, F32), wide(1, F32), wide(1, F32),
            dma((halo_parts,)), dma((halo_parts,)), dma((halo_parts,)), dma((halo_parts,)),
            dma((1,)), dma((1,)), dma((1,)), dma((1,)),
            dma((halo_parts,)), dma((halo_parts,)),
            dma((ctx_count - 1,)), dma((ctx_count - 1,)),
        ],
        compiler_params=pltpu.CompilerParams(
            collective_id=1, has_side_effects=True, vmem_limit_bytes=48 * 1024 * 1024
        ),
        name="hyena_mixers_short",
    )(*args)
    return pl.pallas_call(
        write_out,
        out_shape=tuple(jax.ShapeDtypeStruct(x.shape, x.dtype) for x in results),
        in_specs=[vmem] * 3,
        out_specs=(hbm,) * 3,
        scratch_shapes=[dma((3,))],
        name="write_out",
    )(*[keep(x, pltpu.VMEM) for x in results])


def on_device(k_short, v_short, mr_filter, li_rate, li_residue, gate_out, contig_lengths, grad_out):
    rows, width = k_short.shape
    taps, groups = mr_filter.shape
    ctx_count = lax.axis_size("ctx")
    total = rows * ctx_count
    reach = min(ctx_count - 1, -(-(total // 4) // rows))
    args = (
        contig_lengths, k_short, v_short, mr_filter, li_rate[None], li_residue[None],
        gate_out, grad_out,
    )
    if total // 4 <= rows == taps == LANES:
        return short_call(args, ctx_count)
    halo_parts = 4
    vmem = pl.BlockSpec(memory_space=pltpu.VMEM)
    dma = pltpu.SemaphoreType.DMA
    piece = taps // ctx_count
    return pl.pallas_call(
        functools.partial(kernel, ctx_count, reach, halo_parts),
        out_shape=(
            jax.ShapeDtypeStruct((rows, width), BF16),
            jax.ShapeDtypeStruct((rows, width), BF16),
            jax.ShapeDtypeStruct((piece, groups), F32),
        ),
        in_specs=[pl.BlockSpec(memory_space=pltpu.SMEM)] + [vmem] * 7,
        out_specs=(vmem, vmem, vmem),
        scratch_shapes=[
            pltpu.VMEM((2 * rows, width), BF16),
            pltpu.VMEM((2 * rows, width), BF16),
            pltpu.VMEM((rows, width), F32),
            pltpu.VMEM((rows, width), F32),
            pltpu.VMEM((1, width), F32),
            pltpu.VMEM((groups, taps), F32),
            pltpu.VMEM((groups, taps), F32),
            pltpu.VMEM((rows, 2 * LANES), BF16),
            pltpu.VMEM((rows, 2 * LANES), BF16),
            pltpu.VMEM((rows, LANES), F32),
            pltpu.VMEM((10, rows, LANES), F32),
            pltpu.VMEM((SUB * groups, taps), F32),
            pltpu.VMEM((ctx_count, piece, groups), F32),
            pltpu.VMEM((ctx_count - 1, piece, groups), F32),
            pltpu.VMEM((1, width), F32),
            pltpu.VMEM((1, width), F32),
            pltpu.VMEM((reach, 1, width), F32),
            pltpu.VMEM((reach, 1, width), F32),
            dma((halo_parts,)), dma((halo_parts,)), dma((halo_parts,)), dma((halo_parts,)),
            dma((reach,)), dma((reach,)), dma((reach,)), dma((reach,)),
            dma((ctx_count - 1,)), dma((ctx_count - 1,)),
        ],
        compiler_params=pltpu.CompilerParams(collective_id=0, has_side_effects=True),
        name="hyena_mixers",
    )(*args)


def solution(mesh):
    in_specs = (
        P(("dp", "ctx"), "tp"),
        P(("dp", "ctx"), "tp"),
        P(None, "tp"),
        P("tp"),
        P("tp"),
        P(("dp", "ctx"), "tp"),
        P("dp"),
        P(("dp", "ctx"), "tp"),
    )
    out_specs = (P(("dp", "ctx"), "tp"), P(("dp", "ctx"), "tp"), P(("dp", "ctx"), "tp"))
    return jax.shard_map(
        on_device, mesh=mesh, in_specs=in_specs, out_specs=out_specs, check_vma=False
    )
```

```python
import functools

import jax
import jax.numpy as jnp
from jax import lax
from jax.experimental import pallas as pl
from jax.experimental.pallas import tpu as pltpu
from jax.sharding import PartitionSpec as P

MESH = pl.DeviceIdType.MESH
LANES = 128
SUB = 8
HALO_PARTS = 8
F32 = jnp.float32
BF16 = jnp.bfloat16


def seg_of(lengths_ref, places, total):
    offset = jnp.int32(0)
    seg = jnp.zeros(places.shape, jnp.int32)
    for i in range(lengths_ref.shape[0]):
        seg = seg + (places >= offset).astype(jnp.int32)
        offset = offset + lengths_ref[i]
    return seg + (places >= total).astype(jnp.int32)


def one_minus_exp(x):
    series = jnp.ones_like(x)
    for n in range(9, 1, -1):
        series = 1.0 - x / n * series
    return jnp.where(x < 0.5, x * series, 1.0 - jnp.exp(-x))


def kernel(
    ctx_count, reach, halo_parts,
    lengths, k_ref, v_ref, filt_ref, rate_ref, residue_ref, gate_ref, gout_ref,
    mixed_ref, gv_ref, gf_ref,
    u_ext, g_ext, adj, state, scale, taps, taps_rev, mask_f, mask_b, diag_seg,
    scan_masks, acc, partial, gf_slots, carry_f, carry_b, carry_f_in, carry_b_in,
    u_send, u_recv, g_send, g_recv, cf_send, cf_recv, cb_send, cb_recv, gf_send, gf_recv,
):
    rows, width = k_ref.shape
    groups = filt_ref.shape[1]
    per_group = width // groups
    per_chunk = LANES // per_group
    chunks = width // LANES
    part_width = width // halo_parts
    total = rows * ctx_count
    me = lax.axis_index("ctx")
    first = me * rows

    barrier = pltpu.get_barrier_semaphore()

    @pl.loop(1, ctx_count)
    def _(step):
        pl.semaphore_signal(
            barrier, inc=1, device_id={"ctx": lax.rem(me + step, ctx_count)}, device_id_type=MESH
        )

    pl.semaphore_wait(barrier, ctx_count - 1)

    def u_copy(part):
        cols = pl.ds(part * part_width, part_width)
        return pltpu.make_async_remote_copy(
            src_ref=u_ext.at[pl.ds(rows, rows), cols],
            dst_ref=u_ext.at[pl.ds(0, rows), cols],
            send_sem=u_send.at[part],
            recv_sem=u_recv.at[part],
            device_id={"ctx": lax.rem(me + 1, ctx_count)},
            device_id_type=MESH,
        )

    def g_copy(part):
        cols = pl.ds(part * part_width, part_width)
        return pltpu.make_async_remote_copy(
            src_ref=g_ext.at[pl.ds(0, rows), cols],
            dst_ref=g_ext.at[pl.ds(rows, rows), cols],
            send_sem=g_send.at[part],
            recv_sem=g_recv.at[part],
            device_id={"ctx": lax.rem(me + ctx_count - 1, ctx_count)},
            device_id_type=MESH,
        )

    def carry_copy(k, forward):
        src, dst, send, recv = (
            (carry_f, carry_f_in, cf_send, cf_recv)
            if forward
            else (carry_b, carry_b_in, cb_send, cb_recv)
        )
        peer = me + 1 + k if forward else me + ctx_count - 1 - k
        return pltpu.make_async_remote_copy(
            src_ref=src,
            dst_ref=dst.at[k],
            send_sem=send.at[k],
            recv_sem=recv.at[k],
            device_id={"ctx": lax.rem(peer, ctx_count)},
            device_id_type=MESH,
        )

    for part in range(halo_parts):
        cols = slice(part * part_width, (part + 1) * part_width)
        u_ext[rows:, cols] = (k_ref[:, cols].astype(F32) * v_ref[:, cols].astype(F32)).astype(BF16)

        @pl.when(me < ctx_count - 1)
        def _():
            u_copy(part).start()

    @pl.when(me == 0)
    def _():
        u_ext[:rows, :] = jnp.zeros((rows, width), BF16)

    @pl.when(me == ctx_count - 1)
    def _():
        g_ext[rows:, :] = jnp.zeros((rows, width), BF16)

    rate_all = rate_ref[...]
    scale[...] = residue_ref[...] * jnp.sqrt(one_minus_exp(2.0 * rate_all))
    row = lax.broadcasted_iota(jnp.int32, (rows, LANES), 0)
    seg = seg_of(lengths, first + row, total)
    sub = lax.rem(row, SUB)
    tile = row - sub
    for i, k in enumerate((1, 2, 4)):
        same = (seg == pltpu.roll(seg, k, 0)) & (sub >= k)
        scan_masks[i] = same.astype(F32)
        same = (seg == pltpu.roll(seg, rows - k, 0)) & (sub + k < SUB)
        scan_masks[4 + i] = same.astype(F32)
    scan_masks[3] = (seg == seg_of(lengths, first + tile - 1, total)).astype(F32)
    scan_masks[7] = (seg == seg_of(lengths, first + tile + SUB, total)).astype(F32)
    lane_one = jnp.zeros((1, LANES), jnp.int32)
    seg_before = seg_of(lengths, first - 1 + lane_one, total)
    seg_after = seg_of(lengths, first + rows + lane_one, total)
    scan_masks[8] = (seg == seg_before).astype(F32)
    scan_masks[9] = (seg == seg_after).astype(F32)
    lane = lax.broadcasted_iota(jnp.int32, (rows, LANES), 1)
    lane_row = lax.broadcasted_iota(jnp.int32, (1, LANES), 1)
    seg_prev = seg_of(lengths, first - rows + lane_row, total)
    seg_here = seg_of(lengths, first + lane_row, total)
    seg_next = seg_of(lengths, first + rows + lane_row, total)
    f_left = ((seg == seg_prev) & (lane > row)).astype(F32)
    f_right = ((seg == seg_here) & (lane <= row)).astype(F32)
    mask_f[:, :LANES] = f_left.astype(BF16)
    mask_f[:, LANES:] = f_right.astype(BF16)
    diag_seg[...] = f_left + f_right
    mask_b[:, :LANES] = ((seg == seg_here) & (lane >= row)).astype(F32).astype(BF16)
    mask_b[:, LANES:] = ((seg == seg_next) & (lane < row)).astype(F32).astype(BF16)
    flip = (lax.rem(row + lane, LANES) == 0).astype(F32)
    eye = (row == lane).astype(F32)
    over_taps = (((0,), (0,)), ((), ()))
    filt = filt_ref[...]
    taps[...] = lax.dot_general(filt, eye.astype(BF16), over_taps, preferred_element_type=F32)
    taps_rev[...] = lax.dot_general(filt, flip.astype(BF16), over_taps, preferred_element_type=F32)

    sub8 = lax.broadcasted_iota(jnp.int32, (SUB, LANES), 0).astype(F32)
    tiles = rows // SUB

    def chunk_cols(q):
        return pl.ds(pl.multiple_of(q * LANES, LANES), LANES)

    def scan_tiles(values, rate, forward):
        base = 0 if forward else 4
        steps = [jnp.exp(-k * rate) for k in (1.0, 2.0, 4.0)]
        far = jnp.exp(-((sub8 + 1.0) if forward else (SUB - sub8)) * rate)
        out = [None] * tiles
        carry = None
        for n in range(tiles) if forward else reversed(range(tiles)):
            here = slice(n * SUB, (n + 1) * SUB)
            x = values[here, :]
            for i, k in enumerate((1, 2, 4)):
                shifted = pltpu.roll(x, k if forward else SUB - k, 0)
                x = x + steps[i] * scan_masks[base + i, here, :] * shifted
            if carry is not None:
                x = x + far * scan_masks[base + 3, here, :] * carry
            carry = x[SUB - 1 : SUB, :] if forward else x[0:1, :]
            out[n] = x
        return out, carry

    def carried(slots, cols, rate, forward):
        value = slots[0, :, cols]
        for k in range(1, reach):
            edge = first - 1 - rows * k if forward else first + rows + rows * k
            there = seg_of(lengths, edge + lane_one, total)
            same = (there == (seg_before if forward else seg_after)).astype(F32)
            value = value + slots[k, :, cols] * same * jnp.exp(-float(rows * k) * rate)
        return value

    @pl.loop(0, chunks, unroll=4)
    def _(q):
        cols = chunk_cols(q)
        rate = rate_ref[:, cols]
        long = (scale[:, cols] * gate_ref[:, cols].astype(F32) * gout_ref[:, cols].astype(F32))
        out, carry = scan_tiles(long.astype(BF16).astype(F32), rate, False)
        for n in range(tiles):
            adj[n * SUB : (n + 1) * SUB, cols] = out[n]
        carry_b[:, cols] = carry

    for k in range(reach):

        @pl.when(me >= 1 + k)
        def _():
            carry_copy(k, False).start()

        @pl.when(me + 1 + k >= ctx_count)
        def _():
            carry_b_in[k] = jnp.zeros((1, width), F32)

    for k in range(reach):

        @pl.when(me + 1 + k < ctx_count)
        def _():
            carry_copy(k, False).wait_recv()

    for part in range(halo_parts):
        per_part = chunks // halo_parts

        @pl.loop(part * per_part, (part + 1) * per_part, unroll=4)
        def _(q):
            cols = chunk_cols(q)
            rate = rate_ref[:, cols]
            value = carried(carry_b_in, cols, rate, False)
            far = jnp.exp(-(SUB - sub8) * rate)
            eighth = jnp.exp(-float(SUB) * rate)
            for n in reversed(range(tiles)):
                here = slice(n * SUB, (n + 1) * SUB)
                x = adj[here, cols] + far * scan_masks[9, here, :] * value
                adj[here, cols] = x
                value = value * eighth
            g_ext[:rows, cols] = adj[:, cols].astype(BF16)

        @pl.when(me > 0)
        def _():
            g_copy(part).start()

    def bands(tap_rows, mask):
        blocks = []
        for g in range(per_chunk):
            skew = pltpu.roll(
                jnp.broadcast_to(tap_rows[g : g + 1, :], (SUB, LANES)), 0, 1,
                stride=1, stride_axis=0,
            )
            circ = jnp.concatenate(
                [skew] + [pltpu.roll(skew, n * SUB, 1) for n in range(1, tiles)], axis=0
            ).astype(BF16)
            blocks.append(
                jnp.concatenate([circ * mask[:, :LANES], circ * mask[:, LANES:]], axis=1)
            )
        return jnp.concatenate(blocks, axis=0)

    group_of_lane = lane // per_group

    for part in range(halo_parts):

        @pl.when(me > 0)
        def _():
            u_copy(part).wait_recv()

        @pl.loop(part * per_part, (part + 1) * per_part, unroll=2)
        def _(q):
            cols = chunk_cols(q)
            window = u_ext[:, cols]
            grads = g_ext[:rows, cols]
            group_rows = pl.ds(pl.multiple_of(q * per_chunk, per_chunk), per_chunk)
            all_y = jnp.dot(
                bands(taps_rev[group_rows, :], mask_f), window,
                preferred_element_type=F32,
            )
            y = all_y[:rows, :]
            for g in range(1, per_chunk):
                y = jnp.where(group_of_lane == g, all_y[g * rows : (g + 1) * rows, :], y)
            own = jnp.concatenate(
                [jnp.where(group_of_lane == g, grads, jnp.zeros_like(grads)) for g in range(per_chunk)],
                axis=0,
            )
            all_prod = lax.dot_general(
                own, window, (((1,), (1,)), ((), ())), preferred_element_type=F32
            )
            for g in range(per_chunk):
                prod = all_prod[g * rows : (g + 1) * rows, :]
                prod = jnp.where(lane <= row, prod[:, LANES:], prod[:, :LANES]) * diag_seg[...]
                folded = prod[:SUB, :]
                for n in range(1, tiles):
                    folded = folded + pltpu.roll(
                        prod[n * SUB : (n + 1) * SUB, :], LANES - n * SUB, 1
                    )
                acc[pl.ds(pl.multiple_of((q * per_chunk + g) * SUB, SUB), SUB), :] = folded
            out, carry = scan_tiles(y.astype(BF16).astype(F32), rate_ref[:, cols], True)
            for n in range(tiles):
                state[n * SUB : (n + 1) * SUB, cols] = out[n]
            carry_f[:, cols] = carry

    for k in range(reach):

        @pl.when(me + 1 + k < ctx_count)
        def _():
            carry_copy(k, True).start()

        @pl.when(me < 1 + k)
        def _():
            carry_f_in[k] = jnp.zeros((1, width), F32)

    skewed = acc[pl.ds(0, groups, stride=SUB), :]
    for r in range(1, SUB):
        skewed = skewed + pltpu.roll(acc[pl.ds(r, groups, stride=SUB), :], LANES - r, 1)
    by_tap = lax.dot_general(
        flip, skewed, (((1,), (1,)), ((), ())),
        precision=lax.Precision.HIGHEST, preferred_element_type=F32,
    )
    piece = rows // ctx_count
    for i in range(ctx_count):
        partial[i] = by_tap[i * piece : (i + 1) * piece, :]

    def gf_copy(step):
        peer = lax.rem(me + step, ctx_count)
        return pltpu.make_async_remote_copy(
            src_ref=partial.at[peer],
            dst_ref=gf_slots.at[step - 1],
            send_sem=gf_send.at[step - 1],
            recv_sem=gf_recv.at[step - 1],
            device_id={"ctx": peer},
            device_id_type=MESH,
        )

    @pl.loop(1, ctx_count)
    def _(step):
        gf_copy(step).start()

    def finish_forward():
        for k in range(reach):

            @pl.when(me >= 1 + k)
            def _():
                carry_copy(k, True).wait_recv()

        @pl.loop(0, chunks, unroll=4)
        def _(q):
            cols = chunk_cols(q)
            rate = rate_ref[:, cols]
            value = carried(carry_f_in, cols, rate, True)
            far = jnp.exp(-(sub8 + 1.0) * rate)
            eighth = jnp.exp(-float(SUB) * rate)
            for n in range(tiles):
                here = slice(n * SUB, (n + 1) * SUB)
                x = state[here, cols] + far * scan_masks[8, here, :] * value
                state[here, cols] = x
                value = value * eighth
            z_long = (scale[:, cols] * state[:, cols]).astype(BF16)
            mixed_ref[:, cols] = (gate_ref[:, cols].astype(F32) * z_long.astype(F32)).astype(BF16)

    for part in range(halo_parts):

        @pl.when(me < ctx_count - 1)
        def _():
            g_copy(part).wait_recv()

        @pl.loop(part * per_part, (part + 1) * per_part, unroll=2)
        def _(q):
            cols = chunk_cols(q)
            window = g_ext[:, cols]
            group_rows = pl.ds(pl.multiple_of(q * per_chunk, per_chunk), per_chunk)
            all_u = jnp.dot(
                bands(taps[group_rows, :], mask_b), window,
                preferred_element_type=F32,
            )
            grad_u = all_u[:rows, :]
            for g in range(1, per_chunk):
                grad_u = jnp.where(group_of_lane == g, all_u[g * rows : (g + 1) * rows, :], grad_u)
            gv_ref[:, cols] = (k_ref[:, cols].astype(F32) * grad_u).astype(BF16)

        if part == (halo_parts - 1) // 2:
            finish_forward()

    own = partial[me]

    def add_slot(step, value):
        gf_copy(step).wait_recv()
        return value + gf_slots[step - 1]

    gf_ref[...] = lax.fori_loop(1, ctx_count, add_slot, own)

    @pl.loop(1, ctx_count)
    def _(step):
        gf_copy(step).wait_send()

    for k in range(reach):

        @pl.when(me >= 1 + k)
        def _():
            carry_copy(k, False).wait_send()

        @pl.when(me + 1 + k < ctx_count)
        def _():
            carry_copy(k, True).wait_send()

    for part in range(halo_parts):

        @pl.when(me < ctx_count - 1)
        def _():
            u_copy(part).wait_send()

        @pl.when(me > 0)
        def _():
            g_copy(part).wait_send()


def crossing(lengths_ref, edge):
    offset = jnp.int32(0)
    before = jnp.int32(0)
    after = jnp.int32(0)
    for i in range(lengths_ref.shape[0]):
        end = offset + lengths_ref[i]
        inside = (offset < edge) & (end > edge)
        before = jnp.where(inside, edge - offset, before)
        after = jnp.where(inside, end - edge, after)
        offset = end
    return before, after


def short_kernel(
    ctx_count, halo_parts,
    lengths, k_hbm, v_hbm, filt_ref, rate_ref, residue_ref, gate_hbm, gout_hbm,
    mixed_ref, gv_ref, gf_ref,
    k_ref, v_ref, gate_ref, gout_ref, load,
    u_own, g_own, u_out, g_out, u_in, g_in, relay, adj, y_own, circ_f, circ_b,
    scale, taps, taps_rev, mask_f, mask_b, diag_seg, scan_masks, even_odd, pair_lanes,
    right_rows, left_rows, even_odd_t, left_t, right_t, quad_u, quad_g, u_t, g_t, acc, acc_t, partial, gf_slots,
    carry_f, carry_b, carry_f_in, carry_b_in,
    u_send, u_recv, g_send, g_recv, cf_send, cf_recv, cb_send, cb_recv,
    relay_send, relay_recv, gf_send, gf_recv,
):
    rows, width = k_ref.shape
    groups = filt_ref.shape[1]
    half = rows // 2
    per_group = width // groups
    per_chunk = LANES // per_group
    pairs = per_chunk // 2
    chunks = width // LANES
    per_part = chunks // halo_parts
    part_width = width // halo_parts
    total = rows * ctx_count
    tiles = rows // SUB
    me = lax.axis_index("ctx")
    first = me * rows
    has_next = me < ctx_count - 1
    has_prev = me > 0

    loads = [
        pltpu.make_async_copy(src, dst, load.at[n])
        for n, (src, dst) in enumerate(
            ((gate_hbm, gate_ref), (gout_hbm, gout_ref), (k_hbm, k_ref), (v_hbm, v_ref))
        )
    ]
    for one in loads:
        one.start()

    barrier = pltpu.get_barrier_semaphore()

    @pl.loop(1, ctx_count)
    def _(step):
        pl.semaphore_signal(
            barrier, inc=1, device_id={"ctx": lax.rem(me + step, ctx_count)}, device_id_type=MESH
        )

    def halo_copy(part, forward):
        src, dst, send, recv = (
            (u_out, u_in, u_send, u_recv) if forward else (g_out, g_in, g_send, g_recv)
        )
        cols = pl.ds(pl.multiple_of(part * part_width, LANES), part_width)
        peer = me + 1 if forward else me + ctx_count - 1
        return pltpu.make_async_remote_copy(
            src_ref=src.at[:, cols],
            dst_ref=dst.at[:, cols],
            send_sem=send.at[part],
            recv_sem=recv.at[part],
            device_id={"ctx": lax.rem(peer, ctx_count)},
            device_id_type=MESH,
        )

    def carry_b_copy():
        return pltpu.make_async_remote_copy(
            src_ref=carry_b,
            dst_ref=carry_b_in,
            send_sem=cb_send.at[0],
            recv_sem=cb_recv.at[0],
            device_id={"ctx": lax.rem(me + ctx_count - 1, ctx_count)},
            device_id_type=MESH,
        )

    def carry_f_copy():
        return pltpu.make_async_remote_copy(
            src_ref=carry_f,
            dst_ref=carry_f_in,
            send_sem=cf_send.at[0],
            recv_sem=cf_recv.at[0],
            device_id={"ctx": lax.rem(me + 1, ctx_count)},
            device_id_type=MESH,
        )

    relays = ctx_count == 4

    def relay_copy(part, forward):
        cols = pl.ds(pl.multiple_of(part * part_width, LANES), part_width)
        src, send = (u_out, u_send) if forward else (g_out, g_send)
        return pltpu.make_async_remote_copy(
            src_ref=src.at[:, cols],
            dst_ref=relay.at[:, cols],
            send_sem=send.at[part],
            recv_sem=relay_recv.at[part],
            device_id={"ctx": 3 if forward else 0},
            device_id_type=MESH,
        )

    def onward_copy(part, forward):
        cols = pl.ds(pl.multiple_of(part * part_width, LANES), part_width)
        dst, recv = (u_in, u_recv) if forward else (g_in, g_recv)
        return pltpu.make_async_remote_copy(
            src_ref=relay.at[:, cols],
            dst_ref=dst.at[:, cols],
            send_sem=relay_send.at[part],
            recv_sem=recv.at[part],
            device_id={"ctx": 2 if forward else 1},
            device_id_type=MESH,
        )

    @pl.when(jnp.logical_not(has_prev))
    def _():
        u_in[...] = jnp.zeros(u_in.shape, BF16)
        carry_f_in[...] = jnp.zeros(carry_f_in.shape, F32)

    @pl.when(jnp.logical_not(has_next))
    def _():
        g_in[...] = jnp.zeros(g_in.shape, BF16)
        carry_b_in[...] = jnp.zeros(carry_b_in.shape, F32)

    left_a, left_b = crossing(lengths, first)
    right_a, right_b = crossing(lengths, first + rows)

    rate_all = rate_ref[...]
    scale[...] = residue_ref[...] * jnp.sqrt(one_minus_exp(2.0 * rate_all))
    row = lax.broadcasted_iota(jnp.int32, (rows, LANES), 0)
    lane = lax.broadcasted_iota(jnp.int32, (rows, LANES), 1)
    lane_row = lax.broadcasted_iota(jnp.int32, (1, LANES), 1)
    row_half = lax.broadcasted_iota(jnp.int32, (half, LANES), 0)
    lane_half = lax.broadcasted_iota(jnp.int32, (half, LANES), 1)
    seg = seg_of(lengths, first + row, total)
    sub = lax.rem(row, SUB)
    tile = row - sub
    for i, k in enumerate((1, 2, 4)):
        same = (seg == pltpu.roll(seg, rows - k, 0)) & (sub + k < SUB)
        scan_masks[4 + i] = same.astype(F32)
    scan_masks[7] = (seg == seg_of(lengths, first + tile + SUB, total)).astype(F32)
    lane_one = jnp.zeros((1, LANES), jnp.int32)
    scan_masks[10] = (seg == seg_of(lengths, first + lane_one, total)).astype(F32)
    group_of_lane = lane // per_group
    pair_of_lane = group_of_lane // 2
    send_u = right_a <= half
    send_gpart = left_a <= half
    for e in range(2):
        lanes = lax.rem(group_of_lane, 2) == e
        right_rows[e * rows : (e + 1) * rows, :] = (
            (lanes & (row >= rows - right_a)).astype(F32).astype(BF16)
        )
        left_rows[e * rows : (e + 1) * rows, :] = (
            (lanes & (row < left_b)).astype(F32).astype(BF16)
        )
    flip = (lax.rem(row + lane, LANES) == 0).astype(F32)
    eye = (row == lane).astype(F32)
    over_taps = (((0,), (0,)), ((), ()))
    filt = filt_ref[...]
    taps[...] = lax.dot_general(filt, eye.astype(BF16), over_taps, preferred_element_type=F32)
    taps_rev[...] = lax.dot_general(filt, flip.astype(BF16), over_taps, preferred_element_type=F32)
    sub8 = lax.broadcasted_iota(jnp.int32, (SUB, LANES), 0).astype(F32)

    def chunk_cols(q):
        return pl.ds(pl.multiple_of(q * LANES, LANES), LANES)

    def group_rows(q, g):
        return pl.ds(pl.multiple_of((q * per_chunk + g) * rows, rows), rows)

    def scan_tiles(values, rate, forward, carry=None):
        base = 0 if forward else 4
        steps = [jnp.exp(-k * rate) for k in (1.0, 2.0, 4.0)]
        far = jnp.exp(-((sub8 + 1.0) if forward else (SUB - sub8)) * rate)
        out = [None] * tiles
        for n in range(tiles) if forward else reversed(range(tiles)):
            here = slice(n * SUB, (n + 1) * SUB)
            x = values[here, :]
            for i, k in enumerate((1, 2, 4)):
                shifted = pltpu.roll(x, k if forward else SUB - k, 0)
                x = x + steps[i] * scan_masks[base + i, here, :] * shifted
            if carry is not None:
                x = x + far * scan_masks[base + 3, here, :] * carry
            carry = x[SUB - 1 : SUB, :] if forward else x[0:1, :]
            out[n] = x
        return out, carry

    def circulant(tap_rows, g):
        skew = pltpu.roll(
            jnp.broadcast_to(tap_rows[g : g + 1, :], (2 * SUB, LANES)), 0, 1,
            stride=1, stride_axis=0,
        ).astype(BF16)
        return jnp.concatenate(
            [skew] + [pltpu.roll(skew, 2 * n * SUB, 1) for n in range(1, tiles // 2)], axis=0
        )

    def pick(outs, n_rows, index):
        value = outs[:n_rows, :]
        for p in range(1, outs.shape[0] // n_rows):
            value = jnp.where(index == p, outs[p * n_rows : (p + 1) * n_rows, :], value)
        return value

    def beside(x):
        return jnp.concatenate([x, x], axis=1)

    def twice(x):
        return jnp.concatenate([x, x], axis=0)

    def fold(prod):
        folded = prod[:SUB, :]
        for n in range(1, prod.shape[0] // SUB):
            folded = folded + pltpu.roll(prod[n * SUB : (n + 1) * SUB, :], LANES - n * SUB, 1)
        return folded

    pair_half = lane_half // (2 * per_group)
    across = (((1,), (1,)), ((), ()))

    for one in loads[:2]:
        one.wait()

    @pl.loop(0, chunks // 4)
    def _(step):
        for c in range(4):
            cols = chunk_cols(step * 4 + c)
            rate = rate_ref[:, cols]
            long = scale[:, cols] * gate_ref[:, cols].astype(F32) * gout_ref[:, cols].astype(F32)
            long = long.astype(BF16).astype(F32) * scan_masks[10]
            eighth = jnp.exp(-float(SUB) * rate)
            run = long[rows - SUB :, :]
            for n in reversed(range(tiles - 1)):
                run = run * eighth + long[n * SUB : (n + 1) * SUB, :]
            carry_b[:, cols] = jnp.sum(run * jnp.exp(-sub8 * rate), axis=0, keepdims=True)

    pl.semaphore_wait(barrier, ctx_count - 1)

    for one in loads[2:]:
        one.wait()

    @pl.when(has_prev)
    def _():
        carry_b_copy().start()

    def join(xs):
        return jnp.concatenate(
            [jnp.concatenate(xs[2 * p : 2 * p + 2], axis=1) for p in range(pairs)], axis=0
        )

    def pair_bands(circ, q, mask):
        return jnp.concatenate(
            [
                jnp.concatenate(
                    [circ[group_rows(q, 2 * p + e), :] * mask for e in range(2)], axis=1
                )
                for p in range(pairs)
            ],
            axis=0,
        )

    def own_y(q):
        cols = chunk_cols(q)
        rate = rate_ref[:, cols]
        y = jnp.dot(
            pair_bands(circ_f, q, mask_f[...]), twice(u_own[:, cols]) * even_odd[...],
            preferred_element_type=F32,
        )
        y = pick(y, rows, pair_of_lane)
        y_own[:, cols] = y
        last = y.astype(BF16).astype(F32) * scan_masks[8]
        eighth = jnp.exp(-float(SUB) * rate)
        run = last[:SUB, :]
        for n in range(1, tiles):
            run = run * eighth + last[n * SUB : (n + 1) * SUB, :]
        carry_f[:, cols] = jnp.sum(
            run * jnp.exp(-(SUB - 1.0 - sub8) * rate), axis=0, keepdims=True
        )

    @pl.loop(0, halo_parts)
    def _(part):
        for c in range(per_part):
            q = part * per_part + c
            cols = chunk_cols(q)
            u = (k_ref[:, cols].astype(F32) * v_ref[:, cols].astype(F32)).astype(BF16)
            u_own[:, cols] = u
            long = scale[:, cols] * gate_ref[:, cols].astype(F32) * gout_ref[:, cols].astype(F32)
            out, _ = scan_tiles(long.astype(BF16).astype(F32), rate_ref[:, cols], False)
            for n in range(tiles):
                adj[n * SUB : (n + 1) * SUB, cols] = out[n]
            g = jnp.concatenate(out, axis=0).astype(BF16)
            tap_rows = pl.ds(pl.multiple_of(q * per_chunk, per_chunk), per_chunk)
            f_rows, b_rows = taps_rev[tap_rows, :], taps[tap_rows, :]
            top, bottom = [], []
            for i in range(per_chunk):
                f, b = circulant(f_rows, i), circulant(b_rows, i)
                circ_f[group_rows(q, i), :] = f
                circ_b[group_rows(q, i), :] = b
                top.append(f[:half, :])
                bottom.append(b[half:, :])
            y_part = jnp.dot(join(top), twice(u) * right_rows[...], preferred_element_type=F32)
            y_part = pick(y_part, half, pair_half)
            g_part = jnp.dot(join(bottom), twice(g) * left_rows[...], preferred_element_type=F32)
            g_part = pick(g_part, half, pair_half)
            y_part = jnp.where(row_half < right_b, y_part, 0.0)
            g_part = jnp.where(row_half >= half - left_a, g_part, 0.0)
            u_tail = jnp.where(row_half >= half - right_a, u[half:, :].astype(F32), 0.0)
            g_head = jnp.where(row_half < left_b, g[:half, :].astype(F32), 0.0)
            u_out[:, cols] = jnp.where(send_u, u_tail, y_part).astype(BF16)
            g_out[:, cols] = jnp.where(send_gpart, g_part, g_head).astype(BF16)

        by_relay = lax.rem(part, 2) == 1 if relays else False

        @pl.when(has_next)
        def _():
            if relays:
                pl.when((me == 1) & by_relay)(lambda: relay_copy(part, True).start())
                pl.when((me != 1) | jnp.logical_not(by_relay))(
                    lambda: halo_copy(part, True).start()
                )
            else:
                halo_copy(part, True).start()

        @pl.when(has_prev)
        def _():
            if relays:
                pl.when((me == 2) & by_relay)(lambda: relay_copy(part, False).start())
                pl.when((me != 2) | jnp.logical_not(by_relay))(
                    lambda: halo_copy(part, False).start()
                )
            else:
                halo_copy(part, False).start()

    def own_terms(q):
        cols = chunk_cols(q)
        rate = rate_ref[:, cols]
        value = carry_b_in[:, cols]
        far = jnp.exp(-(SUB - sub8) * rate)
        eighth = jnp.exp(-float(SUB) * rate)
        out = [None] * tiles
        for n in reversed(range(tiles)):
            here = slice(n * SUB, (n + 1) * SUB)
            out[n] = adj[here, cols] + far * scan_masks[9, here, :] * value
            value = value * eighth
        g = jnp.concatenate(out, axis=0).astype(BF16)
        g_own[:, cols] = g
        by_pair = jnp.concatenate([g * pair_lanes[p] for p in range(pairs)], axis=0)
        ut, gt = u_own[:, cols].T, g.T
        t_rows = pl.ds(pl.multiple_of(q * LANES, LANES), LANES)
        u_t[t_rows, :] = ut
        g_t[t_rows, :] = gt
        prods = jnp.dot(by_pair, beside(ut) * even_odd_t[...], preferred_element_type=F32)
        for p in range(pairs):
            for e in range(2):
                prod = prods[p * rows : (p + 1) * rows, e * LANES : (e + 1) * LANES]
                at = pl.multiple_of((q * per_chunk + 2 * p + e) * SUB, SUB)
                acc[pl.ds(at, SUB), :] = fold(prod * diag_seg[...])

    seg = seg_of(lengths, first + row, total)
    for i, k in enumerate((1, 2, 4)):
        same = (seg == pltpu.roll(seg, k, 0)) & (sub >= k)
        scan_masks[i] = same.astype(F32)
    scan_masks[3] = (seg == seg_of(lengths, first + tile - 1, total)).astype(F32)
    lane_one = jnp.zeros((1, LANES), jnp.int32)
    scan_masks[8] = (seg == seg_of(lengths, first + rows - 1 + lane_one, total)).astype(F32)
    scan_masks[9] = (seg == seg_of(lengths, first + rows + lane_one, total)).astype(F32)
    seg_here = seg_of(lengths, first + lane_row, total)
    own = ((seg == seg_here) & (lane <= row)).astype(F32)
    mask_f[...] = own.astype(BF16)
    diag_seg[...] = own
    mask_b[...] = ((seg == seg_here) & (lane >= row)).astype(F32).astype(BF16)
    for e in range(2):
        even_odd[e * rows : (e + 1) * rows, :] = (
            (lax.rem(group_of_lane, 2) == e).astype(F32).astype(BF16)
        )
    group_of_row = row // per_group
    for e in range(2):
        rows_e = lax.rem(group_of_row, 2) == e
        at = slice(e * LANES, (e + 1) * LANES)
        even_odd_t[:, at] = rows_e.astype(F32).astype(BF16)
        left_t[:, at] = jnp.where(
            send_gpart, (rows_e & (lane < left_b)).astype(F32), 0.0
        ).astype(BF16)
        right_t[:, at] = jnp.where(
            send_u, 0.0, (rows_e & (lane >= rows - right_a)).astype(F32)
        ).astype(BF16)
    for p in range(pairs):
        pair_lanes[p] = (pair_of_lane == p).astype(F32).astype(BF16)
    group_half = lane_half // per_group
    for e in range(4):
        lanes = lax.rem(group_half, 4) == e
        quad_u[e * half : (e + 1) * half, :] = (
            jnp.where(send_gpart, lanes.astype(F32), 0.0).astype(BF16)
        )
        quad_g[e * half : (e + 1) * half, :] = (
            jnp.where(send_u, 0.0, lanes.astype(F32)).astype(BF16)
        )

    @pl.when(has_next)
    def _():
        carry_b_copy().wait_recv()

    @pl.loop(0, chunks // 4)
    def _(step):
        if relays:
            for forward, by in ((True, 3), (False, 0)):

                @pl.when(me == by)
                def _():
                    relay_copy(2 * step + 1, forward).wait_recv()
                    onward_copy(2 * step + 1, forward).start()

        for c in range(4):
            own_terms(step * 4 + c)
            own_y(step * 4 + c)

    @pl.when(has_next)
    def _():
        carry_f_copy().start()

    low_lanes = lane < half

    def quad_bands(circ, q, forward):
        quads = []
        for g in range(0, per_chunk, 4):
            halves = []
            for e in (0, 2):
                one = circ[group_rows(q, g + e), :]
                two = circ[group_rows(q, g + e + 1), :]
                if forward:
                    one = jnp.concatenate([one[half:, :], one[:half, :]], axis=0)
                else:
                    two = jnp.concatenate([two[half:, :], two[:half, :]], axis=0)
                halves.append(jnp.where(low_lanes, one, two))
            quads.append(jnp.concatenate(halves, axis=1))
        return jnp.concatenate(quads, axis=0)

    def four(x):
        return jnp.concatenate([x, x, x, x], axis=0)

    quad_of_lane = lane // (4 * per_group)

    def cross_terms(q):
        cols = chunk_cols(q)
        u_msg, g_msg = u_in[:, cols], g_in[:, cols]
        t_rows = pl.ds(pl.multiple_of(q * LANES, LANES), LANES)
        lhs = jnp.concatenate([u_msg * pair_lanes[p, :half, :] for p in range(pairs)], axis=0)
        prods = jnp.dot(lhs, beside(g_t[t_rows, :]) * left_t[...], preferred_element_type=F32)
        lhs = jnp.concatenate([g_msg * pair_lanes[p, :half, :] for p in range(pairs)], axis=0)
        prods2 = jnp.dot(lhs, beside(u_t[t_rows, :]) * right_t[...], preferred_element_type=F32)
        for p in range(pairs):
            for e in range(2):
                at = pl.ds(pl.multiple_of((q * per_chunk + 2 * p + e) * SUB, SUB), SUB)
                cut = (slice(p * half, (p + 1) * half), slice(e * LANES, (e + 1) * LANES))
                acc_t[at, :] = fold(prods[cut])
                acc[at, :] = acc[at, :] + fold(prods2[cut])

    def finish(q):
        cols = chunk_cols(q)
        u_msg, g_msg = u_in[:, cols], g_in[:, cols]
        rate = rate_ref[:, cols]
        y = jnp.dot(
            quad_bands(circ_f, q, True), four(u_msg) * quad_u[...], preferred_element_type=F32
        )
        y = pick(y, rows, quad_of_lane)
        y_part = jnp.where(send_gpart, 0.0, u_msg.astype(F32))
        y = y + jnp.concatenate([y_part, jnp.zeros_like(y_part)], axis=0)
        y = y_own[:, cols] + jnp.where(row < left_b, y, 0.0)
        out, _ = scan_tiles(
            y.astype(BF16).astype(F32), rate, True, carry_f_in[:, cols]
        )
        z_long = (scale[:, cols] * jnp.concatenate(out, axis=0)).astype(BF16)
        mixed_ref[:, cols] = (gate_ref[:, cols].astype(F32) * z_long.astype(F32)).astype(BF16)
        gu = jnp.dot(
            quad_bands(circ_b, q, False), four(g_msg) * quad_g[...], preferred_element_type=F32
        )
        gu = pick(gu, rows, quad_of_lane)
        g_part = jnp.where(send_u, g_msg.astype(F32), 0.0)
        gu = gu + jnp.concatenate([jnp.zeros_like(g_part), g_part], axis=0)
        own = jnp.dot(
            pair_bands(circ_b, q, mask_b[...]), twice(g_own[:, cols]) * even_odd[...],
            preferred_element_type=F32,
        )
        gu = pick(own, rows, pair_of_lane) + jnp.where(row >= rows - right_a, gu, 0.0)
        gv_ref[:, cols] = (k_ref[:, cols].astype(F32) * gu).astype(BF16)

    @pl.loop(0, chunks // 4)
    def _(step):
        @pl.when(has_prev)
        def _():
            for n in range(2):
                halo_copy(step * 2 + n, True).wait_recv()

        @pl.when(has_next)
        def _():
            for n in range(2):
                halo_copy(step * 2 + n, False).wait_recv()

        for c in range(4):
            cross_terms(step * 4 + c)

    skewed = acc[pl.ds(0, groups, stride=SUB), :]
    skewed_t = acc_t[pl.ds(0, groups, stride=SUB), :]
    for r in range(1, SUB):
        turn = LANES - r
        skewed = skewed + pltpu.roll(acc[pl.ds(r, groups, stride=SUB), :], turn, 1)
        skewed_t = skewed_t + pltpu.roll(acc_t[pl.ds(r, groups, stride=SUB), :], turn, 1)
    skewed_t = pltpu.roll(skewed_t, half, 1)
    high = skewed.astype(BF16)
    rest = skewed - high.astype(F32)
    middle = rest.astype(BF16)
    low = (rest - middle.astype(F32)).astype(BF16)
    turned = jnp.dot(
        jnp.concatenate([high, middle, low], axis=0), flip.astype(BF16),
        preferred_element_type=F32,
    )
    by_group = skewed_t + turned[:groups, :]
    for n in range(1, 3):
        by_group = by_group + turned[n * groups : (n + 1) * groups, :]
    by_tap = by_group.T
    piece = rows // ctx_count
    for i in range(ctx_count):
        partial[i] = by_tap[i * piece : (i + 1) * piece, :]

    def gf_copy(step):
        peer = lax.rem(me + step, ctx_count)
        return pltpu.make_async_remote_copy(
            src_ref=partial.at[peer],
            dst_ref=gf_slots.at[step - 1],
            send_sem=gf_send.at[step - 1],
            recv_sem=gf_recv.at[step - 1],
            device_id={"ctx": peer},
            device_id_type=MESH,
        )

    @pl.loop(1, ctx_count)
    def _(step):
        gf_copy(step).start()

    @pl.when(has_prev)
    def _():
        carry_f_copy().wait_recv()

    @pl.loop(0, chunks // 4)
    def _(step):
        for c in range(4):
            finish(step * 4 + c)

    def add_slot(step, value):
        gf_copy(step).wait_recv()
        return value + gf_slots[step - 1]

    gf_ref[...] = lax.fori_loop(1, ctx_count, add_slot, partial[me])

    @pl.loop(1, ctx_count)
    def _(step):
        gf_copy(step).wait_send()

    if relays:
        for forward, by in ((True, 3), (False, 0)):

            @pl.when(me == by)
            def _():
                for part in range(1, halo_parts, 2):
                    onward_copy(part, forward).wait_send()

    @pl.when(has_prev)
    def _():
        carry_b_copy().wait_send()
        for part in range(halo_parts):
            halo_copy(part, False).wait_send()

    @pl.when(has_next)
    def _():
        carry_f_copy().wait_send()
        for part in range(halo_parts):
            halo_copy(part, True).wait_send()


def write_out(*refs):
    copies = [
        pltpu.make_async_copy(refs[n], refs[3 + n], refs[6].at[n]) for n in range(3)
    ]
    for one in copies:
        one.start()
    for one in copies:
        one.wait()


def short_call(args, ctx_count):
    rows, width = args[1].shape
    taps, groups = args[3].shape
    halo_parts = HALO_PARTS
    half = rows // 2
    vmem = pl.BlockSpec(memory_space=pltpu.VMEM)
    hbm = pl.BlockSpec(memory_space=pltpu.HBM)
    dma = pltpu.SemaphoreType.DMA
    piece = taps // ctx_count
    pairs = LANES // (width // groups) // 2
    wide = lambda r, t: pltpu.VMEM((r, width), t)
    square = lambda n, t: pltpu.VMEM((n, LANES), t)
    keep = pltpu.with_memory_space_constraint
    args = [keep(x, pltpu.HBM) for x in args]
    results = pl.pallas_call(
        functools.partial(short_kernel, ctx_count, halo_parts),
        out_shape=(
            pltpu.VMEM((rows, width), BF16),
            pltpu.VMEM((rows, width), BF16),
            pltpu.VMEM((piece, groups), F32),
        ),
        in_specs=[pl.BlockSpec(memory_space=pltpu.SMEM)] + [hbm] * 2 + [vmem] * 3 + [hbm] * 2,
        out_specs=(vmem, vmem, vmem),
        scratch_shapes=[
            wide(rows, BF16), wide(rows, BF16), wide(rows, BF16), wide(rows, BF16), dma((4,)),
            wide(rows, BF16), wide(rows, BF16),
            wide(half, BF16), wide(half, BF16), wide(half, BF16), wide(half, BF16),
            wide(half, BF16),
            wide(rows, F32), wide(rows, F32),
            square(groups * rows, BF16), square(groups * rows, BF16),
            wide(1, F32), pltpu.VMEM((groups, taps), F32), pltpu.VMEM((groups, taps), F32),
            square(rows, BF16), square(rows, BF16), square(rows, F32),
            pltpu.VMEM((11, rows, LANES), F32),
            square(2 * rows, BF16), pltpu.VMEM((pairs, rows, LANES), BF16),
            square(2 * rows, BF16), square(2 * rows, BF16),
            pltpu.VMEM((rows, 2 * LANES), BF16), pltpu.VMEM((rows, 2 * LANES), BF16),
            pltpu.VMEM((rows, 2 * LANES), BF16),
            square(2 * rows, BF16), square(2 * rows, BF16),
            square(width, BF16), square(width, BF16),
            square(SUB * groups, F32), square(SUB * groups, F32),
            pltpu.VMEM((ctx_count, piece, groups), F32),
            pltpu.VMEM((ctx_count - 1, piece, groups), F32),
            wide(1, F32), wide(1, F32), wide(1, F32), wide(1, F32),
            dma((halo_parts,)), dma((halo_parts,)), dma((halo_parts,)), dma((halo_parts,)),
            dma((1,)), dma((1,)), dma((1,)), dma((1,)),
            dma((halo_parts,)), dma((halo_parts,)),
            dma((ctx_count - 1,)), dma((ctx_count - 1,)),
        ],
        compiler_params=pltpu.CompilerParams(
            collective_id=1, has_side_effects=True, vmem_limit_bytes=48 * 1024 * 1024
        ),
        name="hyena_mixers_short",
    )(*args)
    return pl.pallas_call(
        write_out,
        out_shape=tuple(jax.ShapeDtypeStruct(x.shape, x.dtype) for x in results),
        in_specs=[vmem] * 3,
        out_specs=(hbm,) * 3,
        scratch_shapes=[dma((3,))],
        name="write_out",
    )(*[keep(x, pltpu.VMEM) for x in results])


def on_device(k_short, v_short, mr_filter, li_rate, li_residue, gate_out, contig_lengths, grad_out):
    rows, width = k_short.shape
    taps, groups = mr_filter.shape
    ctx_count = lax.axis_size("ctx")
    total = rows * ctx_count
    reach = min(ctx_count - 1, -(-(total // 4) // rows))
    args = (
        contig_lengths, k_short, v_short, mr_filter, li_rate[None], li_residue[None],
        gate_out, grad_out,
    )
    if total // 4 <= rows == taps == LANES:
        return short_call(args, ctx_count)
    halo_parts = 4
    vmem = pl.BlockSpec(memory_space=pltpu.VMEM)
    dma = pltpu.SemaphoreType.DMA
    piece = taps // ctx_count
    return pl.pallas_call(
        functools.partial(kernel, ctx_count, reach, halo_parts),
        out_shape=(
            jax.ShapeDtypeStruct((rows, width), BF16),
            jax.ShapeDtypeStruct((rows, width), BF16),
            jax.ShapeDtypeStruct((piece, groups), F32),
        ),
        in_specs=[pl.BlockSpec(memory_space=pltpu.SMEM)] + [vmem] * 7,
        out_specs=(vmem, vmem, vmem),
        scratch_shapes=[
            pltpu.VMEM((2 * rows, width), BF16),
            pltpu.VMEM((2 * rows, width), BF16),
            pltpu.VMEM((rows, width), F32),
            pltpu.VMEM((rows, width), F32),
            pltpu.VMEM((1, width), F32),
            pltpu.VMEM((groups, taps), F32),
            pltpu.VMEM((groups, taps), F32),
            pltpu.VMEM((rows, 2 * LANES), BF16),
            pltpu.VMEM((rows, 2 * LANES), BF16),
            pltpu.VMEM((rows, LANES), F32),
            pltpu.VMEM((10, rows, LANES), F32),
            pltpu.VMEM((SUB * groups, taps), F32),
            pltpu.VMEM((ctx_count, piece, groups), F32),
            pltpu.VMEM((ctx_count - 1, piece, groups), F32),
            pltpu.VMEM((1, width), F32),
            pltpu.VMEM((1, width), F32),
            pltpu.VMEM((reach, 1, width), F32),
            pltpu.VMEM((reach, 1, width), F32),
            dma((halo_parts,)), dma((halo_parts,)), dma((halo_parts,)), dma((halo_parts,)),
            dma((reach,)), dma((reach,)), dma((reach,)), dma((reach,)),
            dma((ctx_count - 1,)), dma((ctx_count - 1,)),
        ],
        compiler_params=pltpu.CompilerParams(collective_id=0, has_side_effects=True),
        name="hyena_mixers",
    )(*args)


def solution(mesh):
    in_specs = (
        P(("dp", "ctx"), "tp"),
        P(("dp", "ctx"), "tp"),
        P(None, "tp"),
        P("tp"),
        P("tp"),
        P(("dp", "ctx"), "tp"),
        P("dp"),
        P(("dp", "ctx"), "tp"),
    )
    out_specs = (P(("dp", "ctx"), "tp"), P(("dp", "ctx"), "tp"), P(("dp", "ctx"), "tp"))
    return jax.shard_map(
        on_device, mesh=mesh, in_specs=in_specs, out_specs=out_specs, check_vma=False
    )
```
